32 devices in a mesh: fsdp: 8 (over y, x, core), ctx: 4 (over z).
Axes of the slice: x: 2, y: 2, z: 4, core: 2. Of those that a mesh axis runs over, the one named last changes fastest.
Arguments:
- hidden_in: bfloat16 [8, 512, 1024], P('fsdp', 'ctx'), may hold values from -6 to 6
- encoder_states: bfloat16 [8, 2048, 1024], P('fsdp', 'ctx'), may hold values from -6 to 6
- segment_ids: int32 [8, 512], P('fsdp'), may hold values from 0 to 3, never falling along the last dimension, each value on 1 to 256 neighbouring positions
- encoder_docs: int32 [8, 2048], P('fsdp'), may hold values from 0 to 3, as said below
- self_query: bfloat16 [1024, 1024], P('fsdp'), may hold values from -0.046875 to 0.046875
- self_key: bfloat16 [1024, 1024], P('fsdp'), may hold values from -0.1875 to 0.1875
- self_value: bfloat16 [1024, 1024], P('fsdp'), may hold values from -0.1875 to 0.1875
- self_out: bfloat16 [1024, 1024], P('fsdp'), may hold values from -3 to 3
- cross_query: bfloat16 [1024, 1024], P('fsdp'), may hold values from -0.046875 to 0.046875
- cross_key: bfloat16 [1024, 1024], P('fsdp'), may hold values from -0.1875 to 0.1875
- cross_value: bfloat16 [1024, 1024], P('fsdp'), may hold values from -0.1875 to 0.1875
- cross_out: bfloat16 [1024, 1024], P('fsdp'), may hold values from -3 to 3
- feed_gate: bfloat16 [1024, 2816], P('fsdp'), may hold values from -0.1875 to 0.1875
- feed_up: bfloat16 [1024, 2816], P('fsdp'), may hold values from -0.1875 to 0.1875
- feed_down: bfloat16 [2816, 1024], P('fsdp'), may hold values from -0.109375 to 0.109375
- norm_self: bfloat16 [1024], P('fsdp'), may hold values from 0.25 to 1.75
- norm_cross: bfloat16 [1024], P('fsdp'), may hold values from 0.25 to 1.75
- norm_feed: bfloat16 [1024], P('fsdp'), may hold values from 0.25 to 1.75
- bias_table: bfloat16 [512], P('fsdp'), may hold values from -4 to 4
- out_grad: bfloat16 [8, 512, 1024], P('fsdp', 'ctx'), may hold values from -6 to 6
Outputs:
- layer_out: bfloat16 [8, 512, 1024], P('fsdp', 'ctx')
- hidden_grad: float32 [8, 512, 1024], P('fsdp', 'ctx')
- encoder_grad: float32 [8, 2048, 1024], P('fsdp', 'ctx')
- grad_self_query: float32 [1024, 1024], P('fsdp')
- grad_self_key: float32 [1024, 1024], P('fsdp')
- grad_self_value: float32 [1024, 1024], P('fsdp')
- grad_self_out: float32 [1024, 1024], P('fsdp')
- grad_cross_query: float32 [1024, 1024], P('fsdp')
- grad_cross_key: float32 [1024, 1024], P('fsdp')
- grad_cross_value: float32 [1024, 1024], P('fsdp')
- grad_cross_out: float32 [1024, 1024], P('fsdp')
- grad_feed_gate: float32 [1024, 2816], P('fsdp')
- grad_feed_up: float32 [1024, 2816], P('fsdp')
- grad_feed_down: float32 [2816, 1024], P('fsdp')
- grad_norm_self: float32 [1024], P('fsdp')
- grad_norm_cross: float32 [1024], P('fsdp')
- grad_norm_feed: float32 [1024], P('fsdp')
- grad_bias_table: float32 [512], P('fsdp')
The draws below stay inside these ranges and needn't reach their ends.
Inputs may be any that keep to these rules, and one draw needn't show every extreme that they name: `segment_ids`: within a sequence the ids never fall; each of the 4 documents has 1 to 256 tokens, and one has exactly 256. `encoder_docs`: in each sequence the encoder states form 4 aligned blocks of 512, one block for each document id, in an order that differs by sequence.
All inputs are finite; a program needn't handle non-finite values.
Results may differ from the reference program's by a relative error of at most 0.025.
The reference program's roundings to bfloat16 on the way count: a program that leaves them out, or rounds other values in their place, can miss the bound.
Values may be sent and summed in bfloat16 or wider, within the bound.
A program may use at most 192 MiB of HBM per device.

```python
import math
import jax
import jax.numpy as jnp
import numpy as np
from jax import lax

D = 1024
H = 16
HD = 64
FF = 2816
BUCKETS = 32
DOCS = 4
ENC_DOC = 512
SEQS = 8
SEQ = 512
ENC_SEQ = 2048
DOC_MAX = 256


def draw_encoder_docs(key, part):
    sequence_ids = jnp.arange(SEQS, dtype=jnp.int32)
    orders = jax.vmap(lambda number: jax.random.permutation(jax.random.fold_in(key, number), DOCS))(sequence_ids)
    positions = jnp.arange(ENC_SEQ, dtype=jnp.int32) // ENC_DOC
    return orders[:, positions].astype(jnp.int32)


def block_scale(own_key, dims, shards, low, largest):
    factor_of = 1.0
    for position, parts in shards:
        heights = jax.random.uniform(jax.random.fold_in(jax.random.fold_in(own_key, 6), position), (parts,), jnp.float32, low / len(shards), largest / len(shards))
        factor_of = factor_of * jnp.repeat(jnp.exp(heights), dims[position] // parts).reshape((-1,) + (1,) * (len(dims) - 1 - position))
    return factor_of


def profile(count, total, limit, lean):
    loads = [(1 << 20) // math.isqrt(grade ** lean) + 1 for grade in range(2, count + 1)]
    spare, holding = total - limit - (count - 1), [1] * (count - 1)
    while spare > 0:
        free = [i for i in range(count - 1) if holding[i] < limit]
        whole, budget = sum([loads[i] for i in free]), spare
        for i in free:
            addition = min(limit - holding[i], max(1, budget * loads[i] // whole), spare)
            holding[i] = holding[i] + addition
            spare = spare - addition
    return np.array([limit] + holding)


def uneven(key, amount, total, bound, slope):
    if amount == 2:
        one = jax.random.randint(key, (), max(1, total - bound), min(bound, total - 1) + 1)
        return jnp.stack([one, total - one])
    sizes = jnp.asarray(profile(amount, total, bound, slope), jnp.int32)
    twos = (amount - 1) // 2
    donor, sink = sizes[1:1 + 2 * twos:2], sizes[2:2 + 2 * twos:2]
    slack = jnp.minimum(donor - 1, bound - sink)
    shifted = jax.random.randint(jax.random.fold_in(key, 1), (twos,), 0, 1 << 20) % (slack + 1)
    sizes = sizes.at[1:1 + 2 * twos:2].set(donor - shifted).at[2:2 + 2 * twos:2].set(sink + shifted)
    return sizes[jax.random.permutation(jax.random.fold_in(key, 2), amount)]


def bell_draw(own_key, shape, spread, reach, split=(), held_as=jnp.bfloat16):
    values = spread * jax.random.normal(own_key, shape, jnp.float32)
    if split:
        values = values * block_scale(own_key, shape, split, -0.22, 0.18)
    return jnp.clip(values, -reach, reach).astype(held_as)


def setup_inputs(seed: int = 0) -> dict:
    keys = jax.random.split(jax.random.key(seed), 21)
    hidden_in = bell_draw(keys[0], (SEQS, SEQ, D), 1.0, 6.0, ((0, 8), (1, 4)))
    encoder_states = bell_draw(keys[1], (SEQS, ENC_SEQ, D), 1.0, 6.0, ((0, 8), (1, 4)))
    segment_ids = jax.vmap(lambda own: jnp.searchsorted(jnp.cumsum(uneven(own, DOCS, SEQ, DOC_MAX, 2)), jnp.arange(SEQ), side="right"))(jax.random.split(keys[2], SEQS)).reshape((SEQS, SEQ)).astype(jnp.int32)
    encoder_docs = draw_encoder_docs(jax.random.fold_in(keys[20], 71), 0)
    self_query = bell_draw(keys[4], (D, H * HD), (D * HD // 4) ** -0.5, 0.046875, ((0, 8),))
    self_key = bell_draw(keys[5], (D, H * HD), D ** -0.5, 0.1875, ((0, 8),))
    self_value = bell_draw(keys[6], (D, H * HD), D ** -0.5, 0.1875, ((0, 8),))
    self_out = bell_draw(keys[7], (H * HD, D), 4 ** -0.5, 3.0, ((0, 8),))
    cross_query = bell_draw(keys[8], (D, H * HD), (D * HD // 4) ** -0.5, 0.046875, ((0, 8),))
    cross_key = bell_draw(keys[9], (D, H * HD), D ** -0.5, 0.1875, ((0, 8),))
    cross_value = bell_draw(keys[10], (D, H * HD), D ** -0.5, 0.1875, ((0, 8),))
    cross_out = bell_draw(keys[11], (H * HD, D), 4 ** -0.5, 3.0, ((0, 8),))
    feed_gate = bell_draw(keys[12], (D, FF), D ** -0.5, 0.1875, ((0, 8),))
    feed_up = bell_draw(keys[13], (D, FF), D ** -0.5, 0.1875, ((0, 8),))
    feed_down = bell_draw(keys[14], (FF, D), FF ** -0.5, 0.109375, ((0, 8),))
    norm_self = jnp.clip(1.0 + 0.15 * jax.random.normal(keys[15], (D,), jnp.float32), 0.25, 1.75).astype(jnp.bfloat16)
    norm_cross = jnp.clip(1.0 + 0.15 * jax.random.normal(keys[16], (D,), jnp.float32), 0.25, 1.75).astype(jnp.bfloat16)
    norm_feed = jnp.clip(1.0 + 0.15 * jax.random.normal(keys[17], (D,), jnp.float32), 0.25, 1.75).astype(jnp.bfloat16)
    bias_table = bell_draw(keys[18], (H * BUCKETS,), 1.0, 4.0, ((0, 8),))
    out_grad = bell_draw(keys[19], (SEQS, SEQ, D), 1.0, 6.0, ((0, 8), (1, 4)))
    return {"hidden_in": hidden_in, "encoder_states": encoder_states, "segment_ids": segment_ids, "encoder_docs": encoder_docs, "self_query": self_query, "self_key": self_key, "self_value": self_value, "self_out": self_out, "cross_query": cross_query, "cross_key": cross_key, "cross_value": cross_value, "cross_out": cross_out, "feed_gate": feed_gate, "feed_up": feed_up, "feed_down": feed_down, "norm_self": norm_self, "norm_cross": norm_cross, "norm_feed": norm_feed, "bias_table": bias_table, "out_grad": out_grad}


@jax.custom_vjp
def low(v):
    return lax.optimization_barrier(v.astype(jnp.bfloat16)).astype(jnp.float32)

@jax.custom_vjp
def low_back(v):
    return v

def low_keep(v):
    return (low(v), None)

def low_pass(kept, grad):
    return (grad,)

def back_keep(v):
    return (v, None)

def back_low(kept, grad):
    return (low(grad),)
low.defvjp(low_keep, low_pass)
low_back.defvjp(back_keep, back_low)
bucket_edges = (19, 21, 24, 27, 31, 35, 40, 46, 52, 59, 67, 77, 87, 99, 113)
epsilon = 1e-06
masked_value = -1e+30
highest = lax.Precision.HIGHEST

def normalize(values, gain_vector):
    inverse_root = lax.rsqrt(lax.optimization_barrier(jnp.mean(values * values, axis=-1, keepdims=True)) + epsilon)
    return values * inverse_root * gain_vector

def bucket_of(distance):
    bucket_index = jnp.minimum(distance, 16)
    for threshold in bucket_edges:
        bucket_index = bucket_index + (distance >= threshold).astype(jnp.int32)
    return bucket_index

def project(values, weight_matrix):
    return jnp.dot(values, weight_matrix, precision=highest)

def attend(query_part, key_rows, value_rows, allowed, extra_bias):
    scores = low_back(jnp.einsum('qhd,khd->hqk', query_part, key_rows, precision=highest))
    scores = scores + extra_bias
    scores = jnp.where(allowed[None], scores, masked_value)
    weights = low(jax.nn.softmax(scores, axis=-1))
    return jnp.einsum('hqk,khd->qhd', weights, value_rows, precision=highest)

def self_attention(queries, key_rows, value_rows, segments, table_rows):
    length = queries.shape[0]
    block_rows = math.gcd(length, 512)
    key_pos = jnp.arange(length, dtype=jnp.int32)
    table_heads = table_rows.reshape(H, BUCKETS)

    def one_block(row_start):
        query_part = lax.dynamic_slice_in_dim(queries, row_start, block_rows, 0)
        query_pos = row_start + jnp.arange(block_rows, dtype=jnp.int32)
        query_seg = lax.dynamic_slice_in_dim(segments, row_start, block_rows, 0)
        distance = query_pos[:, None] - key_pos[None, :]
        allowed = (distance >= 0) & (query_seg[:, None] == segments[None, :])
        buckets = bucket_of(jnp.maximum(distance, 0))
        onehot = (buckets[:, :, None] == jnp.arange(BUCKETS, dtype=jnp.int32)).astype(jnp.float32)
        extra_bias = jnp.einsum('qkb,hb->hqk', onehot, table_heads, precision=highest)
        return attend(query_part, key_rows, value_rows, allowed, extra_bias)
    starts = jnp.arange(length // block_rows, dtype=jnp.int32) * block_rows
    return lax.map(jax.checkpoint(one_block), starts).reshape(queries.shape)

def cross_attention(queries, key_rows, value_rows, segments, documents):
    length = queries.shape[0]
    block_rows = math.gcd(length, 512)

    def one_block(row_start):
        query_part = lax.dynamic_slice_in_dim(queries, row_start, block_rows, 0)
        query_seg = lax.dynamic_slice_in_dim(segments, row_start, block_rows, 0)
        allowed = query_seg[:, None] == documents[None, :]
        return attend(query_part, key_rows, value_rows, allowed, jnp.zeros((), jnp.float32))
    starts = jnp.arange(length // block_rows, dtype=jnp.int32) * block_rows
    return lax.map(jax.checkpoint(one_block), starts).reshape(queries.shape)

def decoder_layer(inputs, encoded, segments, documents, params):
    self_query, self_key, self_value, self_out, cross_query, cross_key, cross_value, cross_out, feed_gate, feed_up, feed_down, norm_self, norm_cross, norm_feed, bias_table = params
    tokens = inputs.shape[0]
    enc_rows = encoded.shape[0]
    self_normed = low(normalize(inputs, norm_self))
    queries = low(low_back(project(self_normed, self_query))).reshape(tokens, H, HD)
    key_rows = low(low_back(project(self_normed, self_key))).reshape(tokens, H, HD)
    value_rows = low(low_back(project(self_normed, self_value))).reshape(tokens, H, HD)
    attended = self_attention(queries, key_rows, value_rows, segments, bias_table)
    attended = low(low_back(attended.reshape(tokens, H * HD)))
    after_self = inputs + low_back(project(attended, self_out))
    cross_normed = low(normalize(after_self, norm_cross))
    cross_queries = low(low_back(project(cross_normed, cross_query))).reshape(tokens, H, HD)
    cross_keys = low(low_back(project(encoded, cross_key))).reshape(enc_rows, H, HD)
    cross_values = low(low_back(project(encoded, cross_value))).reshape(enc_rows, H, HD)
    crossed = cross_attention(cross_queries, cross_keys, cross_values, segments, documents)
    crossed = low(low_back(crossed.reshape(tokens, H * HD)))
    after_cross = after_self + low_back(project(crossed, cross_out))
    feed_normed = low(normalize(after_cross, norm_feed))
    gate_value = low_back(project(feed_normed, feed_gate))
    up_value = low_back(project(feed_normed, feed_up))
    hidden = low(jax.nn.gelu(gate_value, approximate=True) * up_value)
    return after_cross + low_back(project(hidden, feed_down))

def reference(hidden_in, encoder_states, segment_ids, encoder_docs, self_query, self_key, self_value, self_out, cross_query, cross_key, cross_value, cross_out, feed_gate, feed_up, feed_down, norm_self, norm_cross, norm_feed, bias_table, out_grad):
    params = tuple((weight_arg.astype(jnp.float32) for weight_arg in (self_query, self_key, self_value, self_out, cross_query, cross_key, cross_value, cross_out, feed_gate, feed_up, feed_down, norm_self, norm_cross, norm_feed, bias_table)))

    def whole_batch(inputs, encoded, weights):

        def one_sequence(element):
            return decoder_layer(element[0], element[1], element[2], element[3], weights)
        return lax.map(jax.checkpoint(one_sequence), (inputs, encoded, segment_ids, encoder_docs))
    result, pullback = jax.vjp(whole_batch, hidden_in.astype(jnp.float32), encoder_states.astype(jnp.float32), params)
    input_grad, encoded_grad, weight_grads = pullback(out_grad.astype(jnp.float32))
    return (result.astype(jnp.bfloat16), input_grad, encoded_grad, weight_grads[0], weight_grads[1], weight_grads[2], weight_grads[3], weight_grads[4], weight_grads[5], weight_grads[6], weight_grads[7], weight_grads[8], weight_grads[9], weight_grads[10], weight_grads[11], weight_grads[12], weight_grads[13], weight_grads[14])
```

```python
import functools
import math

import jax
import jax.numpy as jnp
from jax import lax
from jax.experimental import pallas as pl
from jax.experimental.pallas import tpu as pltpu
from jax.sharding import PartitionSpec as P

H = 16
HD = 64
BUCKETS = 32
DOCS = 4
MESH = pl.DeviceIdType.MESH


bucket_edges = (19, 21, 24, 27, 31, 35, 40, 46, 52, 59, 67, 77, 87, 99, 113)
epsilon = 1e-06
masked_value = -1e30
highest = lax.Precision.HIGHEST


def normalize(values, gain_vector):
    inverse_root = lax.rsqrt(jnp.mean(values * values, axis=-1, keepdims=True) + epsilon)
    return values * inverse_root * gain_vector


def norm_back(values, gain_vector, grad_normed):
    unused, pullback = jax.vjp(normalize, values, gain_vector)
    return pullback(grad_normed)


def product(left_side, right_side):
    return jnp.dot(left_side, right_side, preferred_element_type=jnp.float32)


def product_left(left_side, right_side):
    return lax.dot_general(
        left_side, right_side, (((0,), (0,)), ((), ())), preferred_element_type=jnp.float32
    )


def product_right(left_side, right_side):
    return lax.dot_general(
        left_side, right_side, (((1,), (1,)), ((), ())), preferred_element_type=jnp.float32
    )


def bucket_onehot(distance):
    bucket_index = jnp.minimum(distance, 16)
    for threshold in bucket_edges:
        bucket_index = bucket_index + (distance >= threshold).astype(jnp.int32)
    return (bucket_index[:, :, None] == jnp.arange(BUCKETS, dtype=jnp.int32)).astype(jnp.bfloat16)


def split_blocks(rows_all):
    total_rows = rows_all.shape[0]
    block_rows = math.gcd(total_rows, 512)
    return (block_rows, rows_all.reshape(total_rows // block_rows, block_rows, H, HD))


def block_logits(query_heads, key_part, allowed, distance, table_rows):
    scores = jnp.einsum("qhd,khd->hqk", query_heads, key_part, preferred_element_type=jnp.float32)
    onehot = None
    if table_rows is not None:
        onehot = bucket_onehot(distance)
        scores = scores + jnp.einsum(
            "qkb,hb->hqk", onehot, table_rows, preferred_element_type=jnp.float32
        )
    return (jnp.where(allowed[None], scores, masked_value), onehot)


def attention_forward(query_heads, key_rows, value_rows, mask_of, table_rows):
    block_rows, key_blocks = split_blocks(key_rows)
    unused, value_blocks = split_blocks(value_rows)
    numbers = jnp.arange(key_blocks.shape[0], dtype=jnp.int32)
    query_count = query_heads.shape[0]

    def total_step(carried, element):
        number, key_part = element
        allowed, distance = mask_of(number, block_rows)

        def total_live_branch(state):
            running, summed = state
            scores, unused_hot = block_logits(query_heads, key_part, allowed, distance, table_rows)
            newest = jnp.maximum(running, jnp.max(scores, axis=-1))
            exp_terms = jnp.where(allowed[None], jnp.exp(scores - newest[..., None]), 0.0)
            return (newest, summed * jnp.exp(running - newest) + jnp.sum(exp_terms, axis=-1))

        return (lax.cond(jnp.any(allowed), total_live_branch, lambda state: state, carried), None)

    start_state = (
        jnp.full((H, query_count), masked_value, jnp.float32),
        jnp.zeros((H, query_count), jnp.float32),
    )
    (running, summed), unused_out = lax.scan(total_step, start_state, (numbers, key_blocks))
    logsum = running + jnp.log(summed)

    def output_step(carried, element):
        number, key_part, value_part = element
        allowed, distance = mask_of(number, block_rows)

        def output_live_branch(state):
            scores, unused_hot = block_logits(query_heads, key_part, allowed, distance, table_rows)
            weights = jnp.where(allowed[None], jnp.exp(scores - logsum[..., None]), 0.0).astype(
                jnp.bfloat16
            )
            return state + jnp.einsum(
                "hqk,khd->qhd", weights, value_part, preferred_element_type=jnp.float32
            )

        return (lax.cond(jnp.any(allowed), output_live_branch, lambda state: state, carried), None)

    output, unused_out = lax.scan(
        output_step,
        jnp.zeros((query_count, H, HD), jnp.float32),
        (numbers, key_blocks, value_blocks),
    )
    return (output, logsum)


def attention_delta(query_heads, key_rows, value_rows, grad_heads, logsum, mask_of, table_rows):
    block_rows, key_blocks = split_blocks(key_rows)
    unused, value_blocks = split_blocks(value_rows)
    numbers = jnp.arange(key_blocks.shape[0], dtype=jnp.int32)
    query_count = query_heads.shape[0]

    def delta_step(carried, element):
        number, key_part, value_part = element
        allowed, distance = mask_of(number, block_rows)

        def delta_live_branch(state):
            scores, unused_hot = block_logits(query_heads, key_part, allowed, distance, table_rows)
            weights = jnp.where(allowed[None], jnp.exp(scores - logsum[..., None]), 0.0)
            grad_weights = jnp.einsum(
                "qhd,khd->hqk", grad_heads, value_part, preferred_element_type=jnp.float32
            )
            return state + jnp.sum(weights * grad_weights, axis=-1)

        return (lax.cond(jnp.any(allowed), delta_live_branch, lambda state: state, carried), None)

    row_delta, unused_out = lax.scan(
        delta_step, jnp.zeros((H, query_count), jnp.float32), (numbers, key_blocks, value_blocks)
    )
    return row_delta


def attention_backward(
    query_heads, key_rows, value_rows, grad_heads, logsum, row_delta, mask_of, table_rows
):
    block_rows, key_blocks = split_blocks(key_rows)
    unused, value_blocks = split_blocks(value_rows)
    numbers = jnp.arange(key_blocks.shape[0], dtype=jnp.int32)
    query_count = query_heads.shape[0]
    part_shape = (block_rows, H, HD)

    def grad_step(carried, element):
        number, key_part, value_part = element
        allowed, distance = mask_of(number, block_rows)

        def grad_live_branch(state):
            grad_query, grad_table = state
            scores, onehot = block_logits(query_heads, key_part, allowed, distance, table_rows)
            weights = jnp.where(allowed[None], jnp.exp(scores - logsum[..., None]), 0.0)
            grad_weights = jnp.einsum(
                "qhd,khd->hqk", grad_heads, value_part, preferred_element_type=jnp.float32
            )
            grad_scores = weights * (grad_weights - row_delta[..., None])
            rounded = grad_scores.astype(jnp.bfloat16)
            grad_query = grad_query + jnp.einsum(
                "hqk,khd->qhd", rounded, key_part, preferred_element_type=jnp.float32
            )
            if table_rows is not None:
                grad_table = grad_table + jnp.einsum(
                    "hqk,qkb->hb", grad_scores, onehot.astype(jnp.float32), precision=highest
                )
            grad_key_part = jnp.einsum(
                "hqk,qhd->khd", rounded, query_heads, preferred_element_type=jnp.float32
            )
            grad_value_part = jnp.einsum(
                "hqk,qhd->khd",
                weights.astype(jnp.bfloat16),
                grad_heads,
                preferred_element_type=jnp.float32,
            )
            return ((grad_query, grad_table), (grad_key_part, grad_value_part))

        def dead_branch(state):
            return (state, (jnp.zeros(part_shape, jnp.float32), jnp.zeros(part_shape, jnp.float32)))

        return lax.cond(jnp.any(allowed), grad_live_branch, dead_branch, carried)

    table_shape = (H, BUCKETS) if table_rows is not None else (1, 1)
    start_state = (
        jnp.zeros((query_count, H, HD), jnp.float32),
        jnp.zeros(table_shape, jnp.float32),
    )
    (grad_query, grad_table), key_parts = lax.scan(
        grad_step, start_state, (numbers, key_blocks, value_blocks)
    )
    total_rows = key_rows.shape[0]
    return (
        grad_query,
        grad_table,
        key_parts[0].reshape(total_rows, H * HD),
        key_parts[1].reshape(total_rows, H * HD),
    )


def on_device(
    hidden_in,
    encoder_states,
    segment_ids,
    encoder_docs,
    self_query,
    self_key,
    self_value,
    self_out,
    cross_query,
    cross_key,
    cross_value,
    cross_out,
    feed_gate,
    feed_up,
    feed_down,
    norm_self,
    norm_cross,
    norm_feed,
    bias_table,
    out_grad,
):
    gathered = (
        lax.all_gather(self_query, "fsdp", axis=0, tiled=True),
        lax.all_gather(self_key, "fsdp", axis=0, tiled=True),
        lax.all_gather(self_value, "fsdp", axis=0, tiled=True),
        lax.all_gather(self_out, "fsdp", axis=0, tiled=True),
        lax.all_gather(cross_query, "fsdp", axis=0, tiled=True),
        lax.all_gather(cross_key, "fsdp", axis=0, tiled=True),
        lax.all_gather(cross_value, "fsdp", axis=0, tiled=True),
        lax.all_gather(cross_out, "fsdp", axis=0, tiled=True),
        lax.all_gather(feed_gate, "fsdp", axis=0, tiled=True),
        lax.all_gather(feed_up, "fsdp", axis=0, tiled=True),
        lax.all_gather(feed_down, "fsdp", axis=0, tiled=True),
        lax.all_gather(norm_self, "fsdp", axis=0, tiled=True),
        lax.all_gather(norm_cross, "fsdp", axis=0, tiled=True),
        lax.all_gather(norm_feed, "fsdp", axis=0, tiled=True),
        lax.all_gather(bias_table, "fsdp", axis=0, tiled=True),
    )
    tokens = hidden_in[0]
    encoded = encoder_states[0]
    segments = segment_ids[0]
    documents = encoder_docs[0]
    tok_rows = tokens.shape[0]
    first_row = lax.axis_index("ctx") * tok_rows
    query_pos = first_row + jnp.arange(tok_rows, dtype=jnp.int32)
    query_seg = lax.dynamic_slice_in_dim(segments, first_row, tok_rows, 0)

    def self_mask(number, block_rows):
        key_pos = number * block_rows + jnp.arange(block_rows, dtype=jnp.int32)
        key_seg = lax.dynamic_slice_in_dim(segments, number * block_rows, block_rows, 0)
        distance = query_pos[:, None] - key_pos[None, :]
        allowed = (distance >= 0) & (query_seg[:, None] == key_seg[None, :])
        return (allowed, jnp.maximum(distance, 0))

    def cross_mask(number, block_rows):
        key_doc = lax.dynamic_slice_in_dim(documents, number * block_rows, block_rows, 0)
        return (query_seg[:, None] == key_doc[None, :], None)

    inputs = tokens.astype(jnp.float32)
    self_normed = normalize(inputs, gathered[11].astype(jnp.float32)).astype(jnp.bfloat16)
    queries = product(self_normed, gathered[0]).astype(jnp.bfloat16)
    key_local = product(self_normed, gathered[1]).astype(jnp.bfloat16)
    value_local = product(self_normed, gathered[2]).astype(jnp.bfloat16)
    key_rows, value_rows = (
        lax.all_gather(key_local, "ctx", axis=0, tiled=True),
        lax.all_gather(value_local, "ctx", axis=0, tiled=True),
    )
    table_rows = gathered[14].reshape(H, BUCKETS)
    query_heads = queries.reshape(tok_rows, H, HD)
    key_heads = key_rows.reshape(-1, H, HD)
    value_heads = value_rows.reshape(-1, H, HD)
    self_heads, self_logsum = attention_forward(
        query_heads, key_heads, value_heads, self_mask, table_rows
    )
    self_attended = self_heads.reshape(tok_rows, H * HD).astype(jnp.bfloat16)
    after_self = inputs + product(self_attended, gathered[3])
    cross_normed = normalize(after_self, gathered[12].astype(jnp.float32)).astype(jnp.bfloat16)
    cross_queries = product(cross_normed, gathered[4]).astype(jnp.bfloat16)
    cross_key_local = product(encoded, gathered[5]).astype(jnp.bfloat16)
    cross_value_local = product(encoded, gathered[6]).astype(jnp.bfloat16)
    cross_keys, cross_values = (
        lax.all_gather(cross_key_local, "ctx", axis=0, tiled=True),
        lax.all_gather(cross_value_local, "ctx", axis=0, tiled=True),
    )
    cross_query_heads = cross_queries.reshape(tok_rows, H, HD)
    cross_key_heads = cross_keys.reshape(-1, H, HD)
    cross_value_heads = cross_values.reshape(-1, H, HD)
    cross_heads, cross_logsum = attention_forward(
        cross_query_heads, cross_key_heads, cross_value_heads, cross_mask, None
    )
    cross_attended = cross_heads.reshape(tok_rows, H * HD).astype(jnp.bfloat16)
    after_cross = after_self + product(cross_attended, gathered[7])
    feed_normed = normalize(after_cross, gathered[13].astype(jnp.float32)).astype(jnp.bfloat16)
    gate_value = product(feed_normed, gathered[8])
    up_value = product(feed_normed, gathered[9])
    hidden_units = (jax.nn.gelu(gate_value, approximate=True) * up_value).astype(jnp.bfloat16)
    layer_out = (after_cross + product(hidden_units, gathered[10])).astype(jnp.bfloat16)
    grad_after = out_grad[0].astype(jnp.float32)
    grad_round = grad_after.astype(jnp.bfloat16)
    grad_feed_down = product_left(hidden_units, grad_round)
    grad_hidden = product_right(grad_round, gathered[10])
    unused, pullback = jax.vjp(
        lambda gate_in, up_in: jax.nn.gelu(gate_in, approximate=True) * up_in, gate_value, up_value
    )
    grad_gate, grad_up = pullback(grad_hidden)
    gate_round = grad_gate.astype(jnp.bfloat16)
    up_round = grad_up.astype(jnp.bfloat16)
    grad_feed_gate = product_left(feed_normed, gate_round)
    grad_feed_up = product_left(feed_normed, up_round)
    grad_feed_normed = product_right(gate_round, gathered[8]) + product_right(up_round, gathered[9])
    grad_cross_side, grad_norm_feed = norm_back(
        after_cross, gathered[13].astype(jnp.float32), grad_feed_normed
    )
    grad_after_cross = grad_after + grad_cross_side
    cross_round = grad_after_cross.astype(jnp.bfloat16)
    grad_cross_out = product_left(cross_attended, cross_round)
    grad_cross_heads = (
        product_right(cross_round, gathered[7]).astype(jnp.bfloat16).reshape(tok_rows, H, HD)
    )
    cross_delta = attention_delta(
        cross_query_heads,
        cross_key_heads,
        cross_value_heads,
        grad_cross_heads,
        cross_logsum,
        cross_mask,
        None,
    )
    grad_cross_q, unused_table, grad_cross_k, grad_cross_v = attention_backward(
        cross_query_heads,
        cross_key_heads,
        cross_value_heads,
        grad_cross_heads,
        cross_logsum,
        cross_delta,
        cross_mask,
        None,
    )
    cross_key_grad, cross_value_grad = (
        lax.psum_scatter(
            grad_cross_k.astype(jnp.bfloat16), "ctx", scatter_dimension=0, tiled=True
        ).astype(jnp.float32),
        lax.psum_scatter(
            grad_cross_v.astype(jnp.bfloat16), "ctx", scatter_dimension=0, tiled=True
        ).astype(jnp.float32),
    )
    cross_key_round = cross_key_grad.astype(jnp.bfloat16)
    cross_value_round = cross_value_grad.astype(jnp.bfloat16)
    grad_cross_key = product_left(encoded, cross_key_round)
    grad_cross_value = product_left(encoded, cross_value_round)
    encoder_grad = product_right(cross_key_round, gathered[5]) + product_right(
        cross_value_round, gathered[6]
    )
    cross_query_round = grad_cross_q.reshape(tok_rows, H * HD).astype(jnp.bfloat16)
    grad_cross_query = product_left(cross_normed, cross_query_round)
    grad_cross_normed = product_right(cross_query_round, gathered[4])
    grad_self_side, grad_norm_cross = norm_back(
        after_self, gathered[12].astype(jnp.float32), grad_cross_normed
    )
    grad_after_self = grad_after_cross + grad_self_side
    self_round = grad_after_self.astype(jnp.bfloat16)
    grad_self_out = product_left(self_attended, self_round)
    grad_self_flat = product_right(self_round, gathered[3]).astype(jnp.bfloat16)
    grad_self_heads = grad_self_flat.reshape(tok_rows, H, HD)
    back_table = gathered[14].reshape(H, BUCKETS)
    self_delta = attention_delta(
        query_heads, key_heads, value_heads, grad_self_heads, self_logsum, self_mask, back_table
    )
    grad_self_q, grad_table, grad_self_k, grad_self_v = attention_backward(
        query_heads,
        key_heads,
        value_heads,
        grad_self_heads,
        self_logsum,
        self_delta,
        self_mask,
        back_table,
    )
    self_key_grad, self_value_grad = (
        lax.psum_scatter(
            grad_self_k.astype(jnp.bfloat16), "ctx", scatter_dimension=0, tiled=True
        ).astype(jnp.float32),
        lax.psum_scatter(
            grad_self_v.astype(jnp.bfloat16), "ctx", scatter_dimension=0, tiled=True
        ).astype(jnp.float32),
    )
    self_key_round = self_key_grad.astype(jnp.bfloat16)
    self_value_round = self_value_grad.astype(jnp.bfloat16)
    self_query_round = grad_self_q.reshape(tok_rows, H * HD).astype(jnp.bfloat16)
    grad_self_query = product_left(self_normed, self_query_round)
    grad_self_key = product_left(self_normed, self_key_round)
    grad_self_value = product_left(self_normed, self_value_round)
    grad_self_normed = (
        product_right(self_query_round, gathered[0])
        + product_right(self_key_round, gathered[1])
        + product_right(self_value_round, gathered[2])
    )
    grad_input_side, grad_norm_self = norm_back(
        inputs, gathered[11].astype(jnp.float32), grad_self_normed
    )
    hidden_grad = grad_after_self + grad_input_side
    grad_bias_table = grad_table.reshape(H * BUCKETS)
    pieces = (
        lax.psum_scatter(
            grad_self_query.astype(jnp.bfloat16), "fsdp", scatter_dimension=0, tiled=True
        ).astype(jnp.float32),
        lax.psum_scatter(
            grad_self_key.astype(jnp.bfloat16), "fsdp", scatter_dimension=0, tiled=True
        ).astype(jnp.float32),
        lax.psum_scatter(
            grad_self_value.astype(jnp.bfloat16), "fsdp", scatter_dimension=0, tiled=True
        ).astype(jnp.float32),
        lax.psum_scatter(
            grad_self_out.astype(jnp.bfloat16), "fsdp", scatter_dimension=0, tiled=True
        ).astype(jnp.float32),
        lax.psum_scatter(
            grad_cross_query.astype(jnp.bfloat16), "fsdp", scatter_dimension=0, tiled=True
        ).astype(jnp.float32),
        lax.psum_scatter(
            grad_cross_key.astype(jnp.bfloat16), "fsdp", scatter_dimension=0, tiled=True
        ).astype(jnp.float32),
        lax.psum_scatter(
            grad_cross_value.astype(jnp.bfloat16), "fsdp", scatter_dimension=0, tiled=True
        ).astype(jnp.float32),
        lax.psum_scatter(
            grad_cross_out.astype(jnp.bfloat16), "fsdp", scatter_dimension=0, tiled=True
        ).astype(jnp.float32),
        lax.psum_scatter(
            grad_feed_gate.astype(jnp.bfloat16), "fsdp", scatter_dimension=0, tiled=True
        ).astype(jnp.float32),
        lax.psum_scatter(
            grad_feed_up.astype(jnp.bfloat16), "fsdp", scatter_dimension=0, tiled=True
        ).astype(jnp.float32),
        lax.psum_scatter(
            grad_feed_down.astype(jnp.bfloat16), "fsdp", scatter_dimension=0, tiled=True
        ).astype(jnp.float32),
        lax.psum_scatter(
            grad_norm_self.astype(jnp.bfloat16), "fsdp", scatter_dimension=0, tiled=True
        ).astype(jnp.float32),
        lax.psum_scatter(
            grad_norm_cross.astype(jnp.bfloat16), "fsdp", scatter_dimension=0, tiled=True
        ).astype(jnp.float32),
        lax.psum_scatter(
            grad_norm_feed.astype(jnp.bfloat16), "fsdp", scatter_dimension=0, tiled=True
        ).astype(jnp.float32),
        lax.psum_scatter(
            grad_bias_table.astype(jnp.bfloat16), "fsdp", scatter_dimension=0, tiled=True
        ).astype(jnp.float32),
    )
    owned = (
        lax.psum(pieces[0].astype(jnp.bfloat16), "ctx").astype(jnp.float32),
        lax.psum(pieces[1].astype(jnp.bfloat16), "ctx").astype(jnp.float32),
        lax.psum(pieces[2].astype(jnp.bfloat16), "ctx").astype(jnp.float32),
        lax.psum(pieces[3].astype(jnp.bfloat16), "ctx").astype(jnp.float32),
        lax.psum(pieces[4].astype(jnp.bfloat16), "ctx").astype(jnp.float32),
        lax.psum(pieces[5].astype(jnp.bfloat16), "ctx").astype(jnp.float32),
        lax.psum(pieces[6].astype(jnp.bfloat16), "ctx").astype(jnp.float32),
        lax.psum(pieces[7].astype(jnp.bfloat16), "ctx").astype(jnp.float32),
        lax.psum(pieces[8].astype(jnp.bfloat16), "ctx").astype(jnp.float32),
        lax.psum(pieces[9].astype(jnp.bfloat16), "ctx").astype(jnp.float32),
        lax.psum(pieces[10].astype(jnp.bfloat16), "ctx").astype(jnp.float32),
        lax.psum(pieces[11].astype(jnp.bfloat16), "ctx").astype(jnp.float32),
        lax.psum(pieces[12].astype(jnp.bfloat16), "ctx").astype(jnp.float32),
        lax.psum(pieces[13].astype(jnp.bfloat16), "ctx").astype(jnp.float32),
        lax.psum(pieces[14].astype(jnp.bfloat16), "ctx").astype(jnp.float32),
    )
    return (
        layer_out[None],
        hidden_grad[None],
        encoder_grad[None],
        owned[0],
        owned[1],
        owned[2],
        owned[3],
        owned[4],
        owned[5],
        owned[6],
        owned[7],
        owned[8],
        owned[9],
        owned[10],
        owned[11],
        owned[12],
        owned[13],
        owned[14],
    )


def place():
    rank = lax.axis_index("fsdp")
    core = lax.rem(rank, 2)
    along_x = lax.rem(lax.div(rank, 2), 2)
    along_y = lax.div(rank, 4)
    return (rank, core, along_x, along_y, lax.axis_index("ctx"))


def greet(partners):
    barrier = pltpu.get_barrier_semaphore()
    for partner in partners:
        pl.semaphore_signal(barrier, inc=1, device_id=partner, device_id_type=MESH)
    pl.semaphore_wait(barrier, len(partners))


def remote(source, target, send_sem, recv_sem, device):
    return pltpu.make_async_remote_copy(
        src_ref=source,
        dst_ref=target,
        send_sem=send_sem,
        recv_sem=recv_sem,
        device_id=device,
        device_id_type=MESH,
    )


class Gather:
    def __init__(self, owns, fulls, send_sems, recv_sems, local_sems):
        rank, core, along_x, along_y, depth = place()
        self.owns, self.fulls = owns, fulls
        self.send_sems, self.recv_sems, self.local_sems = send_sems, recv_sems, local_sems
        self.rank = rank
        self.by_x = rank + 2 - 4 * along_x
        self.by_y = rank + 4 - 8 * along_y
        self.diag = self.by_x + 4 - 8 * along_y
        self.to_x = (self.by_x, depth)
        self.to_y = (self.by_y, depth)
        self.to_core = (rank + 1 - 2 * core, depth)
        self.shift = 1 - 2 * core

    def rows(self, number, slot, half):
        full = self.fulls[number]
        if half is None:
            return full.at[slot]
        size = full.shape[1] // 2
        return full.at[slot, pl.ds(half * size, size)]

    def copy(self, number, kind, slot, half, device, own=False):
        target = self.rows(number, slot, half)
        return remote(
            self.owns[number] if own else target,
            target,
            self.send_sems.at[number, kind],
            self.recv_sems.at[number, kind],
            device,
        )

    def sent(self, number, kind):
        slot, half, device = (
            (self.rank, None, self.to_x),
            (self.rank, None, self.to_y),
            (self.rank, None, self.to_core),
            (self.by_x, 0, self.to_y),
            (self.by_y, 1, self.to_x),
            (self.by_x, None, self.to_core),
            (self.by_y, None, self.to_core),
            (self.diag, 0, self.to_core),
            (self.diag, 1, self.to_core),
        )[kind]
        return self.copy(number, kind, slot, half, device, kind < 3)

    def landed(self, number, kind):
        shift = self.shift
        slot, half, device = (
            (self.by_x, None, self.to_x),
            (self.by_y, None, self.to_y),
            (self.rank + shift, None, self.to_core),
            (self.diag, 0, self.to_y),
            (self.diag, 1, self.to_x),
            (self.by_x + shift, None, self.to_core),
            (self.by_y + shift, None, self.to_core),
            (self.diag + shift, 0, self.to_core),
            (self.diag + shift, 1, self.to_core),
        )[kind]
        return self.copy(number, kind, slot, half, device)

    def local(self, number):
        return pltpu.make_async_copy(
            self.owns[number], self.fulls[number].at[self.rank], self.local_sems.at[number]
        )

    def issue(self, number):
        for kind in range(3):
            self.sent(number, kind).start()
        self.local(number).start()

    def relay(self, number):
        self.landed(number, 0).wait_recv()
        self.sent(number, 3).start()
        self.landed(number, 1).wait_recv()
        self.sent(number, 4).start()
        self.sent(number, 5).start()
        self.sent(number, 6).start()

    def spread(self, number):
        self.landed(number, 3).wait_recv()
        self.sent(number, 7).start()
        self.landed(number, 4).wait_recv()
        self.sent(number, 8).start()

    def finish(self, number):
        for kind in (2, 5, 6, 7, 8):
            self.landed(number, kind).wait_recv()
        for kind in range(9):
            self.sent(number, kind).wait_send()
        self.local(number).wait()


def column_partners(rank, depth):
    return [(rank, lax.rem(depth + step, DOCS)) for step in range(1, DOCS)]


def gather_kernel(count, *refs):
    owns, (tokens, cotangent) = refs[:count], refs[count : count + 2]
    refs = refs[count + 2 :]
    fulls, (all_tokens, all_cotangent) = refs[:count], refs[count : count + 2]
    send_sems, recv_sems, local_sems, line_send, line_recv, line_local = refs[count + 2 :]
    rank, core, along_x, along_y, depth = place()
    gather = Gather(owns, fulls, send_sems, recv_sems, local_sems)
    column = column_partners(rank, depth)
    greet([gather.to_x, gather.to_y, gather.to_core] + column)
    pairs = ((tokens, all_tokens), (cotangent, all_cotangent))
    line = []
    for number, (own, whole) in enumerate(pairs):
        pltpu.make_async_copy(own, whole.at[depth], line_local.at[number]).start()
        for step, partner in enumerate(column):
            send = remote(
                own, whole.at[depth], line_send.at[number, step], line_recv.at[number, step], partner
            )
            send.start()
            origin = lax.rem(depth + DOCS - 1 - step, DOCS)
            receive = remote(
                own, whole.at[origin], line_send.at[number, step], line_recv.at[number, step], partner
            )
            line.append((send, receive))
    for step in range(count + 3):
        if step < count:
            gather.issue(step)
        if 0 <= step - 1 < count:
            gather.relay(step - 1)
        if 0 <= step - 2 < count:
            gather.spread(step - 2)
        if 0 <= step - 3 < count:
            gather.finish(step - 3)
    for number, (own, whole) in enumerate(pairs):
        pltpu.make_async_copy(own, whole.at[depth], line_local.at[number]).wait()
    for send, receive in line:
        receive.wait_recv()
        send.wait_send()


def gather_call(shards, tokens, cotangent):
    count = len(shards)
    vmem = pl.BlockSpec(memory_space=pltpu.VMEM)
    anywhere = pl.BlockSpec(memory_space=pl.ANY)
    shapes = [jax.ShapeDtypeStruct((8,) + s.shape, s.dtype) for s in shards]
    shapes += [jax.ShapeDtypeStruct((DOCS,) + s.shape, s.dtype) for s in (tokens, cotangent)]
    return pl.pallas_call(
        functools.partial(gather_kernel, count),
        out_shape=shapes,
        in_specs=[vmem] * (count + 2),
        out_specs=[anywhere] * (count + 2),
        scratch_shapes=[
            pltpu.SemaphoreType.DMA((count, 9)),
            pltpu.SemaphoreType.DMA((count, 9)),
            pltpu.SemaphoreType.DMA((count,)),
            pltpu.SemaphoreType.DMA((2, DOCS - 1)),
            pltpu.SemaphoreType.DMA((2, DOCS - 1)),
            pltpu.SemaphoreType.DMA((2,)),
        ],
        compiler_params=pltpu.CompilerParams(collective_id=1, has_side_effects=True),
        name="gather_all",
    )(*shards, tokens, cotangent)


def add_rows(target, source):
    rows = target.shape[-2]
    step = math.gcd(rows, 32)

    def one(index, unused):
        at = pl.ds(index * step, step)
        target[at, :] = target[at, :] + source[at, :]
        return unused

    lax.fori_loop(0, rows // step, one, 0)


class Reduce:
    def __init__(self, grads, outs, buffers, load, send_sems, recv_sems, local_sems):
        rank, core, along_x, along_y, depth = place()
        self.grads, self.outs, self.buffers, self.load = grads, outs, buffers, load
        self.send_sems, self.recv_sems, self.local_sems = send_sems, recv_sems, local_sems
        self.core, self.along_x, self.along_y = core, along_x, along_y
        self.block = 2 * along_y + along_x
        self.to_x = (rank + 2 - 4 * along_x, depth)
        self.to_y = (rank + 4 - 8 * along_y, depth)
        self.to_core = (rank + 1 - 2 * core, depth)
        self.inner = (depth == 1) | (depth == 2)
        self.to_line = (rank, depth + 1 - 2 * lax.rem(depth, 2))
        self.to_middle = (rank, 3 - depth)
        self.partners = [self.to_x, self.to_y, self.to_core, self.to_line, self.to_middle]

    def copy(self, number, kind, source, target, device):
        return remote(
            source,
            target,
            self.send_sems.at[number, kind],
            self.recv_sems.at[number, kind],
            device,
        )

    def halves(self, number):
        size = self.grads[number].shape[1] // 2
        return (pl.ds(0, size), pl.ds(size, size))

    def core_copies(self, number):
        grad, both = self.grads[number], self.buffers[number][0]
        return [
            self.copy(number, q, grad.at[2 * q + 1 - self.core], both.at[q], self.to_core)
            for q in range(4)
        ]

    def loads(self, number):
        grad = self.grads[number]
        return [
            pltpu.make_async_copy(
                grad.at[2 * q + self.core], self.load[number].at[q], self.local_sems.at[number, q]
            )
            for q in range(4)
        ]

    def first_copies(self, number):
        both, from_x, from_y = self.buffers[number][:3]
        low, high = self.halves(number)
        copies = []
        for other in range(2):
            copies.append(
                self.copy(
                    number,
                    4 + other,
                    both.at[2 * other + 1 - self.along_x, low],
                    from_x.at[other],
                    self.to_x,
                )
            )
        for other in range(2):
            copies.append(
                self.copy(
                    number,
                    6 + other,
                    both.at[2 * (1 - self.along_y) + other, high],
                    from_y.at[other],
                    self.to_y,
                )
            )
        return copies

    def second_copies(self, number):
        both, unused_x, unused_y, late_x, late_y = self.buffers[number][:5]
        low, high = self.halves(number)
        return [
            self.copy(
                number,
                8,
                both.at[2 * (1 - self.along_y) + self.along_x, low],
                late_y,
                self.to_y,
            ),
            self.copy(
                number,
                9,
                both.at[2 * self.along_y + 1 - self.along_x, high],
                late_x,
                self.to_x,
            ),
        ]

    def line_copy(self, number):
        return self.copy(
            number,
            10,
            self.buffers[number][0].at[self.block],
            self.buffers[number][5],
            self.to_line,
        )

    def middle_copy(self, number):
        return self.copy(
            number,
            11,
            self.buffers[number][0].at[self.block],
            self.buffers[number][6],
            self.to_middle,
        )

    def return_copy(self, number):
        return self.copy(
            number,
            10,
            self.buffers[number][5],
            self.buffers[number][5],
            self.to_line,
        )

    def write(self, number):
        return pltpu.make_async_copy(
            self.buffers[number][5], self.outs[number], self.local_sems.at[number, 4]
        )

    def stage(self, number, level):
        both, from_x, from_y, late_x, late_y, on_line, on_middle = self.buffers[number]
        low, high = self.halves(number)
        if level == 0:
            for copy in self.core_copies(number) + self.loads(number):
                copy.start()
        elif level == 1:
            for q, (copy, load) in enumerate(zip(self.core_copies(number), self.loads(number))):
                copy.wait_recv()
                load.wait()
                add_rows(both.at[q], self.load[number].at[q])
            for copy in self.first_copies(number):
                copy.start()
        elif level == 2:
            copies = self.first_copies(number)
            for other in range(2):
                copies[other].wait_recv()
                copies[other].wait_send()
                add_rows(both.at[2 * other + self.along_x, low], from_x.at[other])
            for other in range(2):
                copies[2 + other].wait_recv()
                copies[2 + other].wait_send()
                add_rows(both.at[2 * self.along_y + other, high], from_y.at[other])
            for copy in self.second_copies(number):
                copy.start()
        elif level == 3:
            to_y, to_x = self.second_copies(number)
            to_y.wait_recv()
            add_rows(both.at[self.block, low], late_y)
            to_x.wait_recv()
            add_rows(both.at[self.block, high], late_x)
            to_y.wait_send()
            to_x.wait_send()

            @pl.when(jnp.logical_not(self.inner))
            def _():
                self.line_copy(number).start()
        elif level == 4:

            @pl.when(self.inner)
            def _():
                self.line_copy(number).wait_recv()
                add_rows(both.at[self.block], on_line)
                self.middle_copy(number).start()
        elif level == 5:

            @pl.when(self.inner)
            def _():
                middle = self.middle_copy(number)
                middle.wait_recv()
                rows = on_line.shape[0]
                step = math.gcd(rows, 32)

                def one(index, unused):
                    at = pl.ds(index * step, step)
                    on_line[at, :] = both[self.block, at, :] + on_middle[at, :]
                    return unused

                lax.fori_loop(0, rows // step, one, 0)
                middle.wait_send()
                self.return_copy(number).start()
        else:
            line = self.line_copy(number)

            @pl.when(jnp.logical_not(self.inner))
            def _():
                line.wait_send()
                line.wait_recv()

            @pl.when(self.inner)
            def _():
                self.return_copy(number).wait_send()

            for copy in self.core_copies(number):
                copy.wait_send()
            self.write(number).start()

    levels = 7


def buffer_shapes(rows, width, dtype):
    return [
        pltpu.VMEM((4, rows, width), dtype),
        pltpu.VMEM((2, rows // 2, width), dtype),
        pltpu.VMEM((2, rows // 2, width), dtype),
        pltpu.VMEM((rows // 2, width), dtype),
        pltpu.VMEM((rows // 2, width), dtype),
        pltpu.VMEM((rows, width), dtype),
        pltpu.VMEM((rows, width), dtype),
    ]


def reduce_kernel(count, shared, *refs):
    grads, backs = refs[:count], refs[count : count + 2]
    refs = refs[count + 2 :]
    outs, back_outs = refs[:count], refs[count : count + 2]
    refs = refs[count + 2 :]
    buffers = [refs[7 * i : 7 * i + 7] for i in range(count)]
    refs = refs[7 * count :]
    loads = [refs[shared[i]] for i in range(count)]
    refs = refs[max(shared) + 1 :]
    landing, send_sems, recv_sems, local_sems, line_send, line_recv = refs
    rank, core, along_x, along_y, depth = place()
    reduce = Reduce(grads, outs, buffers, loads, send_sems, recv_sems, local_sems)
    column = column_partners(rank, depth)
    greet([reduce.to_x, reduce.to_y, reduce.to_core] + column)
    line = []
    for number, back in enumerate(backs):
        for step, (unused, partner) in enumerate(column):
            send = remote(
                back.at[partner],
                landing.at[number, step],
                line_send.at[number, step],
                line_recv.at[number, step],
                (rank, partner),
            )
            send.start()
            line.append(send)
    for step in range(count + reduce.levels - 1):
        for level in range(reduce.levels):
            if 0 <= step - level < count:
                reduce.stage(step - level, level)
    for copy in line:
        copy.wait_recv()
        copy.wait_send()
    rows = backs[0].shape[1]
    chunk = math.gcd(rows, 32)
    for number, back in enumerate(backs):

        def one(index, unused):
            at = pl.ds(index * chunk, chunk)
            total = back[depth, at, :].astype(jnp.float32)
            for step in range(DOCS - 1):
                total = total + landing[number, step, at, :].astype(jnp.float32)
            back_outs[number][at, :] = total.astype(jnp.bfloat16)
            return unused

        lax.fori_loop(0, rows // chunk, one, 0)
    for number in range(count):
        reduce.write(number).wait()


def reduce_call(grads, backs):
    count = len(grads)
    vmem = pl.BlockSpec(memory_space=pltpu.VMEM)
    anywhere = pl.BlockSpec(memory_space=pl.ANY)
    scratch, load_shapes, shared = [], [], []
    for grad in grads:
        scratch += buffer_shapes(grad.shape[1], grad.shape[2], grad.dtype)
        shape = ((4,) + grad.shape[1:], grad.dtype)
        held = [i for i, s in enumerate(load_shapes) if s == shape]
        if len(held) < 2:
            shared.append(len(load_shapes))
            load_shapes.append(shape)
        else:
            turns = [i for i in shared if load_shapes[i] == shape]
            shared.append(held[0] if turns[-1] == held[1] else held[1])
    scratch += [pltpu.VMEM(*shape) for shape in load_shapes]
    return pl.pallas_call(
        functools.partial(reduce_kernel, count, shared),
        out_shape=[jax.ShapeDtypeStruct(g.shape[1:], g.dtype) for g in grads]
        + [jax.ShapeDtypeStruct(b.shape[1:], b.dtype) for b in backs],
        in_specs=[anywhere] * count + [vmem] * 2,
        out_specs=[anywhere] * count + [vmem] * 2,
        scratch_shapes=scratch
        + [
            pltpu.VMEM((2, DOCS - 1) + backs[0].shape[1:], jnp.bfloat16),
            pltpu.SemaphoreType.DMA((count, 12)),
            pltpu.SemaphoreType.DMA((count, 12)),
            pltpu.SemaphoreType.DMA((count, 5)),
            pltpu.SemaphoreType.DMA((2, DOCS - 1)),
            pltpu.SemaphoreType.DMA((2, DOCS - 1)),
        ],
        compiler_params=pltpu.CompilerParams(
            collective_id=2, has_side_effects=True, vmem_limit_bytes=60 * 2**20
        ),
        name="reduce_all",
    )(*grads, *backs)


def pack_small(norms, table):
    rows = [n.astype(jnp.float32) for n in norms]
    rows.append(jnp.pad(table.astype(jnp.float32), (0, 128 - table.shape[0])))
    return jnp.pad(jnp.stack(rows), ((0, 12), (0, 0)))


def by_document(
    hidden_in,
    encoder_states,
    segment_ids,
    encoder_docs,
    self_query,
    self_key,
    self_value,
    self_out,
    cross_query,
    cross_key,
    cross_value,
    cross_out,
    feed_gate,
    feed_up,
    feed_down,
    norm_self,
    norm_cross,
    norm_feed,
    bias_table,
    out_grad,
):
    width = hidden_in.shape[2]
    total = segment_ids.shape[1]
    most = total // 2
    encoded = encoder_states[0]
    small = pack_small((norm_self, norm_cross, norm_feed), bias_table)
    gathered = gather_call(
        (
            small,
            cross_key,
            cross_value,
            self_query,
            self_key,
            self_value,
            self_out,
            cross_query,
            cross_out,
            feed_gate,
            feed_up,
            feed_down,
        ),
        hidden_in[0],
        out_grad[0],
    )
    smalls = gathered[0]
    w_ck, w_cv, w_sq, w_sk, w_sv, w_so, w_cq, w_co, w_fg, w_fu, w_fd = (
        w.reshape(-1, w.shape[2]) for w in gathered[1:12]
    )
    all_tokens = gathered[12].reshape(total, width)
    all_cotangent = gathered[13].reshape(total, width)
    gain_self, gain_cross, gain_feed = (smalls[:, i].reshape(-1) for i in range(3))
    table = smalls[:, 3, : bias_table.shape[0]].reshape(H, BUCKETS).astype(jnp.bfloat16)

    document = lax.dynamic_slice_in_dim(
        encoder_docs[0], lax.axis_index("ctx") * encoded.shape[0], 1, 0
    )
    segments = segment_ids[0]
    start = jnp.sum((segments < document).astype(jnp.int32))
    length = jnp.sum((segments == document).astype(jnp.int32))
    row = lax.broadcasted_iota(jnp.int32, (most, total), 0)
    column = lax.broadcasted_iota(jnp.int32, (most, total), 1)
    chosen = ((row + start == column) & (row < length)).astype(jnp.bfloat16)

    inputs = product(chosen, all_tokens)
    grad_after = product(chosen, all_cotangent)
    grad_round = grad_after.astype(jnp.bfloat16)

    position = jnp.arange(most, dtype=jnp.int32)
    distance = position[:, None] - position[None, :]
    causal = (distance >= 0)[None]
    onehot = bucket_onehot(jnp.maximum(distance, 0))

    def heads(values):
        return values.reshape(values.shape[0], H, HD)

    def flat(values):
        return values.reshape(values.shape[0], H * HD).astype(jnp.bfloat16)

    def attend(q, k, v, bias, allowed):
        scores = jnp.einsum("qhd,khd->hqk", q, k, preferred_element_type=jnp.float32)
        if bias is not None:
            scores = jnp.where(allowed, scores + bias, masked_value)
        p = jax.nn.softmax(scores, axis=-1)
        out = jnp.einsum(
            "hqk,khd->qhd", p.astype(jnp.bfloat16), v, preferred_element_type=jnp.float32
        )
        return (p, out)

    def attend_back(q, k, v, p, grad):
        grad_p = jnp.einsum("qhd,khd->hqk", grad, v, preferred_element_type=jnp.float32)
        grad_s = p * (grad_p - jnp.sum(p * grad_p, axis=-1, keepdims=True))
        rounded = grad_s.astype(jnp.bfloat16)
        grad_q = jnp.einsum("hqk,khd->qhd", rounded, k, preferred_element_type=jnp.float32)
        grad_k = jnp.einsum("hqk,qhd->khd", rounded, q, preferred_element_type=jnp.float32)
        grad_v = jnp.einsum(
            "hqk,qhd->khd", p.astype(jnp.bfloat16), grad, preferred_element_type=jnp.float32
        )
        return (grad_s, flat(grad_q), flat(grad_k), flat(grad_v))

    self_normed = normalize(inputs, gain_self).astype(jnp.bfloat16)
    queries = heads(product(self_normed, w_sq).astype(jnp.bfloat16))
    keys = heads(product(self_normed, w_sk).astype(jnp.bfloat16))
    values = heads(product(self_normed, w_sv).astype(jnp.bfloat16))
    bias = jnp.einsum("qkb,hb->hqk", onehot, table, preferred_element_type=jnp.float32)
    self_p, self_heads = attend(queries, keys, values, bias, causal)
    self_attended = flat(self_heads)
    after_self = inputs + product(self_attended, w_so)
    cross_normed = normalize(after_self, gain_cross).astype(jnp.bfloat16)
    cross_q = heads(product(cross_normed, w_cq).astype(jnp.bfloat16))
    cross_k = heads(product(encoded, w_ck).astype(jnp.bfloat16))
    cross_v = heads(product(encoded, w_cv).astype(jnp.bfloat16))
    cross_p, cross_heads = attend(cross_q, cross_k, cross_v, None, None)
    cross_attended = flat(cross_heads)
    after_cross = after_self + product(cross_attended, w_co)
    feed_normed = normalize(after_cross, gain_feed).astype(jnp.bfloat16)
    gate_value = product(feed_normed, w_fg)
    up_value = product(feed_normed, w_fu)

    def gated(gate_in, up_in):
        return jax.nn.gelu(gate_in, approximate=True) * up_in

    hidden_units, pullback = jax.vjp(gated, gate_value, up_value)
    hidden_units = hidden_units.astype(jnp.bfloat16)
    layer_out = (after_cross + product(hidden_units, w_fd)).astype(jnp.bfloat16)

    grad_fd = product_left(hidden_units, grad_round)
    grad_gate, grad_up = pullback(product_right(grad_round, w_fd))
    gate_round = grad_gate.astype(jnp.bfloat16)
    up_round = grad_up.astype(jnp.bfloat16)
    grad_fg = product_left(feed_normed, gate_round)
    grad_fu = product_left(feed_normed, up_round)
    grad_normed = product_right(gate_round, w_fg) + product_right(up_round, w_fu)
    side, grad_gain_feed = norm_back(after_cross, gain_feed, grad_normed)
    grad_after_cross = grad_after + side
    cross_round = grad_after_cross.astype(jnp.bfloat16)
    grad_co = product_left(cross_attended, cross_round)
    grad_heads = heads(product_right(cross_round, w_co).astype(jnp.bfloat16))
    unused, grad_q, grad_k, grad_v = attend_back(cross_q, cross_k, cross_v, cross_p, grad_heads)
    grad_ck = product_left(encoded, grad_k)
    grad_cv = product_left(encoded, grad_v)
    encoder_grad = product_right(grad_k, w_ck) + product_right(grad_v, w_cv)
    grad_cq = product_left(cross_normed, grad_q)
    side, grad_gain_cross = norm_back(after_self, gain_cross, product_right(grad_q, w_cq))
    grad_after_self = grad_after_cross + side
    self_round = grad_after_self.astype(jnp.bfloat16)
    grad_so = product_left(self_attended, self_round)
    grad_heads = heads(product_right(self_round, w_so).astype(jnp.bfloat16))
    grad_s, grad_q, grad_k, grad_v = attend_back(queries, keys, values, self_p, grad_heads)
    grad_table = jnp.einsum(
        "hqk,qkb->hb", grad_s, onehot.astype(jnp.float32), precision=highest
    )
    grad_sq = product_left(self_normed, grad_q)
    grad_sk = product_left(self_normed, grad_k)
    grad_sv = product_left(self_normed, grad_v)
    grad_normed = (
        product_right(grad_q, w_sq) + product_right(grad_k, w_sk) + product_right(grad_v, w_sv)
    )
    side, grad_gain_self = norm_back(inputs, gain_self, grad_normed)
    hidden_grad = (grad_after_self + side).astype(jnp.bfloat16)

    def back(values):
        return product_left(chosen, values).astype(jnp.bfloat16).reshape(DOCS, -1, width)

    table_rows = jnp.pad(grad_table.reshape(8, -1), ((0, 0), (0, 64)))
    small_grads = jnp.stack(
        [g.reshape(8, 128) for g in (grad_gain_self, grad_gain_cross, grad_gain_feed)]
        + [table_rows],
        axis=1,
    )
    small_grads = jnp.pad(small_grads, ((0, 0), (0, 12), (0, 0)))

    def shards(grad):
        return grad.astype(jnp.bfloat16).reshape(8, -1, grad.shape[1])

    names = (
        grad_fd,
        grad_fg,
        grad_fu,
        grad_co,
        grad_ck,
        grad_cv,
        grad_cq,
        grad_so,
        grad_sq,
        grad_sk,
        grad_sv,
    )
    reduced = reduce_call(
        tuple(shards(g) for g in names) + (small_grads,), (back(layer_out), back(hidden_grad))
    )
    fd, fg, fu, co, ck, cv, cq, so, sq, sk, sv = (r.astype(jnp.float32) for r in reduced[:11])
    smalls = reduced[11]
    return (
        reduced[12][None],
        reduced[13].astype(jnp.float32)[None],
        encoder_grad[None],
        sq,
        sk,
        sv,
        so,
        cq,
        ck,
        cv,
        co,
        fg,
        fu,
        fd,
        smalls[0],
        smalls[1],
        smalls[2],
        smalls[3, : bias_table.shape[0]],
    )


def layer(sizes, *args):
    encoder_states, encoder_docs = args[1], args[3]
    whole_document = encoder_states.shape[1] * DOCS == encoder_docs.shape[1]
    if whole_document and sizes["fsdp"] == 8 and sizes["ctx"] == DOCS:
        return by_document(*args)
    return on_device(*args)


def solution(mesh):
    in_specs = (
        P("fsdp", "ctx", None),
        P("fsdp", "ctx", None),
        P("fsdp", None),
        P("fsdp", None),
        P("fsdp", None),
        P("fsdp", None),
        P("fsdp", None),
        P("fsdp", None),
        P("fsdp", None),
        P("fsdp", None),
        P("fsdp", None),
        P("fsdp", None),
        P("fsdp", None),
        P("fsdp", None),
        P("fsdp", None),
        P("fsdp"),
        P("fsdp"),
        P("fsdp"),
        P("fsdp"),
        P("fsdp", "ctx", None),
    )
    out_specs = (
        P("fsdp", "ctx", None),
        P("fsdp", "ctx", None),
        P("fsdp", "ctx", None),
        P("fsdp", None),
        P("fsdp", None),
        P("fsdp", None),
        P("fsdp", None),
        P("fsdp", None),
        P("fsdp", None),
        P("fsdp", None),
        P("fsdp", None),
        P("fsdp", None),
        P("fsdp", None),
        P("fsdp", None),
        P("fsdp"),
        P("fsdp"),
        P("fsdp"),
        P("fsdp"),
    )
    return jax.shard_map(
        functools.partial(layer, dict(mesh.shape)), mesh=mesh, in_specs=in_specs, out_specs=out_specs, check_vma=False
    )
```

```python
import functools
import math

import jax
import jax.numpy as jnp
from jax import lax
from jax.experimental import pallas as pl
from jax.experimental.pallas import tpu as pltpu
from jax.sharding import PartitionSpec as P

H = 16
HD = 64
BUCKETS = 32
DOCS = 4
MESH = pl.DeviceIdType.MESH


bucket_edges = (19, 21, 24, 27, 31, 35, 40, 46, 52, 59, 67, 77, 87, 99, 113)
epsilon = 1e-06
masked_value = -1e30
highest = lax.Precision.HIGHEST


def normalize(values, gain_vector):
    inverse_root = lax.rsqrt(jnp.mean(values * values, axis=-1, keepdims=True) + epsilon)
    return values * inverse_root * gain_vector


def norm_back(values, gain_vector, grad_normed):
    unused, pullback = jax.vjp(normalize, values, gain_vector)
    return pullback(grad_normed)


def product(left_side, right_side):
    return jnp.dot(left_side, right_side, preferred_element_type=jnp.float32)


def product_left(left_side, right_side):
    return lax.dot_general(
        left_side, right_side, (((0,), (0,)), ((), ())), preferred_element_type=jnp.float32
    )


def product_right(left_side, right_side):
    return lax.dot_general(
        left_side, right_side, (((1,), (1,)), ((), ())), preferred_element_type=jnp.float32
    )


def bucket_of(distance):
    bucket_index = jnp.minimum(distance, 16)
    for threshold in bucket_edges:
        bucket_index = bucket_index + (distance >= threshold).astype(jnp.int32)
    return bucket_index


def bucket_onehot(distance):
    return (bucket_of(distance)[:, :, None] == jnp.arange(BUCKETS, dtype=jnp.int32)).astype(jnp.bfloat16)


def split_blocks(rows_all):
    total_rows = rows_all.shape[0]
    block_rows = math.gcd(total_rows, 512)
    return (block_rows, rows_all.reshape(total_rows // block_rows, block_rows, H, HD))


def block_logits(query_heads, key_part, allowed, distance, table_rows):
    scores = jnp.einsum("qhd,khd->hqk", query_heads, key_part, preferred_element_type=jnp.float32)
    onehot = None
    if table_rows is not None:
        onehot = bucket_onehot(distance)
        scores = scores + jnp.einsum(
            "qkb,hb->hqk", onehot, table_rows, preferred_element_type=jnp.float32
        )
    return (jnp.where(allowed[None], scores, masked_value), onehot)


def attention_forward(query_heads, key_rows, value_rows, mask_of, table_rows):
    block_rows, key_blocks = split_blocks(key_rows)
    unused, value_blocks = split_blocks(value_rows)
    numbers = jnp.arange(key_blocks.shape[0], dtype=jnp.int32)
    query_count = query_heads.shape[0]

    def total_step(carried, element):
        number, key_part = element
        allowed, distance = mask_of(number, block_rows)

        def total_live_branch(state):
            running, summed = state
            scores, unused_hot = block_logits(query_heads, key_part, allowed, distance, table_rows)
            newest = jnp.maximum(running, jnp.max(scores, axis=-1))
            exp_terms = jnp.where(allowed[None], jnp.exp(scores - newest[..., None]), 0.0)
            return (newest, summed * jnp.exp(running - newest) + jnp.sum(exp_terms, axis=-1))

        return (lax.cond(jnp.any(allowed), total_live_branch, lambda state: state, carried), None)

    start_state = (
        jnp.full((H, query_count), masked_value, jnp.float32),
        jnp.zeros((H, query_count), jnp.float32),
    )
    (running, summed), unused_out = lax.scan(total_step, start_state, (numbers, key_blocks))
    logsum = running + jnp.log(summed)

    def output_step(carried, element):
        number, key_part, value_part = element
        allowed, distance = mask_of(number, block_rows)

        def output_live_branch(state):
            scores, unused_hot = block_logits(query_heads, key_part, allowed, distance, table_rows)
            weights = jnp.where(allowed[None], jnp.exp(scores - logsum[..., None]), 0.0).astype(
                jnp.bfloat16
            )
            return state + jnp.einsum(
                "hqk,khd->qhd", weights, value_part, preferred_element_type=jnp.float32
            )

        return (lax.cond(jnp.any(allowed), output_live_branch, lambda state: state, carried), None)

    output, unused_out = lax.scan(
        output_step,
        jnp.zeros((query_count, H, HD), jnp.float32),
        (numbers, key_blocks, value_blocks),
    )
    return (output, logsum)


def attention_delta(query_heads, key_rows, value_rows, grad_heads, logsum, mask_of, table_rows):
    block_rows, key_blocks = split_blocks(key_rows)
    unused, value_blocks = split_blocks(value_rows)
    numbers = jnp.arange(key_blocks.shape[0], dtype=jnp.int32)
    query_count = query_heads.shape[0]

    def delta_step(carried, element):
        number, key_part, value_part = element
        allowed, distance = mask_of(number, block_rows)

        def delta_live_branch(state):
            scores, unused_hot = block_logits(query_heads, key_part, allowed, distance, table_rows)
            weights = jnp.where(allowed[None], jnp.exp(scores - logsum[..., None]), 0.0)
            grad_weights = jnp.einsum(
                "qhd,khd->hqk", grad_heads, value_part, preferred_element_type=jnp.float32
            )
            return state + jnp.sum(weights * grad_weights, axis=-1)

        return (lax.cond(jnp.any(allowed), delta_live_branch, lambda state: state, carried), None)

    row_delta, unused_out = lax.scan(
        delta_step, jnp.zeros((H, query_count), jnp.float32), (numbers, key_blocks, value_blocks)
    )
    return row_delta


def attention_backward(
    query_heads, key_rows, value_rows, grad_heads, logsum, row_delta, mask_of, table_rows
):
    block_rows, key_blocks = split_blocks(key_rows)
    unused, value_blocks = split_blocks(value_rows)
    numbers = jnp.arange(key_blocks.shape[0], dtype=jnp.int32)
    query_count = query_heads.shape[0]
    part_shape = (block_rows, H, HD)

    def grad_step(carried, element):
        number, key_part, value_part = element
        allowed, distance = mask_of(number, block_rows)

        def grad_live_branch(state):
            grad_query, grad_table = state
            scores, onehot = block_logits(query_heads, key_part, allowed, distance, table_rows)
            weights = jnp.where(allowed[None], jnp.exp(scores - logsum[..., None]), 0.0)
            grad_weights = jnp.einsum(
                "qhd,khd->hqk", grad_heads, value_part, preferred_element_type=jnp.float32
            )
            grad_scores = weights * (grad_weights - row_delta[..., None])
            rounded = grad_scores.astype(jnp.bfloat16)
            grad_query = grad_query + jnp.einsum(
                "hqk,khd->qhd", rounded, key_part, preferred_element_type=jnp.float32
            )
            if table_rows is not None:
                grad_table = grad_table + jnp.einsum(
                    "hqk,qkb->hb", grad_scores, onehot.astype(jnp.float32), precision=highest
                )
            grad_key_part = jnp.einsum(
                "hqk,qhd->khd", rounded, query_heads, preferred_element_type=jnp.float32
            )
            grad_value_part = jnp.einsum(
                "hqk,qhd->khd",
                weights.astype(jnp.bfloat16),
                grad_heads,
                preferred_element_type=jnp.float32,
            )
            return ((grad_query, grad_table), (grad_key_part, grad_value_part))

        def dead_branch(state):
            return (state, (jnp.zeros(part_shape, jnp.float32), jnp.zeros(part_shape, jnp.float32)))

        return lax.cond(jnp.any(allowed), grad_live_branch, dead_branch, carried)

    table_shape = (H, BUCKETS) if table_rows is not None else (1, 1)
    start_state = (
        jnp.zeros((query_count, H, HD), jnp.float32),
        jnp.zeros(table_shape, jnp.float32),
    )
    (grad_query, grad_table), key_parts = lax.scan(
        grad_step, start_state, (numbers, key_blocks, value_blocks)
    )
    total_rows = key_rows.shape[0]
    return (
        grad_query,
        grad_table,
        key_parts[0].reshape(total_rows, H * HD),
        key_parts[1].reshape(total_rows, H * HD),
    )


def on_device(
    hidden_in,
    encoder_states,
    segment_ids,
    encoder_docs,
    self_query,
    self_key,
    self_value,
    self_out,
    cross_query,
    cross_key,
    cross_value,
    cross_out,
    feed_gate,
    feed_up,
    feed_down,
    norm_self,
    norm_cross,
    norm_feed,
    bias_table,
    out_grad,
):
    gathered = (
        lax.all_gather(self_query, "fsdp", axis=0, tiled=True),
        lax.all_gather(self_key, "fsdp", axis=0, tiled=True),
        lax.all_gather(self_value, "fsdp", axis=0, tiled=True),
        lax.all_gather(self_out, "fsdp", axis=0, tiled=True),
        lax.all_gather(cross_query, "fsdp", axis=0, tiled=True),
        lax.all_gather(cross_key, "fsdp", axis=0, tiled=True),
        lax.all_gather(cross_value, "fsdp", axis=0, tiled=True),
        lax.all_gather(cross_out, "fsdp", axis=0, tiled=True),
        lax.all_gather(feed_gate, "fsdp", axis=0, tiled=True),
        lax.all_gather(feed_up, "fsdp", axis=0, tiled=True),
        lax.all_gather(feed_down, "fsdp", axis=0, tiled=True),
        lax.all_gather(norm_self, "fsdp", axis=0, tiled=True),
        lax.all_gather(norm_cross, "fsdp", axis=0, tiled=True),
        lax.all_gather(norm_feed, "fsdp", axis=0, tiled=True),
        lax.all_gather(bias_table, "fsdp", axis=0, tiled=True),
    )
    tokens = hidden_in[0]
    encoded = encoder_states[0]
    segments = segment_ids[0]
    documents = encoder_docs[0]
    tok_rows = tokens.shape[0]
    first_row = lax.axis_index("ctx") * tok_rows
    query_pos = first_row + jnp.arange(tok_rows, dtype=jnp.int32)
    query_seg = lax.dynamic_slice_in_dim(segments, first_row, tok_rows, 0)

    def self_mask(number, block_rows):
        key_pos = number * block_rows + jnp.arange(block_rows, dtype=jnp.int32)
        key_seg = lax.dynamic_slice_in_dim(segments, number * block_rows, block_rows, 0)
        distance = query_pos[:, None] - key_pos[None, :]
        allowed = (distance >= 0) & (query_seg[:, None] == key_seg[None, :])
        return (allowed, jnp.maximum(distance, 0))

    def cross_mask(number, block_rows):
        key_doc = lax.dynamic_slice_in_dim(documents, number * block_rows, block_rows, 0)
        return (query_seg[:, None] == key_doc[None, :], None)

    inputs = tokens.astype(jnp.float32)
    self_normed = normalize(inputs, gathered[11].astype(jnp.float32)).astype(jnp.bfloat16)
    queries = product(self_normed, gathered[0]).astype(jnp.bfloat16)
    key_local = product(self_normed, gathered[1]).astype(jnp.bfloat16)
    value_local = product(self_normed, gathered[2]).astype(jnp.bfloat16)
    key_rows, value_rows = (
        lax.all_gather(key_local, "ctx", axis=0, tiled=True),
        lax.all_gather(value_local, "ctx", axis=0, tiled=True),
    )
    table_rows = gathered[14].reshape(H, BUCKETS)
    query_heads = queries.reshape(tok_rows, H, HD)
    key_heads = key_rows.reshape(-1, H, HD)
    value_heads = value_rows.reshape(-1, H, HD)
    self_heads, self_logsum = attention_forward(
        query_heads, key_heads, value_heads, self_mask, table_rows
    )
    self_attended = self_heads.reshape(tok_rows, H * HD).astype(jnp.bfloat16)
    after_self = inputs + product(self_attended, gathered[3])
    cross_normed = normalize(after_self, gathered[12].astype(jnp.float32)).astype(jnp.bfloat16)
    cross_queries = product(cross_normed, gathered[4]).astype(jnp.bfloat16)
    cross_key_local = product(encoded, gathered[5]).astype(jnp.bfloat16)
    cross_value_local = product(encoded, gathered[6]).astype(jnp.bfloat16)
    cross_keys, cross_values = (
        lax.all_gather(cross_key_local, "ctx", axis=0, tiled=True),
        lax.all_gather(cross_value_local, "ctx", axis=0, tiled=True),
    )
    cross_query_heads = cross_queries.reshape(tok_rows, H, HD)
    cross_key_heads = cross_keys.reshape(-1, H, HD)
    cross_value_heads = cross_values.reshape(-1, H, HD)
    cross_heads, cross_logsum = attention_forward(
        cross_query_heads, cross_key_heads, cross_value_heads, cross_mask, None
    )
    cross_attended = cross_heads.reshape(tok_rows, H * HD).astype(jnp.bfloat16)
    after_cross = after_self + product(cross_attended, gathered[7])
    feed_normed = normalize(after_cross, gathered[13].astype(jnp.float32)).astype(jnp.bfloat16)
    gate_value = product(feed_normed, gathered[8])
    up_value = product(feed_normed, gathered[9])
    hidden_units = (jax.nn.gelu(gate_value, approximate=True) * up_value).astype(jnp.bfloat16)
    layer_out = (after_cross + product(hidden_units, gathered[10])).astype(jnp.bfloat16)
    grad_after = out_grad[0].astype(jnp.float32)
    grad_round = grad_after.astype(jnp.bfloat16)
    grad_feed_down = product_left(hidden_units, grad_round)
    grad_hidden = product_right(grad_round, gathered[10])
    unused, pullback = jax.vjp(
        lambda gate_in, up_in: jax.nn.gelu(gate_in, approximate=True) * up_in, gate_value, up_value
    )
    grad_gate, grad_up = pullback(grad_hidden)
    gate_round = grad_gate.astype(jnp.bfloat16)
    up_round = grad_up.astype(jnp.bfloat16)
    grad_feed_gate = product_left(feed_normed, gate_round)
    grad_feed_up = product_left(feed_normed, up_round)
    grad_feed_normed = product_right(gate_round, gathered[8]) + product_right(up_round, gathered[9])
    grad_cross_side, grad_norm_feed = norm_back(
        after_cross, gathered[13].astype(jnp.float32), grad_feed_normed
    )
    grad_after_cross = grad_after + grad_cross_side
    cross_round = grad_after_cross.astype(jnp.bfloat16)
    grad_cross_out = product_left(cross_attended, cross_round)
    grad_cross_heads = (
        product_right(cross_round, gathered[7]).astype(jnp.bfloat16).reshape(tok_rows, H, HD)
    )
    cross_delta = attention_delta(
        cross_query_heads,
        cross_key_heads,
        cross_value_heads,
        grad_cross_heads,
        cross_logsum,
        cross_mask,
        None,
    )
    grad_cross_q, unused_table, grad_cross_k, grad_cross_v = attention_backward(
        cross_query_heads,
        cross_key_heads,
        cross_value_heads,
        grad_cross_heads,
        cross_logsum,
        cross_delta,
        cross_mask,
        None,
    )
    cross_key_grad, cross_value_grad = (
        lax.psum_scatter(
            grad_cross_k.astype(jnp.bfloat16), "ctx", scatter_dimension=0, tiled=True
        ).astype(jnp.float32),
        lax.psum_scatter(
            grad_cross_v.astype(jnp.bfloat16), "ctx", scatter_dimension=0, tiled=True
        ).astype(jnp.float32),
    )
    cross_key_round = cross_key_grad.astype(jnp.bfloat16)
    cross_value_round = cross_value_grad.astype(jnp.bfloat16)
    grad_cross_key = product_left(encoded, cross_key_round)
    grad_cross_value = product_left(encoded, cross_value_round)
    encoder_grad = product_right(cross_key_round, gathered[5]) + product_right(
        cross_value_round, gathered[6]
    )
    cross_query_round = grad_cross_q.reshape(tok_rows, H * HD).astype(jnp.bfloat16)
    grad_cross_query = product_left(cross_normed, cross_query_round)
    grad_cross_normed = product_right(cross_query_round, gathered[4])
    grad_self_side, grad_norm_cross = norm_back(
        after_self, gathered[12].astype(jnp.float32), grad_cross_normed
    )
    grad_after_self = grad_after_cross + grad_self_side
    self_round = grad_after_self.astype(jnp.bfloat16)
    grad_self_out = product_left(self_attended, self_round)
    grad_self_flat = product_right(self_round, gathered[3]).astype(jnp.bfloat16)
    grad_self_heads = grad_self_flat.reshape(tok_rows, H, HD)
    back_table = gathered[14].reshape(H, BUCKETS)
    self_delta = attention_delta(
        query_heads, key_heads, value_heads, grad_self_heads, self_logsum, self_mask, back_table
    )
    grad_self_q, grad_table, grad_self_k, grad_self_v = attention_backward(
        query_heads,
        key_heads,
        value_heads,
        grad_self_heads,
        self_logsum,
        self_delta,
        self_mask,
        back_table,
    )
    self_key_grad, self_value_grad = (
        lax.psum_scatter(
            grad_self_k.astype(jnp.bfloat16), "ctx", scatter_dimension=0, tiled=True
        ).astype(jnp.float32),
        lax.psum_scatter(
            grad_self_v.astype(jnp.bfloat16), "ctx", scatter_dimension=0, tiled=True
        ).astype(jnp.float32),
    )
    self_key_round = self_key_grad.astype(jnp.bfloat16)
    self_value_round = self_value_grad.astype(jnp.bfloat16)
    self_query_round = grad_self_q.reshape(tok_rows, H * HD).astype(jnp.bfloat16)
    grad_self_query = product_left(self_normed, self_query_round)
    grad_self_key = product_left(self_normed, self_key_round)
    grad_self_value = product_left(self_normed, self_value_round)
    grad_self_normed = (
        product_right(self_query_round, gathered[0])
        + product_right(self_key_round, gathered[1])
        + product_right(self_value_round, gathered[2])
    )
    grad_input_side, grad_norm_self = norm_back(
        inputs, gathered[11].astype(jnp.float32), grad_self_normed
    )
    hidden_grad = grad_after_self + grad_input_side
    grad_bias_table = grad_table.reshape(H * BUCKETS)
    pieces = (
        lax.psum_scatter(
            grad_self_query.astype(jnp.bfloat16), "fsdp", scatter_dimension=0, tiled=True
        ).astype(jnp.float32),
        lax.psum_scatter(
            grad_self_key.astype(jnp.bfloat16), "fsdp", scatter_dimension=0, tiled=True
        ).astype(jnp.float32),
        lax.psum_scatter(
            grad_self_value.astype(jnp.bfloat16), "fsdp", scatter_dimension=0, tiled=True
        ).astype(jnp.float32),
        lax.psum_scatter(
            grad_self_out.astype(jnp.bfloat16), "fsdp", scatter_dimension=0, tiled=True
        ).astype(jnp.float32),
        lax.psum_scatter(
            grad_cross_query.astype(jnp.bfloat16), "fsdp", scatter_dimension=0, tiled=True
        ).astype(jnp.float32),
        lax.psum_scatter(
            grad_cross_key.astype(jnp.bfloat16), "fsdp", scatter_dimension=0, tiled=True
        ).astype(jnp.float32),
        lax.psum_scatter(
            grad_cross_value.astype(jnp.bfloat16), "fsdp", scatter_dimension=0, tiled=True
        ).astype(jnp.float32),
        lax.psum_scatter(
            grad_cross_out.astype(jnp.bfloat16), "fsdp", scatter_dimension=0, tiled=True
        ).astype(jnp.float32),
        lax.psum_scatter(
            grad_feed_gate.astype(jnp.bfloat16), "fsdp", scatter_dimension=0, tiled=True
        ).astype(jnp.float32),
        lax.psum_scatter(
            grad_feed_up.astype(jnp.bfloat16), "fsdp", scatter_dimension=0, tiled=True
        ).astype(jnp.float32),
        lax.psum_scatter(
            grad_feed_down.astype(jnp.bfloat16), "fsdp", scatter_dimension=0, tiled=True
        ).astype(jnp.float32),
        lax.psum_scatter(
            grad_norm_self.astype(jnp.bfloat16), "fsdp", scatter_dimension=0, tiled=True
        ).astype(jnp.float32),
        lax.psum_scatter(
            grad_norm_cross.astype(jnp.bfloat16), "fsdp", scatter_dimension=0, tiled=True
        ).astype(jnp.float32),
        lax.psum_scatter(
            grad_norm_feed.astype(jnp.bfloat16), "fsdp", scatter_dimension=0, tiled=True
        ).astype(jnp.float32),
        lax.psum_scatter(
            grad_bias_table.astype(jnp.bfloat16), "fsdp", scatter_dimension=0, tiled=True
        ).astype(jnp.float32),
    )
    owned = (
        lax.psum(pieces[0].astype(jnp.bfloat16), "ctx").astype(jnp.float32),
        lax.psum(pieces[1].astype(jnp.bfloat16), "ctx").astype(jnp.float32),
        lax.psum(pieces[2].astype(jnp.bfloat16), "ctx").astype(jnp.float32),
        lax.psum(pieces[3].astype(jnp.bfloat16), "ctx").astype(jnp.float32),
        lax.psum(pieces[4].astype(jnp.bfloat16), "ctx").astype(jnp.float32),
        lax.psum(pieces[5].astype(jnp.bfloat16), "ctx").astype(jnp.float32),
        lax.psum(pieces[6].astype(jnp.bfloat16), "ctx").astype(jnp.float32),
        lax.psum(pieces[7].astype(jnp.bfloat16), "ctx").astype(jnp.float32),
        lax.psum(pieces[8].astype(jnp.bfloat16), "ctx").astype(jnp.float32),
        lax.psum(pieces[9].astype(jnp.bfloat16), "ctx").astype(jnp.float32),
        lax.psum(pieces[10].astype(jnp.bfloat16), "ctx").astype(jnp.float32),
        lax.psum(pieces[11].astype(jnp.bfloat16), "ctx").astype(jnp.float32),
        lax.psum(pieces[12].astype(jnp.bfloat16), "ctx").astype(jnp.float32),
        lax.psum(pieces[13].astype(jnp.bfloat16), "ctx").astype(jnp.float32),
        lax.psum(pieces[14].astype(jnp.bfloat16), "ctx").astype(jnp.float32),
    )
    return (
        layer_out[None],
        hidden_grad[None],
        encoder_grad[None],
        owned[0],
        owned[1],
        owned[2],
        owned[3],
        owned[4],
        owned[5],
        owned[6],
        owned[7],
        owned[8],
        owned[9],
        owned[10],
        owned[11],
        owned[12],
        owned[13],
        owned[14],
    )


def place():
    rank = lax.axis_index("fsdp")
    core = lax.rem(rank, 2)
    along_x = lax.rem(lax.div(rank, 2), 2)
    along_y = lax.div(rank, 4)
    return (rank, core, along_x, along_y, lax.axis_index("ctx"))


def greet(partners):
    barrier = pltpu.get_barrier_semaphore()
    for partner in partners:
        pl.semaphore_signal(barrier, inc=1, device_id=partner, device_id_type=MESH)
    pl.semaphore_wait(barrier, len(partners))


def remote(source, target, send_sem, recv_sem, device):
    return pltpu.make_async_remote_copy(
        src_ref=source,
        dst_ref=target,
        send_sem=send_sem,
        recv_sem=recv_sem,
        device_id=device,
        device_id_type=MESH,
    )


class Gather:
    def __init__(self, owns, fulls, send_sems, recv_sems, local_sems):
        rank, core, along_x, along_y, depth = place()
        self.owns, self.fulls = owns, fulls
        self.send_sems, self.recv_sems, self.local_sems = send_sems, recv_sems, local_sems
        self.rank = rank
        self.by_x = rank + 2 - 4 * along_x
        self.by_y = rank + 4 - 8 * along_y
        self.diag = self.by_x + 4 - 8 * along_y
        self.to_x = (self.by_x, depth)
        self.to_y = (self.by_y, depth)
        self.to_core = (rank + 1 - 2 * core, depth)
        self.shift = 1 - 2 * core

    def rows(self, number, slot, half):
        size = self.owns[number].shape[0]
        start = pl.multiple_of(slot * size, size)
        if half is None:
            return self.fulls[number].at[pl.ds(start, size)]
        size = size // 2
        return self.fulls[number].at[pl.ds(pl.multiple_of(start + half * size, size), size)]

    def copy(self, number, kind, slot, half, device, own=False):
        target = self.rows(number, slot, half)
        return remote(
            self.owns[number] if own else target,
            target,
            self.send_sems.at[number, kind],
            self.recv_sems.at[number, kind],
            device,
        )

    def sent(self, number, kind):
        slot, half, device = (
            (self.rank, None, self.to_x),
            (self.rank, None, self.to_y),
            (self.rank, None, self.to_core),
            (self.by_x, 0, self.to_y),
            (self.by_y, 1, self.to_x),
            (self.by_x, None, self.to_core),
            (self.by_y, None, self.to_core),
            (self.diag, 0, self.to_core),
            (self.diag, 1, self.to_core),
        )[kind]
        return self.copy(number, kind, slot, half, device, kind < 3)

    def landed(self, number, kind):
        shift = self.shift
        slot, half, device = (
            (self.by_x, None, self.to_x),
            (self.by_y, None, self.to_y),
            (self.rank + shift, None, self.to_core),
            (self.diag, 0, self.to_y),
            (self.diag, 1, self.to_x),
            (self.by_x + shift, None, self.to_core),
            (self.by_y + shift, None, self.to_core),
            (self.diag + shift, 0, self.to_core),
            (self.diag + shift, 1, self.to_core),
        )[kind]
        return self.copy(number, kind, slot, half, device)

    def local(self, number):
        return pltpu.make_async_copy(
            self.owns[number], self.rows(number, self.rank, None), self.local_sems.at[number]
        )

    def issue(self, number):
        for kind in range(3):
            self.sent(number, kind).start()
        self.local(number).start()

    def relay(self, number):
        self.landed(number, 0).wait_recv()
        self.sent(number, 3).start()
        self.landed(number, 1).wait_recv()
        self.sent(number, 4).start()
        self.sent(number, 5).start()
        self.sent(number, 6).start()

    def spread(self, number):
        self.landed(number, 3).wait_recv()
        self.sent(number, 7).start()
        self.landed(number, 4).wait_recv()
        self.sent(number, 8).start()

    def finish(self, number):
        for kind in (2, 5, 6, 7, 8):
            self.landed(number, kind).wait_recv()
        for kind in range(9):
            self.sent(number, kind).wait_send()
        self.local(number).wait()


def column_partners(rank, depth):
    return [(rank, lax.rem(depth + step, DOCS)) for step in range(1, DOCS)]


def tile(index, size=256):
    return pl.ds(pl.multiple_of(index * size, size), size)


def each(count, body):
    def one(index, unused):
        body(index)
        return unused

    lax.fori_loop(0, count, one, 0)


def by_columns(left, right, write):
    def one(index):
        at = tile(index)
        write(at, product(left[...], right[:, at]))

    each(right.shape[1] // 256, one)


def store_as(target):
    def write(at, value):
        target[:, at] = value.astype(target.dtype)

    return write


def rms_rows(values, gain, normed):
    def one(index):
        at = tile(index, 32)
        v = values[at, :]
        root = lax.rsqrt(jnp.mean(v * v, axis=-1, keepdims=True) + epsilon)
        normed[at, :] = (v * root * gain).astype(jnp.bfloat16)

    each(values.shape[0] // 32, one)


def half_masks():
    lane = lax.broadcasted_iota(jnp.int32, (1, 2 * HD), 1)
    low = (lane < HD).astype(jnp.float32)
    return (low.astype(jnp.bfloat16), (1.0 - low).astype(jnp.bfloat16))


def causal_bias(smalls, spread, pair, half):
    row = smalls[tile(pair, 16), :][3:4]
    size = spread.shape[2]
    row = jnp.broadcast_to(row, (8, 128)).astype(jnp.bfloat16)
    line = product(row, spread[half])[0:1]
    bias = pltpu.roll(jnp.broadcast_to(line, (size, size)), 0, 1, stride=1, stride_axis=0)
    here = lax.broadcasted_iota(jnp.int32, (size, size), 0)
    there = lax.broadcasted_iota(jnp.int32, (size, size), 1)
    return jnp.where(there <= here, bias, masked_value)


def softmax_rows(scores):
    terms = jnp.exp(scores - jnp.max(scores, axis=-1, keepdims=True))
    return terms * (1.0 / jnp.sum(terms, axis=-1, keepdims=True))


def attend_heads(queries, keys, values, out, bias_of):
    masks = half_masks()

    def pair(index):
        at = tile(index, 2 * HD)
        q, k, v = queries[:, at], keys[:, at], values[:, at]
        total = jnp.zeros(q.shape, jnp.float32)
        for half in range(2):
            scores = product_right(q * masks[half], k)
            if bias_of is not None:
                scores = scores + bias_of(index, half)
            weights = softmax_rows(scores).astype(jnp.bfloat16)
            total = total + product(weights, v * masks[half])
        out[:, at] = total.astype(jnp.bfloat16)

    each(H // 2, pair)


def column_partners(rank, depth):
    return [(rank, lax.rem(depth + step, DOCS)) for step in range(1, DOCS)]


class Kept:
    inputs, normed, q, k, u, o1, after, normed2, cq = range(9)
    ck, cv, o2, after2, normed3, w, slope, gelu, cot = range(9, 18)
    normed_t, q_t, o1_t, normed2_t, cq_t, o2_t, normed3_t, states_t = range(18, 26)
    count = 26
    wide = (14, 15, 16)
    exact = (0, 6, 12, 15, 16)
    states = (9, 10)
    flipped = tuple(range(18, 26))
    inside = (1, 5, 7, 11, 13)


def forward_kernel(count, *refs):
    owns, refs = refs[:count], refs[count:]
    (tokens, cotangent, chosen, encoded, spread), refs = refs[:5], refs[5:]
    fulls, refs = refs[:count], refs[count:]
    n = Kept.count
    outs, refs = refs[:n], refs[n:]
    grad_out, refs = refs[0], refs[1:]
    keep, refs = refs[:n], refs[n:]
    (
        grad_fd,
        smalls,
        gains,
        all_tokens,
        all_cotangent,
        square,
        wide,
        send_sems,
        recv_sems,
        local_sems,
        line_send,
        line_recv,
        line_local,
        load_sems,
        save_sems,
    ) = refs
    rank, core, along_x, along_y, depth = place()
    gather = Gather(owns, fulls, send_sems, recv_sems, local_sems)
    column = column_partners(rank, depth)
    greet([gather.to_x, gather.to_y, gather.to_core] + column)

    def line_copies(number):
        own, whole = ((tokens, all_tokens), (cotangent, all_cotangent))[number]
        rows = own.shape[0]
        at = whole.at[pl.ds(pl.multiple_of(depth * rows, rows), rows)]
        here = pltpu.make_async_copy(own, at, line_local.at[number])
        sends, receives = [], []
        for step, partner in enumerate(column):
            sems = (line_send.at[number, step], line_recv.at[number, step])
            sends.append(remote(own, at, sems[0], sems[1], partner))
            origin = lax.rem(depth + DOCS - 1 - step, DOCS)
            landing = whole.at[pl.ds(pl.multiple_of(origin * rows, rows), rows)]
            receives.append(remote(own, landing, sems[0], sems[1], partner))
        return (here, sends, receives)

    def line_finish(number):
        here, sends, receives = line_copies(number)
        here.wait()
        for copy in receives:
            copy.wait_recv()
        for copy in sends:
            copy.wait_send()

    for number in range(2):
        here, sends, unused = line_copies(number)
        here.start()
        for copy in sends:
            copy.start()

    def flip(source, name):
        turn(source, keep[name])
        save(name)

    def save(name):
        if name in Kept.inside:
            return
        pltpu.make_async_copy(keep[name], outs[name], save_sems.at[name]).start()

    def load(number, buffer):
        copy = pltpu.make_async_copy(fulls[number], buffer, load_sems.at[number])
        copy.start()
        copy.wait()

    def project(left, number, name):
        load(number, square)
        by_columns(left, square, store_as(keep[name]))
        save(name)

    def residual(before, left, number, name, gain, normed, turned):
        load(number, square)

        def write(at, value):
            keep[name][:, at] = keep[before][:, at] + value

        by_columns(keep[left], square, write)
        save(name)
        rms_rows(keep[name], gains[gain : gain + 1, :], keep[normed])
        flip(keep[normed], turned)

    def start():
        load(0, smalls)
        for slot in range(8):
            gains[0:3, 128 * slot : 128 * slot + 128] = smalls[16 * slot : 16 * slot + 3, :]
        line_finish(0)
        by_columns(chosen, all_tokens, store_as(keep[Kept.inputs]))
        save(Kept.inputs)
        rms_rows(keep[Kept.inputs], gains[0:1, :], keep[Kept.normed])
        flip(keep[Kept.normed], Kept.normed_t)
        flip(encoded, Kept.states_t)

    def keys():
        flip(keep[Kept.q], Kept.q_t)
        project(keep[Kept.normed], 4, Kept.k)

    def self_heads():
        project(keep[Kept.normed], 5, Kept.u)
        attend_heads(
            keep[Kept.q], keep[Kept.k], keep[Kept.u], keep[Kept.o1], functools.partial(causal_bias, smalls, spread)
        )
        flip(keep[Kept.o1], Kept.o1_t)

    def cross_heads():
        project(keep[Kept.normed2], 7, Kept.cq)
        flip(keep[Kept.cq], Kept.cq_t)
        attend_heads(keep[Kept.cq], keep[Kept.ck], keep[Kept.cv], keep[Kept.o2], None)
        flip(keep[Kept.o2], Kept.o2_t)
        line_finish(1)
        by_columns(chosen, all_cotangent, store_as(keep[Kept.cot]))
        save(Kept.cot)

    def gate():
        load(9, wide)
        by_columns(keep[Kept.normed3], wide, store_as(keep[Kept.slope]))

    def up():
        load(10, wide)
        scale = math.sqrt(2.0 / math.pi)

        def write(at, b):
            a = keep[Kept.slope][:, at]
            t = jnp.tanh(scale * (a + 0.044715 * (a * a * a)))
            gelu = 0.5 * a * (1.0 + t)
            slope = 0.5 * (1.0 + t) + 0.5 * a * (1.0 - t * t) * scale * (
                1.0 + 3 * 0.044715 * (a * a)
            )
            keep[Kept.gelu][:, at] = gelu
            keep[Kept.slope][:, at] = slope * b
            w = (gelu * b).astype(jnp.bfloat16)
            keep[Kept.w][:, at] = w
            grad_fd[at, :] = product_left(w, keep[Kept.cot][...]).astype(jnp.bfloat16)

        by_columns(keep[Kept.normed3], wide, write)
        for name in (Kept.gelu, Kept.slope, Kept.w):
            save(name)
        pltpu.make_async_copy(grad_fd, grad_out, save_sems.at[n]).start()

    compute = (
        start,
        lambda: project(encoded, 1, Kept.ck),
        lambda: project(encoded, 2, Kept.cv),
        lambda: project(keep[Kept.normed], 3, Kept.q),
        keys,
        self_heads,
        lambda: residual(Kept.inputs, Kept.o1, 6, Kept.after, 1, Kept.normed2, Kept.normed2_t),
        cross_heads,
        lambda: residual(Kept.after, Kept.o2, 8, Kept.after2, 2, Kept.normed3, Kept.normed3_t),
        gate,
        up,
        lambda: None,
    )
    for step in range(count + 4):
        if step < count:
            gather.issue(step)
        if 0 <= step - 2 < count:
            gather.relay(step - 2)
        if 0 <= step - 3 < count:
            gather.spread(step - 3)
        if 0 <= step - 4 < count:
            gather.finish(step - 4)
            compute[step - 4]()
    for name in range(n):
        if name not in Kept.inside:
            pltpu.make_async_copy(keep[name], outs[name], save_sems.at[name]).wait()
    pltpu.make_async_copy(grad_fd, grad_out, save_sems.at[n]).wait()


def forward_call(shards, tokens, cotangent, chosen, encoded, spread):
    count = len(shards)
    vmem = pl.BlockSpec(memory_space=pltpu.VMEM)
    anywhere = pl.BlockSpec(memory_space=pl.ANY)
    most, total = chosen.shape
    shapes = [jax.ShapeDtypeStruct((8 * s.shape[0], s.shape[1]), s.dtype) for s in shards]
    saved = []
    for name in range(Kept.count):
        if name in Kept.flipped:
            rows = encoded.shape[0] if name == Kept.states_t else most
            saved.append(((shards[1].shape[1], rows), jnp.bfloat16))
            continue
        rows = encoded.shape[0] if name in Kept.states else most
        width = shards[9].shape[1] if name in Kept.wide else shards[1].shape[1]
        saved.append(((rows, width), jnp.float32 if name in Kept.exact else jnp.bfloat16))
    shapes += [jax.ShapeDtypeStruct(*s) for s in saved]
    down = shapes[count - 1]
    square = shards[1].shape[1]
    return pl.pallas_call(
        functools.partial(forward_kernel, count),
        out_shape=shapes + [down],
        in_specs=[vmem] * (count + 5),
        out_specs=[anywhere] * (len(shapes) + 1),
        scratch_shapes=[pltpu.VMEM(*s) for s in saved]
        + [
            pltpu.VMEM(down.shape, down.dtype),
            pltpu.VMEM(shapes[0].shape, jnp.float32),
            pltpu.VMEM((8, square), jnp.float32),
            pltpu.VMEM((total, square), jnp.bfloat16),
            pltpu.VMEM((total, square), jnp.bfloat16),
            pltpu.VMEM((square, square), jnp.bfloat16),
            pltpu.VMEM((square, shards[9].shape[1]), jnp.bfloat16),
            pltpu.SemaphoreType.DMA((count, 9)),
            pltpu.SemaphoreType.DMA((count, 9)),
            pltpu.SemaphoreType.DMA((count,)),
            pltpu.SemaphoreType.DMA((2, DOCS - 1)),
            pltpu.SemaphoreType.DMA((2, DOCS - 1)),
            pltpu.SemaphoreType.DMA((2,)),
            pltpu.SemaphoreType.DMA((count,)),
            pltpu.SemaphoreType.DMA((len(saved) + 1,)),
        ],
        compiler_params=pltpu.CompilerParams(
            collective_id=1, has_side_effects=True, vmem_limit_bytes=60 * 2**20
        ),
        name="forward",
    )(*shards, tokens, cotangent, chosen, encoded, spread)


def add_rows(target, source):
    rows = target.shape[-2]
    step = math.gcd(rows, 32)

    def one(index, unused):
        at = pl.ds(index * step, step)
        target[at, :] = target[at, :] + source[at, :]
        return unused

    lax.fori_loop(0, rows // step, one, 0)


class Reduce:
    def __init__(self, pieces, buffers, load, send_sems, recv_sems, local_sems):
        rank, core, along_x, along_y, depth = place()
        self.pieces, self.buffers, self.load = pieces, buffers, load
        self.send_sems, self.recv_sems, self.local_sems = send_sems, recv_sems, local_sems
        self.core, self.along_x, self.along_y = core, along_x, along_y
        self.block = 2 * along_y + along_x
        self.to_x = (rank + 2 - 4 * along_x, depth)
        self.to_y = (rank + 4 - 8 * along_y, depth)
        self.to_core = (rank + 1 - 2 * core, depth)
        self.inner = (depth == 1) | (depth == 2)
        self.to_line = (rank, depth + 1 - 2 * lax.rem(depth, 2))
        self.to_middle = (rank, 3 - depth)
        self.partners = [self.to_x, self.to_y, self.to_core, self.to_line, self.to_middle]

    def copy(self, number, kind, source, target, device):
        return remote(
            source,
            target,
            self.send_sems.at[number, kind],
            self.recv_sems.at[number, kind],
            device,
        )

    def halves(self, number):
        size = self.pieces[number].rows // 2
        return (pl.ds(0, size), pl.ds(size, size))

    def core_copies(self, number):
        piece, both = self.pieces[number], self.buffers[number][0]
        return [
            self.copy(number, q, piece.slot(2 * q + 1 - self.core), both.at[q], self.to_core)
            for q in range(4)
        ]

    def own_load(self, number, q):
        return pltpu.make_async_copy(
            self.pieces[number].slot(2 * q + self.core),
            self.load[number].at[q % 2],
            self.local_sems.at[number, q],
        )

    def first_copies(self, number):
        both, from_x, from_y = self.buffers[number][:3]
        low, high = self.halves(number)
        copies = []
        for other in range(2):
            copies.append(
                self.copy(
                    number,
                    4 + other,
                    both.at[2 * other + 1 - self.along_x, low],
                    from_x.at[other],
                    self.to_x,
                )
            )
        for other in range(2):
            copies.append(
                self.copy(
                    number,
                    6 + other,
                    both.at[2 * (1 - self.along_y) + other, high],
                    from_y.at[other],
                    self.to_y,
                )
            )
        return copies

    def second_copies(self, number):
        both, unused_x, unused_y, late_x, late_y = self.buffers[number][:5]
        low, high = self.halves(number)
        return [
            self.copy(
                number,
                8,
                both.at[2 * (1 - self.along_y) + self.along_x, low],
                late_y,
                self.to_y,
            ),
            self.copy(
                number,
                9,
                both.at[2 * self.along_y + 1 - self.along_x, high],
                late_x,
                self.to_x,
            ),
        ]

    def line_copy(self, number):
        return self.copy(
            number,
            10,
            self.buffers[number][0].at[self.block],
            self.buffers[number][5],
            self.to_line,
        )

    def middle_copy(self, number):
        return self.copy(
            number,
            11,
            self.buffers[number][0].at[self.block],
            self.buffers[number][6],
            self.to_middle,
        )

    def return_copy(self, number):
        return self.copy(
            number,
            10,
            self.buffers[number][5],
            self.buffers[number][5],
            self.to_line,
        )

    def write(self, number):
        return pltpu.make_async_copy(
            self.buffers[number][5],
            self.pieces[number].out.at[:, self.pieces[number].columns],
            self.local_sems.at[number, 4],
        )

    def stage(self, number, level):
        both, from_x, from_y, late_x, late_y, on_line, on_middle = self.buffers[number]
        low, high = self.halves(number)
        if level == 0:
            for copy in self.core_copies(number):
                copy.start()
            self.own_load(number, 0).start()
            self.own_load(number, 1).start()
        elif level == 1:
            for q, copy in enumerate(self.core_copies(number)):
                copy.wait_recv()
                self.own_load(number, q).wait()
                add_rows(both.at[q], self.load[number].at[q % 2])
                if q < 2:
                    self.own_load(number, q + 2).start()
            for copy in self.first_copies(number):
                copy.start()
        elif level == 2:
            copies = self.first_copies(number)
            for other in range(2):
                copies[other].wait_recv()
                copies[other].wait_send()
                add_rows(both.at[2 * other + self.along_x, low], from_x.at[other])
            for other in range(2):
                copies[2 + other].wait_recv()
                copies[2 + other].wait_send()
                add_rows(both.at[2 * self.along_y + other, high], from_y.at[other])
            for copy in self.second_copies(number):
                copy.start()
        elif level == 3:
            to_y, to_x = self.second_copies(number)
            to_y.wait_recv()
            add_rows(both.at[self.block, low], late_y)
            to_x.wait_recv()
            add_rows(both.at[self.block, high], late_x)
            to_y.wait_send()
            to_x.wait_send()

            @pl.when(jnp.logical_not(self.inner))
            def _():
                self.line_copy(number).start()
        elif level == 4:

            @pl.when(self.inner)
            def _():
                self.line_copy(number).wait_recv()
                add_rows(both.at[self.block], on_line)
                self.middle_copy(number).start()
        elif level == 5:

            @pl.when(self.inner)
            def _():
                middle = self.middle_copy(number)
                middle.wait_recv()
                rows = on_line.shape[0]
                step = math.gcd(rows, 32)

                def one(index, unused):
                    at = pl.ds(index * step, step)
                    on_line[at, :] = both[self.block, at, :] + on_middle[at, :]
                    return unused

                lax.fori_loop(0, rows // step, one, 0)
                middle.wait_send()
                self.return_copy(number).start()
        else:
            line = self.line_copy(number)

            @pl.when(jnp.logical_not(self.inner))
            def _():
                line.wait_send()
                line.wait_recv()

            @pl.when(self.inner)
            def _():
                self.return_copy(number).wait_send()

            for copy in self.core_copies(number):
                copy.wait_send()
            self.write(number).start()

    levels = 7


def buffer_shapes(rows, width, dtype):
    return [
        pltpu.VMEM((4, rows, width), dtype),
        pltpu.VMEM((2, rows // 2, width), dtype),
        pltpu.VMEM((2, rows // 2, width), dtype),
        pltpu.VMEM((rows // 2, width), dtype),
        pltpu.VMEM((rows // 2, width), dtype),
        pltpu.VMEM((rows, width), dtype),
        pltpu.VMEM((rows, width), dtype),
    ]


class Piece:
    def __init__(self, grad, out, start, width):
        self.grad, self.out = grad, out
        self.columns = pl.ds(start, width)
        self.rows, self.width = grad.shape[1], width

    def slot(self, index):
        return self.grad.at[index, :, self.columns]


def pieces_of(width):
    return [(start, min(1024, width - start)) for start in range(0, width, 1024)]


def rms_back(values, cotangent, gain, carry, out, gain_grad):
    def one(index):
        at = tile(index, 32)
        v, gz = values[at, :], cotangent[at, :]
        root = lax.rsqrt(jnp.mean(v * v, axis=-1, keepdims=True) + epsilon)
        scaled = gain * gz
        inner = jnp.mean(scaled * v, axis=-1, keepdims=True)
        gain_grad[...] += jnp.sum(gz * v * root, axis=0, keepdims=True)
        result = carry[at, :].astype(jnp.float32) + root * scaled - v * (root * root * root * inner)
        out[at, :] = result.astype(out.dtype)

    gain_grad[...] = jnp.zeros_like(gain_grad)
    each(values.shape[0] // 32, one)


def diagonal_sums(grad):
    size = grad.shape[1]
    total = grad[0:8]
    for group in range(1, grad.shape[0] // 8):
        part = grad[8 * group : 8 * group + 8]
        total = total + pltpu.roll(part, size - 8 * group, 1)
    row = lax.broadcasted_iota(jnp.int32, total.shape, 0)
    line = jnp.where(row == 0, total, 0.0)
    for step in range(1, 8):
        line = line + jnp.where(row == step, pltpu.roll(total, size - step, 1), 0.0)
    return jnp.sum(line, axis=0, keepdims=True)


def attend_back_heads(
    first, last, queries, flipped, keys, values, grad, grad_flipped, grad_q, grad_k, grad_v, bias_of, bias_grad
):
    masks = half_masks()
    row = lax.broadcasted_iota(jnp.int32, (2 * HD, 1), 0)
    low = (row < HD).astype(jnp.float32)
    sides = (low.astype(jnp.bfloat16), (1.0 - low).astype(jnp.bfloat16))

    def pair(index):
        at = tile(index + first, 2 * HD)
        q, k, v, g = queries[:, at], keys[:, at], values[:, at], grad[:, at]
        qt, gt = flipped[at, :], grad_flipped[at, :]
        total_q = jnp.zeros(q.shape, jnp.float32)
        total_k = jnp.zeros((2 * HD, k.shape[0]), jnp.float32)
        total_v = jnp.zeros((2 * HD, k.shape[0]), jnp.float32)
        for half in range(2):
            scores = product_right(q * masks[half], k)
            if bias_of is not None:
                scores = scores + bias_of(index + first, half)
            weights = softmax_rows(scores)
            grad_w = product_right(g * masks[half], v)
            inner = jnp.sum(weights * grad_w, axis=-1, keepdims=True)
            grad_s = weights * (grad_w - inner)
            if bias_grad is not None:
                bias_grad(index + first, half, grad_s)
            rounded = grad_s.astype(jnp.bfloat16)
            total_q = total_q + product(rounded, k * masks[half])
            total_k = total_k + product(qt * sides[half], rounded)
            total_v = total_v + product(gt * sides[half], weights.astype(jnp.bfloat16))
        grad_q[:, at] = total_q.astype(jnp.bfloat16)
        grad_k[at, :] = total_k.astype(jnp.bfloat16)
        grad_v[at, :] = total_v.astype(jnp.bfloat16)

    each(last - first, pair)


def turn(source, target):
    step = min(256, source.shape[0])

    def one(index):
        at = tile(index, step)
        target[:, at] = source[at, :].T

    each(source.shape[0] // step, one)


class Given:
    inputs, normed_t, q, q_t, k, u, o1_t, after, normed2_t = range(9)
    cq, cq_t, ck, cv, o2_t, after2, normed3_t, w, slope, gelu, cot = range(9, 20)
    states_t, chosen_t, spread, smalls = range(20, 24)
    w_ck, w_cv, w_sq, w_sk, w_sv, w_so, w_cq, w_co, w_fg, w_fu, w_fd = range(24, 35)
    grad_fd = 35
    count = 36


def backward_kernel(names, shared, *refs):
    given, refs = refs[: Given.count], refs[Given.count :]
    n = len(names)
    grads, refs = (given[Given.grad_fd],) + refs[: n - 1], refs[n - 1 :]
    outs, refs = refs[:n], refs[n:]
    (encoder_out, layer_out, hidden_out), refs = refs[:3], refs[3:]
    pieces = []
    for grad, out in zip(grads, outs):
        for start, width in pieces_of(grad.shape[2]) if grad.shape[1] < 256 else thirds(grad.shape[2]):
            pieces.append(Piece(grad, out, start, width))
    order = piece_order(len(pieces))
    pieces = [pieces[i] for i in order]
    count = len(pieces)
    buffers, refs = [refs[7 * i : 7 * i + 7] for i in range(count)], refs[7 * count :]
    loads = [refs[shared[i]] for i in range(count)]
    refs = refs[max(shared) + 1 :]
    (
        one_w,
        two_w,
        three_w,
        backs,
        stage,
        state_stage,
        grad_x,
        grad_n,
        value,
        other,
        cot,
        half_a,
        half_b,
        half_c,
        half_d,
        left,
        turned_q,
        turned_g,
        chosen_t,
        spread,
        smalls,
        gains,
        gain_grad,
        small_grads,
        landing,
        send_sems,
        recv_sems,
        local_sems,
        line_send,
        line_recv,
        load_sems,
        stage_sems,
        out_sem,
    ) = refs
    rank, core, along_x, along_y, depth = place()
    reduce = Reduce(pieces, buffers, loads, send_sems, recv_sems, local_sems)
    column = column_partners(rank, depth)
    greet([reduce.to_x, reduce.to_y, reduce.to_core] + column)
    ticks = iter(range(count + reduce.levels - 1))

    def tick():
        step = next(ticks)
        for level in range(reduce.levels):
            if 0 <= step - level < count:
                reduce.stage(step - level, level)

    def fetch(*pairs):
        copies = [
            pltpu.make_async_copy(source, target, load_sems.at[i])
            for i, (source, target) in enumerate(pairs)
        ]
        for copy in copies:
            copy.start()
        for copy in copies:
            copy.wait()

    def staged(buffers_of, target_of, values, tiles):
        def copy(index):
            slot = lax.rem(index, 2)
            return pltpu.make_async_copy(buffers_of.at[slot], target_of(index), stage_sems.at[slot])

        def one(index):
            @pl.when(index >= 2)
            def _():
                copy(index - 2).wait()

            buffers_of[lax.rem(index, 2)] = values(tile(index))
            copy(index).start()

        each(tiles, one)
        for index in range(max(0, tiles - 2), tiles):
            copy(jnp.int32(index)).wait()

    def weight_grad(number, right, start=0, width=None, flipped=False):
        width = grads[number].shape[2] if width is None else width

        def values(at):
            if flipped:
                result = product_right(left[...], right[at, :])
            else:
                result = product(left[:, 0 : right.shape[0]], right[:, at])
            return result.astype(jnp.bfloat16).reshape(stage.shape[1:])

        def target(index):
            column_start = pl.multiple_of(start + index * 256, 256)
            return grads[number].at[:, :, pl.ds(column_start, 256)]

        staged(stage, target, values, width // 256)

    def send_back(number, rows):
        def write(index):
            at = tile(index)
            result = product(chosen_t[...], rows[:, at]).astype(jnp.bfloat16)
            backs[number, :, :, at] = result.reshape(backs.shape[1:3] + (256,))

        each(rows.shape[1] // 256, write)
        for step, (unused, partner) in enumerate(column):
            back_copy(number, step, partner).start()

    def back_copy(number, step, partner):
        return remote(
            backs.at[number, partner],
            landing.at[number, step],
            line_send.at[number, step],
            line_recv.at[number, step],
            (rank, partner),
        )

    def receive_back(number, out):
        for step, (unused, partner) in enumerate(column):
            copy = back_copy(number, step, partner)
            copy.wait_recv()
            copy.wait_send()

        def one(index):
            at = tile(index, 32)
            total = backs[number, depth, at, :].astype(jnp.float32)
            for step in range(DOCS - 1):
                total = total + landing[number, step, at, :].astype(jnp.float32)
            out[at, :] = total.astype(jnp.bfloat16)

        each(out.shape[0] // 32, one)

    def norm_grad(values, gain, carry, out):
        rms_back(values, grad_n, gains[gain : gain + 1, :], carry, out, gain_grad)
        for slot in range(8):
            small_grads[slot, gain : gain + 1, :] = gain_grad[:, 128 * slot : 128 * slot + 128]

    def round_rows(source, target):
        def one(index):
            at = tile(index, 32)
            target[at, :] = source[at, :].astype(jnp.bfloat16)

        each(source.shape[0] // 32, one)

    def through(right_rows, weights, write):
        def one(index):
            at = tile(index)
            write(at, product_right(right_rows[...], weights[at, :]))

        each(weights.shape[0] // 256, one)

    def head_grads(weights):
        through(half_a, weights, store_as(half_b))

        def one(index):
            at = tile(index)
            turned_g[at, :] = product_right(weights[at, :], half_a[...]).astype(jnp.bfloat16)

        each(weights.shape[0] // 256, one)

    tick()
    fetch(
        (given[Given.cot], cot),
        (given[Given.normed3_t], left),
        (given[Given.chosen_t], chosen_t),
        (given[Given.spread], spread),
        (given[Given.smalls], smalls),
    )
    for slot in range(8):
        gains[0:3, 128 * slot : 128 * slot + 128] = smalls[16 * slot : 16 * slot + 3, :]
    small_grads[...] = jnp.zeros_like(small_grads)
    tick()
    for start, width in pieces_of(given[Given.w].shape[1]):
        at = pl.ds(start, width)
        down, gate, up = one_w.at[0:width], two_w.at[:, 0:width], three_w.at[:, 0:width]
        part = half_a.at[:, 0:width]
        slope, gelu = value.at[:, 0:width], other.at[:, 0:width]
        gate_grad, up_grad = half_b.at[:, 0:width], half_c.at[:, 0:width]
        fetch(
            (given[Given.w_fd].at[at], down),
            (given[Given.w_fg].at[:, at], gate),
            (given[Given.w_fu].at[:, at], up),
            (given[Given.w].at[:, at], part),
            (given[Given.slope].at[:, at], slope),
            (given[Given.gelu].at[:, at], gelu),
        )

        def split(at, grad_w):
            gate_grad[:, at] = (grad_w * slope[:, at]).astype(jnp.bfloat16)
            up_grad[:, at] = (grad_w * gelu[:, at]).astype(jnp.bfloat16)

        through(cot, down, split)
        weight_grad(1, gate_grad, start, width)
        weight_grad(2, up_grad, start, width)

        def add(index):
            at = tile(index)
            forward = product(part[...], down[:, at])
            back = product_right(gate_grad[...], gate[at, :]) + product_right(up_grad[...], up[at, :])
            if start:
                forward, back = forward + grad_x[:, at], back + grad_n[:, at]
            grad_x[:, at] = forward
            grad_n[:, at] = back

        each(grad_x.shape[1] // 256, add)
        tick()

    fetch(
        (given[Given.after2], value),
        (given[Given.o2_t], left),
        (given[Given.w_co], one_w),
        (given[Given.cq], half_c),
        (given[Given.cq_t], turned_q),
        (given[Given.ck], two_w.at[0:512]),
        (given[Given.cv], two_w.at[512:1024]),
    )

    def layer(index):
        at = tile(index, 32)
        half_a[at, :] = (value[at, :] + grad_x[at, :]).astype(jnp.bfloat16)

    each(value.shape[0] // 32, layer)
    send_back(0, half_a)
    norm_grad(value, 2, cot, grad_x)
    round_rows(grad_x, half_a)
    weight_grad(3, half_a)
    head_grads(one_w)
    tick()
    keys_grad, values_grad = three_w.at[:, 0:512], three_w.at[:, 512:1024]

    def cross(first, last):
        attend_back_heads(
            first,
            last,
            half_c,
            turned_q,
            two_w.at[0:512],
            two_w.at[512:1024],
            half_b,
            turned_g,
            half_d,
            keys_grad,
            values_grad,
            None,
            None,
        )

    cross(0, 4)
    tick()
    cross(4, 8)
    tick()
    states = one_w.at[:, 0:512]
    fetch((given[Given.states_t], states))

    def state_grad(number, right):
        def values(at):
            result = product_right(states[...], right[at, :])
            return result.astype(jnp.bfloat16).reshape(stage.shape[1:])

        def target(index):
            return grads[number].at[:, :, tile(index)]

        staged(stage, target, values, 4)

    state_grad(4, keys_grad)
    state_grad(5, values_grad)
    turn(keys_grad, two_w.at[0:512])
    turn(values_grad, two_w.at[512:1024])
    fetch((given[Given.w_ck], one_w), (given[Given.w_cv], three_w), (given[Given.normed2_t], left))
    tick()
    staged(
        state_stage,
        lambda index: encoder_out.at[:, tile(index)],
        lambda at: product_right(two_w[0:512], one_w[at, :])
        + product_right(two_w[512:1024], three_w[at, :]),
        4,
    )
    fetch(
        (given[Given.w_cq], one_w),
        (given[Given.w_so], three_w),
        (given[Given.after], value),
        (given[Given.q], half_c),
        (given[Given.q_t], turned_q),
        (given[Given.k], two_w.at[0:256]),
        (given[Given.u], two_w.at[256:512]),
    )
    tick()
    weight_grad(6, half_d)
    through(half_d, one_w, store_as(grad_n))
    norm_grad(value, 1, grad_x, grad_x)
    round_rows(grad_x, half_a)
    fetch((given[Given.o1_t], left))
    weight_grad(7, half_a)
    head_grads(three_w)
    tick()

    def table_grad(index, half, grad_s):
        line = jnp.broadcast_to(diagonal_sums(grad_s), (8, grad_s.shape[1]))
        table = lax.dot_general(
            line,
            spread[half].astype(jnp.float32),
            (((1,), (1,)), ((), ())),
            precision=highest,
            preferred_element_type=jnp.float32,
        )
        small_grads[index, 3:4, :] = small_grads[index, 3:4, :] + table[0:1]

    keys_grad, values_grad = three_w.at[:, 0:256], three_w.at[:, 256:512]

    def own(first, last):
        attend_back_heads(
            first,
            last,
            half_c,
            turned_q,
            two_w.at[0:256],
            two_w.at[256:512],
            half_b,
            turned_g,
            half_d,
            keys_grad,
            values_grad,
            functools.partial(causal_bias, smalls, spread),
            table_grad,
        )

    own(0, 4)
    tick()
    own(4, 8)
    turn(keys_grad, half_a)
    turn(values_grad, half_b)
    tick()
    fetch(
        (given[Given.normed_t], left),
        (given[Given.inputs], value),
        (given[Given.w_sq], one_w),
        (given[Given.w_sk], two_w),
        (given[Given.w_sv], three_w),
    )
    weight_grad(8, half_d)
    weight_grad(9, half_a)
    weight_grad(10, half_b)
    tick()

    def sum_three(index):
        at = tile(index)
        grad_n[:, at] = (
            product_right(half_d[...], one_w[at, :])
            + product_right(half_a[...], two_w[at, :])
            + product_right(half_b[...], three_w[at, :])
        )

    each(grad_n.shape[1] // 256, sum_three)
    norm_grad(value, 0, grad_x, half_c)
    small_copy = pltpu.make_async_copy(small_grads, grads[11], out_sem)
    small_copy.start()
    small_copy.wait()
    send_back(1, half_c)
    for unused in range(count + reduce.levels):
        try:
            tick()
        except StopIteration:
            break
    receive_back(0, layer_out)
    receive_back(1, hidden_out)
    for number in range(count):
        reduce.write(number).wait()


def thirds(width):
    return [(0, 384), (384, 384), (768, width - 768)]


def piece_order(count):
    return [0, 1, 2, 3, 6, 4, 7, 5, 8] + list(range(9, count))


def backward_call(operands, rows):
    count = Given.count
    anywhere = pl.BlockSpec(memory_space=pl.ANY)
    vmem = pl.BlockSpec(memory_space=pltpu.VMEM)
    grad_fd = operands[Given.grad_fd]
    width, wide = operands[Given.w_fg].shape
    square = jax.ShapeDtypeStruct((8, width // 8, width), jnp.bfloat16)
    broad = jax.ShapeDtypeStruct((8, width // 8, wide), jnp.bfloat16)
    small = jax.ShapeDtypeStruct((8, 16, 128), jnp.float32)
    full = [jax.ShapeDtypeStruct(grad_fd.shape, grad_fd.dtype), broad, broad] + [square] * 8 + [small]
    outs = [jax.ShapeDtypeStruct(g.shape[1:], g.dtype) for g in full]
    most = operands[Given.inputs].shape[0]
    states = operands[Given.ck].shape[0]
    total = operands[Given.chosen_t].shape[0]
    tail = [
        jax.ShapeDtypeStruct((states, width), jnp.float32),
        jax.ShapeDtypeStruct((rows, width), jnp.bfloat16),
        jax.ShapeDtypeStruct((rows, width), jnp.bfloat16),
    ]
    shapes = []
    for grad in full:
        for start, part in pieces_of(grad.shape[2]) if grad.shape[1] < 256 else thirds(grad.shape[2]):
            shapes.append(((grad.shape[1], part), grad.dtype))
    shapes = [shapes[i] for i in piece_order(len(shapes))]
    scratch, load_shapes, shared, turns = [], [], [], []
    for shape, dtype in shapes:
        scratch += buffer_shapes(shape[0], shape[1], dtype)
        key = ((2,) + shape, dtype)
        held = [i for i, s in enumerate(load_shapes) if s == key]
        if len(held) < 2:
            shared.append(len(load_shapes))
            load_shapes.append(key)
        else:
            last = [i for i in shared if i in held][-1]
            shared.append(held[0] if last == held[1] else held[1])
    scratch += [pltpu.VMEM(*s) for s in load_shapes]
    pieces = len(shapes)
    bf16, f32 = jnp.bfloat16, jnp.float32
    scratch += [pltpu.VMEM((width, width), bf16)] * 3
    scratch += [
        pltpu.VMEM((2, DOCS, total // DOCS, width), bf16),
        pltpu.VMEM((2, 8, width // 8, 256), bf16),
        pltpu.VMEM((2, states, 256), f32),
    ]
    scratch += [pltpu.VMEM((most, width), f32)] * 4
    scratch += [pltpu.VMEM((most, width), bf16)] * 5
    scratch += [pltpu.VMEM((width, most), bf16)] * 3
    scratch += [
        pltpu.VMEM((total, most), bf16),
        pltpu.VMEM((2, 128, most), bf16),
        pltpu.VMEM((128, 128), f32),
        pltpu.VMEM((8, width), f32),
        pltpu.VMEM((1, width), f32),
        pltpu.VMEM((8, 16, 128), f32),
        pltpu.VMEM((2, DOCS - 1, rows, width), bf16),
        pltpu.SemaphoreType.DMA((pieces, 12)),
        pltpu.SemaphoreType.DMA((pieces, 12)),
        pltpu.SemaphoreType.DMA((pieces, 5)),
        pltpu.SemaphoreType.DMA((2, DOCS - 1)),
        pltpu.SemaphoreType.DMA((2, DOCS - 1)),
        pltpu.SemaphoreType.DMA((8,)),
        pltpu.SemaphoreType.DMA((2,)),
        pltpu.SemaphoreType.DMA,
    ]
    return pl.pallas_call(
        functools.partial(backward_kernel, range(12), shared),
        out_shape=full[1:] + outs + tail,
        in_specs=[anywhere] * count,
        out_specs=[anywhere] * (len(full) - 1 + len(outs) + 1) + [vmem] * 2,
        scratch_shapes=scratch,
        compiler_params=pltpu.CompilerParams(
            collective_id=2, has_side_effects=True, vmem_limit_bytes=67043328
        ),
        name="backward",
    )(*operands)


def pack_small(norms, table):
    rows = [n.astype(jnp.float32) for n in norms]
    rows.append(jnp.pad(table.astype(jnp.float32), (0, 128 - table.shape[0])))
    return jnp.pad(jnp.stack(rows), ((0, 12), (0, 0)))


def by_document(
    hidden_in,
    encoder_states,
    segment_ids,
    encoder_docs,
    self_query,
    self_key,
    self_value,
    self_out,
    cross_query,
    cross_key,
    cross_value,
    cross_out,
    feed_gate,
    feed_up,
    feed_down,
    norm_self,
    norm_cross,
    norm_feed,
    bias_table,
    out_grad,
):
    width = hidden_in.shape[2]
    total = segment_ids.shape[1]
    most = total // 2
    encoded = encoder_states[0]
    small = pack_small((norm_self, norm_cross, norm_feed), bias_table)
    document = lax.dynamic_slice_in_dim(
        encoder_docs[0], lax.axis_index("ctx") * encoded.shape[0], 1, 0
    )
    segments = segment_ids[0]
    start = jnp.sum((segments < document).astype(jnp.int32))
    length = jnp.sum((segments == document).astype(jnp.int32))
    row = lax.broadcasted_iota(jnp.int32, (most, total), 0)
    column = lax.broadcasted_iota(jnp.int32, (most, total), 1)
    chosen = ((row + start == column) & (row < length)).astype(jnp.bfloat16)

    slot = jnp.arange(2 * HD, dtype=jnp.int32)
    position = jnp.arange(most, dtype=jnp.int32)
    bucket = bucket_of(lax.rem(most - position, most))
    spread = jnp.stack(
        [(slot[:, None] == bucket[None] + BUCKETS * half) for half in range(2)]
    ).astype(jnp.bfloat16)
    results = forward_call(
        (
            small,
            cross_key,
            cross_value,
            self_query,
            self_key,
            self_value,
            self_out,
            cross_query,
            cross_out,
            feed_gate,
            feed_up,
            feed_down,
        ),
        hidden_in[0],
        out_grad[0],
        chosen,
        encoded,
        spread,
    )
    kept = results[12:]
    grad_fd = results[-1].reshape(8, -1, width)
    forward_side = [
        kept[i]
        for i in (
            Kept.inputs,
            Kept.normed_t,
            Kept.q,
            Kept.q_t,
            Kept.k,
            Kept.u,
            Kept.o1_t,
            Kept.after,
            Kept.normed2_t,
            Kept.cq,
            Kept.cq_t,
            Kept.ck,
            Kept.cv,
            Kept.o2_t,
            Kept.after2,
            Kept.normed3_t,
            Kept.w,
            Kept.slope,
            Kept.gelu,
            Kept.cot,
            Kept.states_t,
        )
    ]
    results = backward_call(
        forward_side + [chosen.T, spread] + list(results[:12]) + [grad_fd], hidden_in.shape[1]
    )[11:]
    fd, fg, fu, co, ck, cv, cq, so, sq, sk, sv = (r.astype(jnp.float32) for r in results[:11])
    smalls, encoder_grad, layer_out, hidden_grad = results[11:]
    return (
        layer_out[None],
        hidden_grad.astype(jnp.float32)[None],
        encoder_grad[None],
        sq,
        sk,
        sv,
        so,
        cq,
        ck,
        cv,
        co,
        fg,
        fu,
        fd,
        smalls[0],
        smalls[1],
        smalls[2],
        smalls[3, : bias_table.shape[0]],
    )


def layer(sizes, *args):
    encoder_states, encoder_docs = args[1], args[3]
    whole_document = encoder_states.shape[1] * DOCS == encoder_docs.shape[1]
    if whole_document and sizes["fsdp"] == 8 and sizes["ctx"] == DOCS:
        return by_document(*args)
    return on_device(*args)


def solution(mesh):
    in_specs = (
        P("fsdp", "ctx", None),
        P("fsdp", "ctx", None),
        P("fsdp", None),
        P("fsdp", None),
        P("fsdp", None),
        P("fsdp", None),
        P("fsdp", None),
        P("fsdp", None),
        P("fsdp", None),
        P("fsdp", None),
        P("fsdp", None),
        P("fsdp", None),
        P("fsdp", None),
        P("fsdp", None),
        P("fsdp", None),
        P("fsdp"),
        P("fsdp"),
        P("fsdp"),
        P("fsdp"),
        P("fsdp", "ctx", None),
    )
    out_specs = (
        P("fsdp", "ctx", None),
        P("fsdp", "ctx", None),
        P("fsdp", "ctx", None),
        P("fsdp", None),
        P("fsdp", None),
        P("fsdp", None),
        P("fsdp", None),
        P("fsdp", None),
        P("fsdp", None),
        P("fsdp", None),
        P("fsdp", None),
        P("fsdp", None),
        P("fsdp", None),
        P("fsdp", None),
        P("fsdp"),
        P("fsdp"),
        P("fsdp"),
        P("fsdp"),
    )
    return jax.shard_map(
        functools.partial(layer, dict(mesh.shape)), mesh=mesh, in_specs=in_specs, out_specs=out_specs, check_vma=False
    )
```

```python
import functools
import math

import jax
import jax.numpy as jnp
from jax import lax
from jax.experimental import pallas as pl
from jax.experimental.pallas import tpu as pltpu
from jax.sharding import PartitionSpec as P

H = 16
HD = 64
BUCKETS = 32
DOCS = 4
MESH = pl.DeviceIdType.MESH


bucket_edges = (19, 21, 24, 27, 31, 35, 40, 46, 52, 59, 67, 77, 87, 99, 113)
epsilon = 1e-06
masked_value = -1e30
highest = lax.Precision.HIGHEST


def normalize(values, gain_vector):
    inverse_root = lax.rsqrt(jnp.mean(values * values, axis=-1, keepdims=True) + epsilon)
    return values * inverse_root * gain_vector


def norm_back(values, gain_vector, grad_normed):
    unused, pullback = jax.vjp(normalize, values, gain_vector)
    return pullback(grad_normed)


def product(left_side, right_side):
    return jnp.dot(left_side, right_side, preferred_element_type=jnp.float32)


def product_left(left_side, right_side):
    return lax.dot_general(
        left_side, right_side, (((0,), (0,)), ((), ())), preferred_element_type=jnp.float32
    )


def product_right(left_side, right_side):
    return lax.dot_general(
        left_side, right_side, (((1,), (1,)), ((), ())), preferred_element_type=jnp.float32
    )


def bucket_of(distance):
    bucket_index = jnp.minimum(distance, 16)
    for threshold in bucket_edges:
        bucket_index = bucket_index + (distance >= threshold).astype(jnp.int32)
    return bucket_index


def bucket_onehot(distance):
    return (bucket_of(distance)[:, :, None] == jnp.arange(BUCKETS, dtype=jnp.int32)).astype(jnp.bfloat16)


def split_blocks(rows_all):
    total_rows = rows_all.shape[0]
    block_rows = math.gcd(total_rows, 512)
    return (block_rows, rows_all.reshape(total_rows // block_rows, block_rows, H, HD))


def block_logits(query_heads, key_part, allowed, distance, table_rows):
    scores = jnp.einsum("qhd,khd->hqk", query_heads, key_part, preferred_element_type=jnp.float32)
    onehot = None
    if table_rows is not None:
        onehot = bucket_onehot(distance)
        scores = scores + jnp.einsum(
            "qkb,hb->hqk", onehot, table_rows, preferred_element_type=jnp.float32
        )
    return (jnp.where(allowed[None], scores, masked_value), onehot)


def attention_forward(query_heads, key_rows, value_rows, mask_of, table_rows):
    block_rows, key_blocks = split_blocks(key_rows)
    unused, value_blocks = split_blocks(value_rows)
    numbers = jnp.arange(key_blocks.shape[0], dtype=jnp.int32)
    query_count = query_heads.shape[0]

    def total_step(carried, element):
        number, key_part = element
        allowed, distance = mask_of(number, block_rows)

        def total_live_branch(state):
            running, summed = state
            scores, unused_hot = block_logits(query_heads, key_part, allowed, distance, table_rows)
            newest = jnp.maximum(running, jnp.max(scores, axis=-1))
            exp_terms = jnp.where(allowed[None], jnp.exp(scores - newest[..., None]), 0.0)
            return (newest, summed * jnp.exp(running - newest) + jnp.sum(exp_terms, axis=-1))

        return (lax.cond(jnp.any(allowed), total_live_branch, lambda state: state, carried), None)

    start_state = (
        jnp.full((H, query_count), masked_value, jnp.float32),
        jnp.zeros((H, query_count), jnp.float32),
    )
    (running, summed), unused_out = lax.scan(total_step, start_state, (numbers, key_blocks))
    logsum = running + jnp.log(summed)

    def output_step(carried, element):
        number, key_part, value_part = element
        allowed, distance = mask_of(number, block_rows)

        def output_live_branch(state):
            scores, unused_hot = block_logits(query_heads, key_part, allowed, distance, table_rows)
            weights = jnp.where(allowed[None], jnp.exp(scores - logsum[..., None]), 0.0).astype(
                jnp.bfloat16
            )
            return state + jnp.einsum(
                "hqk,khd->qhd", weights, value_part, preferred_element_type=jnp.float32
            )

        return (lax.cond(jnp.any(allowed), output_live_branch, lambda state: state, carried), None)

    output, unused_out = lax.scan(
        output_step,
        jnp.zeros((query_count, H, HD), jnp.float32),
        (numbers, key_blocks, value_blocks),
    )
    return (output, logsum)


def attention_delta(query_heads, key_rows, value_rows, grad_heads, logsum, mask_of, table_rows):
    block_rows, key_blocks = split_blocks(key_rows)
    unused, value_blocks = split_blocks(value_rows)
    numbers = jnp.arange(key_blocks.shape[0], dtype=jnp.int32)
    query_count = query_heads.shape[0]

    def delta_step(carried, element):
        number, key_part, value_part = element
        allowed, distance = mask_of(number, block_rows)

        def delta_live_branch(state):
            scores, unused_hot = block_logits(query_heads, key_part, allowed, distance, table_rows)
            weights = jnp.where(allowed[None], jnp.exp(scores - logsum[..., None]), 0.0)
            grad_weights = jnp.einsum(
                "qhd,khd->hqk", grad_heads, value_part, preferred_element_type=jnp.float32
            )
            return state + jnp.sum(weights * grad_weights, axis=-1)

        return (lax.cond(jnp.any(allowed), delta_live_branch, lambda state: state, carried), None)

    row_delta, unused_out = lax.scan(
        delta_step, jnp.zeros((H, query_count), jnp.float32), (numbers, key_blocks, value_blocks)
    )
    return row_delta


def attention_backward(
    query_heads, key_rows, value_rows, grad_heads, logsum, row_delta, mask_of, table_rows
):
    block_rows, key_blocks = split_blocks(key_rows)
    unused, value_blocks = split_blocks(value_rows)
    numbers = jnp.arange(key_blocks.shape[0], dtype=jnp.int32)
    query_count = query_heads.shape[0]
    part_shape = (block_rows, H, HD)

    def grad_step(carried, element):
        number, key_part, value_part = element
        allowed, distance = mask_of(number, block_rows)

        def grad_live_branch(state):
            grad_query, grad_table = state
            scores, onehot = block_logits(query_heads, key_part, allowed, distance, table_rows)
            weights = jnp.where(allowed[None], jnp.exp(scores - logsum[..., None]), 0.0)
            grad_weights = jnp.einsum(
                "qhd,khd->hqk", grad_heads, value_part, preferred_element_type=jnp.float32
            )
            grad_scores = weights * (grad_weights - row_delta[..., None])
            rounded = grad_scores.astype(jnp.bfloat16)
            grad_query = grad_query + jnp.einsum(
                "hqk,khd->qhd", rounded, key_part, preferred_element_type=jnp.float32
            )
            if table_rows is not None:
                grad_table = grad_table + jnp.einsum(
                    "hqk,qkb->hb", grad_scores, onehot.astype(jnp.float32), precision=highest
                )
            grad_key_part = jnp.einsum(
                "hqk,qhd->khd", rounded, query_heads, preferred_element_type=jnp.float32
            )
            grad_value_part = jnp.einsum(
                "hqk,qhd->khd",
                weights.astype(jnp.bfloat16),
                grad_heads,
                preferred_element_type=jnp.float32,
            )
            return ((grad_query, grad_table), (grad_key_part, grad_value_part))

        def dead_branch(state):
            return (state, (jnp.zeros(part_shape, jnp.float32), jnp.zeros(part_shape, jnp.float32)))

        return lax.cond(jnp.any(allowed), grad_live_branch, dead_branch, carried)

    table_shape = (H, BUCKETS) if table_rows is not None else (1, 1)
    start_state = (
        jnp.zeros((query_count, H, HD), jnp.float32),
        jnp.zeros(table_shape, jnp.float32),
    )
    (grad_query, grad_table), key_parts = lax.scan(
        grad_step, start_state, (numbers, key_blocks, value_blocks)
    )
    total_rows = key_rows.shape[0]
    return (
        grad_query,
        grad_table,
        key_parts[0].reshape(total_rows, H * HD),
        key_parts[1].reshape(total_rows, H * HD),
    )


def on_device(
    hidden_in,
    encoder_states,
    segment_ids,
    encoder_docs,
    self_query,
    self_key,
    self_value,
    self_out,
    cross_query,
    cross_key,
    cross_value,
    cross_out,
    feed_gate,
    feed_up,
    feed_down,
    norm_self,
    norm_cross,
    norm_feed,
    bias_table,
    out_grad,
):
    gathered = (
        lax.all_gather(self_query, "fsdp", axis=0, tiled=True),
        lax.all_gather(self_key, "fsdp", axis=0, tiled=True),
        lax.all_gather(self_value, "fsdp", axis=0, tiled=True),
        lax.all_gather(self_out, "fsdp", axis=0, tiled=True),
        lax.all_gather(cross_query, "fsdp", axis=0, tiled=True),
        lax.all_gather(cross_key, "fsdp", axis=0, tiled=True),
        lax.all_gather(cross_value, "fsdp", axis=0, tiled=True),
        lax.all_gather(cross_out, "fsdp", axis=0, tiled=True),
        lax.all_gather(feed_gate, "fsdp", axis=0, tiled=True),
        lax.all_gather(feed_up, "fsdp", axis=0, tiled=True),
        lax.all_gather(feed_down, "fsdp", axis=0, tiled=True),
        lax.all_gather(norm_self, "fsdp", axis=0, tiled=True),
        lax.all_gather(norm_cross, "fsdp", axis=0, tiled=True),
        lax.all_gather(norm_feed, "fsdp", axis=0, tiled=True),
        lax.all_gather(bias_table, "fsdp", axis=0, tiled=True),
    )
    tokens = hidden_in[0]
    encoded = encoder_states[0]
    segments = segment_ids[0]
    documents = encoder_docs[0]
    tok_rows = tokens.shape[0]
    first_row = lax.axis_index("ctx") * tok_rows
    query_pos = first_row + jnp.arange(tok_rows, dtype=jnp.int32)
    query_seg = lax.dynamic_slice_in_dim(segments, first_row, tok_rows, 0)

    def self_mask(number, block_rows):
        key_pos = number * block_rows + jnp.arange(block_rows, dtype=jnp.int32)
        key_seg = lax.dynamic_slice_in_dim(segments, number * block_rows, block_rows, 0)
        distance = query_pos[:, None] - key_pos[None, :]
        allowed = (distance >= 0) & (query_seg[:, None] == key_seg[None, :])
        return (allowed, jnp.maximum(distance, 0))

    def cross_mask(number, block_rows):
        key_doc = lax.dynamic_slice_in_dim(documents, number * block_rows, block_rows, 0)
        return (query_seg[:, None] == key_doc[None, :], None)

    inputs = tokens.astype(jnp.float32)
    self_normed = normalize(inputs, gathered[11].astype(jnp.float32)).astype(jnp.bfloat16)
    queries = product(self_normed, gathered[0]).astype(jnp.bfloat16)
    key_local = product(self_normed, gathered[1]).astype(jnp.bfloat16)
    value_local = product(self_normed, gathered[2]).astype(jnp.bfloat16)
    key_rows, value_rows = (
        lax.all_gather(key_local, "ctx", axis=0, tiled=True),
        lax.all_gather(value_local, "ctx", axis=0, tiled=True),
    )
    table_rows = gathered[14].reshape(H, BUCKETS)
    query_heads = queries.reshape(tok_rows, H, HD)
    key_heads = key_rows.reshape(-1, H, HD)
    value_heads = value_rows.reshape(-1, H, HD)
    self_heads, self_logsum = attention_forward(
        query_heads, key_heads, value_heads, self_mask, table_rows
    )
    self_attended = self_heads.reshape(tok_rows, H * HD).astype(jnp.bfloat16)
    after_self = inputs + product(self_attended, gathered[3])
    cross_normed = normalize(after_self, gathered[12].astype(jnp.float32)).astype(jnp.bfloat16)
    cross_queries = product(cross_normed, gathered[4]).astype(jnp.bfloat16)
    cross_key_local = product(encoded, gathered[5]).astype(jnp.bfloat16)
    cross_value_local = product(encoded, gathered[6]).astype(jnp.bfloat16)
    cross_keys, cross_values = (
        lax.all_gather(cross_key_local, "ctx", axis=0, tiled=True),
        lax.all_gather(cross_value_local, "ctx", axis=0, tiled=True),
    )
    cross_query_heads = cross_queries.reshape(tok_rows, H, HD)
    cross_key_heads = cross_keys.reshape(-1, H, HD)
    cross_value_heads = cross_values.reshape(-1, H, HD)
    cross_heads, cross_logsum = attention_forward(
        cross_query_heads, cross_key_heads, cross_value_heads, cross_mask, None
    )
    cross_attended = cross_heads.reshape(tok_rows, H * HD).astype(jnp.bfloat16)
    after_cross = after_self + product(cross_attended, gathered[7])
    feed_normed = normalize(after_cross, gathered[13].astype(jnp.float32)).astype(jnp.bfloat16)
    gate_value = product(feed_normed, gathered[8])
    up_value = product(feed_normed, gathered[9])
    hidden_units = (jax.nn.gelu(gate_value, approximate=True) * up_value).astype(jnp.bfloat16)
    layer_out = (after_cross + product(hidden_units, gathered[10])).astype(jnp.bfloat16)
    grad_after = out_grad[0].astype(jnp.float32)
    grad_round = grad_after.astype(jnp.bfloat16)
    grad_feed_down = product_left(hidden_units, grad_round)
    grad_hidden = product_right(grad_round, gathered[10])
    unused, pullback = jax.vjp(
        lambda gate_in, up_in: jax.nn.gelu(gate_in, approximate=True) * up_in, gate_value, up_value
    )
    grad_gate, grad_up = pullback(grad_hidden)
    gate_round = grad_gate.astype(jnp.bfloat16)
    up_round = grad_up.astype(jnp.bfloat16)
    grad_feed_gate = product_left(feed_normed, gate_round)
    grad_feed_up = product_left(feed_normed, up_round)
    grad_feed_normed = product_right(gate_round, gathered[8]) + product_right(up_round, gathered[9])
    grad_cross_side, grad_norm_feed = norm_back(
        after_cross, gathered[13].astype(jnp.float32), grad_feed_normed
    )
    grad_after_cross = grad_after + grad_cross_side
    cross_round = grad_after_cross.astype(jnp.bfloat16)
    grad_cross_out = product_left(cross_attended, cross_round)
    grad_cross_heads = (
        product_right(cross_round, gathered[7]).astype(jnp.bfloat16).reshape(tok_rows, H, HD)
    )
    cross_delta = attention_delta(
        cross_query_heads,
        cross_key_heads,
        cross_value_heads,
        grad_cross_heads,
        cross_logsum,
        cross_mask,
        None,
    )
    grad_cross_q, unused_table, grad_cross_k, grad_cross_v = attention_backward(
        cross_query_heads,
        cross_key_heads,
        cross_value_heads,
        grad_cross_heads,
        cross_logsum,
        cross_delta,
        cross_mask,
        None,
    )
    cross_key_grad, cross_value_grad = (
        lax.psum_scatter(
            grad_cross_k.astype(jnp.bfloat16), "ctx", scatter_dimension=0, tiled=True
        ).astype(jnp.float32),
        lax.psum_scatter(
            grad_cross_v.astype(jnp.bfloat16), "ctx", scatter_dimension=0, tiled=True
        ).astype(jnp.float32),
    )
    cross_key_round = cross_key_grad.astype(jnp.bfloat16)
    cross_value_round = cross_value_grad.astype(jnp.bfloat16)
    grad_cross_key = product_left(encoded, cross_key_round)
    grad_cross_value = product_left(encoded, cross_value_round)
    encoder_grad = product_right(cross_key_round, gathered[5]) + product_right(
        cross_value_round, gathered[6]
    )
    cross_query_round = grad_cross_q.reshape(tok_rows, H * HD).astype(jnp.bfloat16)
    grad_cross_query = product_left(cross_normed, cross_query_round)
    grad_cross_normed = product_right(cross_query_round, gathered[4])
    grad_self_side, grad_norm_cross = norm_back(
        after_self, gathered[12].astype(jnp.float32), grad_cross_normed
    )
    grad_after_self = grad_after_cross + grad_self_side
    self_round = grad_after_self.astype(jnp.bfloat16)
    grad_self_out = product_left(self_attended, self_round)
    grad_self_flat = product_right(self_round, gathered[3]).astype(jnp.bfloat16)
    grad_self_heads = grad_self_flat.reshape(tok_rows, H, HD)
    back_table = gathered[14].reshape(H, BUCKETS)
    self_delta = attention_delta(
        query_heads, key_heads, value_heads, grad_self_heads, self_logsum, self_mask, back_table
    )
    grad_self_q, grad_table, grad_self_k, grad_self_v = attention_backward(
        query_heads,
        key_heads,
        value_heads,
        grad_self_heads,
        self_logsum,
        self_delta,
        self_mask,
        back_table,
    )
    self_key_grad, self_value_grad = (
        lax.psum_scatter(
            grad_self_k.astype(jnp.bfloat16), "ctx", scatter_dimension=0, tiled=True
        ).astype(jnp.float32),
        lax.psum_scatter(
            grad_self_v.astype(jnp.bfloat16), "ctx", scatter_dimension=0, tiled=True
        ).astype(jnp.float32),
    )
    self_key_round = self_key_grad.astype(jnp.bfloat16)
    self_value_round = self_value_grad.astype(jnp.bfloat16)
    self_query_round = grad_self_q.reshape(tok_rows, H * HD).astype(jnp.bfloat16)
    grad_self_query = product_left(self_normed, self_query_round)
    grad_self_key = product_left(self_normed, self_key_round)
    grad_self_value = product_left(self_normed, self_value_round)
    grad_self_normed = (
        product_right(self_query_round, gathered[0])
        + product_right(self_key_round, gathered[1])
        + product_right(self_value_round, gathered[2])
    )
    grad_input_side, grad_norm_self = norm_back(
        inputs, gathered[11].astype(jnp.float32), grad_self_normed
    )
    hidden_grad = grad_after_self + grad_input_side
    grad_bias_table = grad_table.reshape(H * BUCKETS)
    pieces = (
        lax.psum_scatter(
            grad_self_query.astype(jnp.bfloat16), "fsdp", scatter_dimension=0, tiled=True
        ).astype(jnp.float32),
        lax.psum_scatter(
            grad_self_key.astype(jnp.bfloat16), "fsdp", scatter_dimension=0, tiled=True
        ).astype(jnp.float32),
        lax.psum_scatter(
            grad_self_value.astype(jnp.bfloat16), "fsdp", scatter_dimension=0, tiled=True
        ).astype(jnp.float32),
        lax.psum_scatter(
            grad_self_out.astype(jnp.bfloat16), "fsdp", scatter_dimension=0, tiled=True
        ).astype(jnp.float32),
        lax.psum_scatter(
            grad_cross_query.astype(jnp.bfloat16), "fsdp", scatter_dimension=0, tiled=True
        ).astype(jnp.float32),
        lax.psum_scatter(
            grad_cross_key.astype(jnp.bfloat16), "fsdp", scatter_dimension=0, tiled=True
        ).astype(jnp.float32),
        lax.psum_scatter(
            grad_cross_value.astype(jnp.bfloat16), "fsdp", scatter_dimension=0, tiled=True
        ).astype(jnp.float32),
        lax.psum_scatter(
            grad_cross_out.astype(jnp.bfloat16), "fsdp", scatter_dimension=0, tiled=True
        ).astype(jnp.float32),
        lax.psum_scatter(
            grad_feed_gate.astype(jnp.bfloat16), "fsdp", scatter_dimension=0, tiled=True
        ).astype(jnp.float32),
        lax.psum_scatter(
            grad_feed_up.astype(jnp.bfloat16), "fsdp", scatter_dimension=0, tiled=True
        ).astype(jnp.float32),
        lax.psum_scatter(
            grad_feed_down.astype(jnp.bfloat16), "fsdp", scatter_dimension=0, tiled=True
        ).astype(jnp.float32),
        lax.psum_scatter(
            grad_norm_self.astype(jnp.bfloat16), "fsdp", scatter_dimension=0, tiled=True
        ).astype(jnp.float32),
        lax.psum_scatter(
            grad_norm_cross.astype(jnp.bfloat16), "fsdp", scatter_dimension=0, tiled=True
        ).astype(jnp.float32),
        lax.psum_scatter(
            grad_norm_feed.astype(jnp.bfloat16), "fsdp", scatter_dimension=0, tiled=True
        ).astype(jnp.float32),
        lax.psum_scatter(
            grad_bias_table.astype(jnp.bfloat16), "fsdp", scatter_dimension=0, tiled=True
        ).astype(jnp.float32),
    )
    owned = (
        lax.psum(pieces[0].astype(jnp.bfloat16), "ctx").astype(jnp.float32),
        lax.psum(pieces[1].astype(jnp.bfloat16), "ctx").astype(jnp.float32),
        lax.psum(pieces[2].astype(jnp.bfloat16), "ctx").astype(jnp.float32),
        lax.psum(pieces[3].astype(jnp.bfloat16), "ctx").astype(jnp.float32),
        lax.psum(pieces[4].astype(jnp.bfloat16), "ctx").astype(jnp.float32),
        lax.psum(pieces[5].astype(jnp.bfloat16), "ctx").astype(jnp.float32),
        lax.psum(pieces[6].astype(jnp.bfloat16), "ctx").astype(jnp.float32),
        lax.psum(pieces[7].astype(jnp.bfloat16), "ctx").astype(jnp.float32),
        lax.psum(pieces[8].astype(jnp.bfloat16), "ctx").astype(jnp.float32),
        lax.psum(pieces[9].astype(jnp.bfloat16), "ctx").astype(jnp.float32),
        lax.psum(pieces[10].astype(jnp.bfloat16), "ctx").astype(jnp.float32),
        lax.psum(pieces[11].astype(jnp.bfloat16), "ctx").astype(jnp.float32),
        lax.psum(pieces[12].astype(jnp.bfloat16), "ctx").astype(jnp.float32),
        lax.psum(pieces[13].astype(jnp.bfloat16), "ctx").astype(jnp.float32),
        lax.psum(pieces[14].astype(jnp.bfloat16), "ctx").astype(jnp.float32),
    )
    return (
        layer_out[None],
        hidden_grad[None],
        encoder_grad[None],
        owned[0],
        owned[1],
        owned[2],
        owned[3],
        owned[4],
        owned[5],
        owned[6],
        owned[7],
        owned[8],
        owned[9],
        owned[10],
        owned[11],
        owned[12],
        owned[13],
        owned[14],
    )


def place():
    rank = lax.axis_index("fsdp")
    core = lax.rem(rank, 2)
    along_x = lax.rem(lax.div(rank, 2), 2)
    along_y = lax.div(rank, 4)
    return (rank, core, along_x, along_y, lax.axis_index("ctx"))


def greet(partners):
    barrier = pltpu.get_barrier_semaphore()
    for partner in partners:
        pl.semaphore_signal(barrier, inc=1, device_id=partner, device_id_type=MESH)
    pl.semaphore_wait(barrier, len(partners))


def remote(source, target, send_sem, recv_sem, device):
    return pltpu.make_async_remote_copy(
        src_ref=source,
        dst_ref=target,
        send_sem=send_sem,
        recv_sem=recv_sem,
        device_id=device,
        device_id_type=MESH,
    )


class Gather:
    def __init__(self, owns, fulls, send_sems, recv_sems, local_sems):
        rank, core, along_x, along_y, depth = place()
        self.owns, self.fulls = owns, fulls
        self.send_sems, self.recv_sems, self.local_sems = send_sems, recv_sems, local_sems
        self.rank = rank
        self.by_x = rank + 2 - 4 * along_x
        self.by_y = rank + 4 - 8 * along_y
        self.diag = self.by_x + 4 - 8 * along_y
        self.to_x = (self.by_x, depth)
        self.to_y = (self.by_y, depth)
        self.to_core = (rank + 1 - 2 * core, depth)
        self.shift = 1 - 2 * core

    def rows(self, number, slot, half):
        size = self.owns[number].shape[0]
        start = pl.multiple_of(slot * size, size)
        if half is None:
            return self.fulls[number].at[pl.ds(start, size)]
        size = size // 2
        return self.fulls[number].at[pl.ds(pl.multiple_of(start + half * size, size), size)]

    def copy(self, number, kind, slot, half, device, own=False):
        target = self.rows(number, slot, half)
        return remote(
            self.owns[number] if own else target,
            target,
            self.send_sems.at[number, kind],
            self.recv_sems.at[number, kind],
            device,
        )

    def sent(self, number, kind):
        slot, half, device = (
            (self.rank, None, self.to_x),
            (self.rank, None, self.to_y),
            (self.rank, None, self.to_core),
            (self.by_x, 0, self.to_y),
            (self.by_y, 1, self.to_x),
            (self.by_x, None, self.to_core),
            (self.by_y, None, self.to_core),
            (self.diag, 0, self.to_core),
            (self.diag, 1, self.to_core),
        )[kind]
        return self.copy(number, kind, slot, half, device, kind < 3)

    def landed(self, number, kind):
        shift = self.shift
        slot, half, device = (
            (self.by_x, None, self.to_x),
            (self.by_y, None, self.to_y),
            (self.rank + shift, None, self.to_core),
            (self.diag, 0, self.to_y),
            (self.diag, 1, self.to_x),
            (self.by_x + shift, None, self.to_core),
            (self.by_y + shift, None, self.to_core),
            (self.diag + shift, 0, self.to_core),
            (self.diag + shift, 1, self.to_core),
        )[kind]
        return self.copy(number, kind, slot, half, device)

    def local(self, number):
        return pltpu.make_async_copy(
            self.owns[number], self.rows(number, self.rank, None), self.local_sems.at[number]
        )

    def issue(self, number):
        for kind in range(3):
            self.sent(number, kind).start()
        self.local(number).start()

    def relay(self, number):
        self.landed(number, 0).wait_recv()
        self.sent(number, 3).start()
        self.landed(number, 1).wait_recv()
        self.sent(number, 4).start()
        self.sent(number, 5).start()
        self.sent(number, 6).start()

    def spread(self, number):
        self.landed(number, 3).wait_recv()
        self.sent(number, 7).start()
        self.landed(number, 4).wait_recv()
        self.sent(number, 8).start()

    def finish(self, number):
        for kind in (2, 5, 6, 7, 8):
            self.landed(number, kind).wait_recv()
        for kind in range(9):
            self.sent(number, kind).wait_send()
        self.local(number).wait()


def column_partners(rank, depth):
    return [(rank, lax.rem(depth + step, DOCS)) for step in range(1, DOCS)]


def tile(index, size=256):
    return pl.ds(pl.multiple_of(index * size, size), size)


def each(count, body):
    def one(index, unused):
        body(index)
        return unused

    lax.fori_loop(0, count, one, 0)


def by_columns(left, right, write):
    def one(index):
        at = tile(index)
        write(at, product(left[...], right[:, at]))

    each(right.shape[1] // 256, one)


def store_as(target):
    def write(at, value):
        target[:, at] = value.astype(target.dtype)

    return write


def rms_rows(values, gain, normed):
    def one(index):
        at = tile(index, 32)
        v = values[at, :]
        root = lax.rsqrt(jnp.mean(v * v, axis=-1, keepdims=True) + epsilon)
        normed[at, :] = (v * root * gain).astype(jnp.bfloat16)

    each(values.shape[0] // 32, one)


def half_masks():
    lane = lax.broadcasted_iota(jnp.int32, (1, 2 * HD), 1)
    low = (lane < HD).astype(jnp.float32)
    return (low.astype(jnp.bfloat16), (1.0 - low).astype(jnp.bfloat16))


def causal_bias(smalls, spread, pair, half):
    row = smalls[tile(pair, 16), :][3:4]
    size = spread.shape[2]
    row = jnp.broadcast_to(row, (8, 128)).astype(jnp.bfloat16)
    line = product(row, spread[half])[0:1]
    bias = pltpu.roll(jnp.broadcast_to(line, (size, size)), 0, 1, stride=1, stride_axis=0)
    here = lax.broadcasted_iota(jnp.int32, (size, size), 0)
    there = lax.broadcasted_iota(jnp.int32, (size, size), 1)
    return jnp.where(there <= here, bias, masked_value)


def softmax_rows(scores):
    terms = jnp.exp(scores - jnp.max(scores, axis=-1, keepdims=True))
    return terms * (1.0 / jnp.sum(terms, axis=-1, keepdims=True))


def attend_heads(queries, keys, values, out, bias_of):
    masks = half_masks()

    def pair(index):
        at = tile(index, 2 * HD)
        q, k, v = queries[:, at], keys[:, at], values[:, at]
        total = jnp.zeros(q.shape, jnp.float32)
        for half in range(2):
            scores = product_right(q * masks[half], k)
            if bias_of is not None:
                scores = scores + bias_of(index, half)
            weights = softmax_rows(scores).astype(jnp.bfloat16)
            total = total + product(weights, v * masks[half])
        out[:, at] = total.astype(jnp.bfloat16)

    each(H // 2, pair)


def column_partners(rank, depth):
    return [(rank, lax.rem(depth + step, DOCS)) for step in range(1, DOCS)]


class Kept:
    inputs, normed, q, k, u, o1, after, normed2, cq = range(9)
    ck, cv, o2, after2, normed3, w, slope, gelu, cot = range(9, 18)
    normed_t, q_t, o1_t, normed2_t, cq_t, o2_t, normed3_t, states_t = range(18, 26)
    count = 26
    wide = (14, 15, 16)
    exact = (0, 6, 12, 15, 16)
    states = (9, 10)
    flipped = tuple(range(18, 26))
    inside = (1, 5, 7, 11, 13)


def forward_kernel(count, *refs):
    owns, refs = refs[:count], refs[count:]
    (tokens, cotangent, chosen, encoded, spread), refs = refs[:5], refs[5:]
    fulls, refs = refs[:count], refs[count:]
    n = Kept.count
    outs, refs = refs[:n], refs[n:]
    grad_out, refs = refs[0], refs[1:]
    keep, refs = refs[:n], refs[n:]
    (
        grad_fd,
        smalls,
        gains,
        all_tokens,
        all_cotangent,
        square,
        wide,
        send_sems,
        recv_sems,
        local_sems,
        line_send,
        line_recv,
        line_local,
        load_sems,
        save_sems,
    ) = refs
    rank, core, along_x, along_y, depth = place()
    gather = Gather(owns, fulls, send_sems, recv_sems, local_sems)
    column = column_partners(rank, depth)
    greet([gather.to_x, gather.to_y, gather.to_core] + column)

    def line_copies(number):
        own, whole = ((tokens, all_tokens), (cotangent, all_cotangent))[number]
        rows = own.shape[0]
        at = whole.at[pl.ds(pl.multiple_of(depth * rows, rows), rows)]
        here = pltpu.make_async_copy(own, at, line_local.at[number])
        sends, receives = [], []
        for step, partner in enumerate(column):
            sems = (line_send.at[number, step], line_recv.at[number, step])
            sends.append(remote(own, at, sems[0], sems[1], partner))
            origin = lax.rem(depth + DOCS - 1 - step, DOCS)
            landing = whole.at[pl.ds(pl.multiple_of(origin * rows, rows), rows)]
            receives.append(remote(own, landing, sems[0], sems[1], partner))
        return (here, sends, receives)

    def line_finish(number):
        here, sends, receives = line_copies(number)
        here.wait()
        for copy in receives:
            copy.wait_recv()
        for copy in sends:
            copy.wait_send()

    for number in range(2):
        here, sends, unused = line_copies(number)
        here.start()
        for copy in sends:
            copy.start()

    def flip(source, name):
        turn(source, keep[name])
        save(name)

    def save(name):
        if name in Kept.inside:
            return
        pltpu.make_async_copy(keep[name], outs[name], save_sems.at[name]).start()

    def load(number, buffer):
        copy = pltpu.make_async_copy(fulls[number], buffer, load_sems.at[number])
        copy.start()
        copy.wait()

    def project(left, number, name):
        load(number, square)
        by_columns(left, square, store_as(keep[name]))
        save(name)

    def residual(before, left, number, name, gain, normed, turned):
        load(number, square)

        def write(at, value):
            keep[name][:, at] = keep[before][:, at] + value

        by_columns(keep[left], square, write)
        save(name)
        rms_rows(keep[name], gains[gain : gain + 1, :], keep[normed])
        flip(keep[normed], turned)

    def start():
        load(0, smalls)
        for slot in range(8):
            gains[0:3, 128 * slot : 128 * slot + 128] = smalls[16 * slot : 16 * slot + 3, :]
        line_finish(0)
        by_columns(chosen, all_tokens, store_as(keep[Kept.inputs]))
        save(Kept.inputs)
        rms_rows(keep[Kept.inputs], gains[0:1, :], keep[Kept.normed])
        flip(keep[Kept.normed], Kept.normed_t)
        flip(encoded, Kept.states_t)

    def keys():
        flip(keep[Kept.q], Kept.q_t)
        project(keep[Kept.normed], 4, Kept.k)

    def self_heads():
        project(keep[Kept.normed], 5, Kept.u)
        attend_heads(
            keep[Kept.q], keep[Kept.k], keep[Kept.u], keep[Kept.o1], functools.partial(causal_bias, smalls, spread)
        )
        flip(keep[Kept.o1], Kept.o1_t)

    def cross_heads():
        project(keep[Kept.normed2], 7, Kept.cq)
        flip(keep[Kept.cq], Kept.cq_t)
        attend_heads(keep[Kept.cq], keep[Kept.ck], keep[Kept.cv], keep[Kept.o2], None)
        flip(keep[Kept.o2], Kept.o2_t)
        line_finish(1)
        by_columns(chosen, all_cotangent, store_as(keep[Kept.cot]))
        save(Kept.cot)

    def gate():
        load(9, wide)
        by_columns(keep[Kept.normed3], wide, store_as(keep[Kept.slope]))

    def up():
        load(10, wide)
        scale = math.sqrt(2.0 / math.pi)

        def write(at, b):
            a = keep[Kept.slope][:, at]
            t = jnp.tanh(scale * (a + 0.044715 * (a * a * a)))
            gelu = 0.5 * a * (1.0 + t)
            slope = 0.5 * (1.0 + t) + 0.5 * a * (1.0 - t * t) * scale * (
                1.0 + 3 * 0.044715 * (a * a)
            )
            keep[Kept.gelu][:, at] = gelu
            keep[Kept.slope][:, at] = slope * b
            w = (gelu * b).astype(jnp.bfloat16)
            keep[Kept.w][:, at] = w
            grad = product_left(w, keep[Kept.cot][...]).astype(jnp.bfloat16)
            for part in range(grad_fd.shape[0]):
                grad_fd[part, at, :] = grad[:, 256 * part : 256 * part + 256]

        by_columns(keep[Kept.normed3], wide, write)
        for name in (Kept.gelu, Kept.slope, Kept.w):
            save(name)
        pltpu.make_async_copy(grad_fd, grad_out, save_sems.at[n]).start()

    compute = (
        start,
        lambda: project(encoded, 1, Kept.ck),
        lambda: project(encoded, 2, Kept.cv),
        lambda: project(keep[Kept.normed], 3, Kept.q),
        keys,
        self_heads,
        lambda: residual(Kept.inputs, Kept.o1, 6, Kept.after, 1, Kept.normed2, Kept.normed2_t),
        cross_heads,
        lambda: residual(Kept.after, Kept.o2, 8, Kept.after2, 2, Kept.normed3, Kept.normed3_t),
        gate,
        up,
        lambda: None,
    )
    for step in range(count + 4):
        if step < count:
            gather.issue(step)
        if 0 <= step - 2 < count:
            gather.relay(step - 2)
        if 0 <= step - 3 < count:
            gather.spread(step - 3)
        if 0 <= step - 4 < count:
            gather.finish(step - 4)
            compute[step - 4]()
    for name in range(n):
        if name not in Kept.inside:
            pltpu.make_async_copy(keep[name], outs[name], save_sems.at[name]).wait()
    pltpu.make_async_copy(grad_fd, grad_out, save_sems.at[n]).wait()


def forward_call(shards, tokens, cotangent, chosen, encoded, spread):
    count = len(shards)
    vmem = pl.BlockSpec(memory_space=pltpu.VMEM)
    anywhere = pl.BlockSpec(memory_space=pl.ANY)
    most, total = chosen.shape
    shapes = [jax.ShapeDtypeStruct((8 * s.shape[0], s.shape[1]), s.dtype) for s in shards]
    saved = []
    for name in range(Kept.count):
        if name in Kept.flipped:
            rows = encoded.shape[0] if name == Kept.states_t else most
            saved.append(((shards[1].shape[1], rows), jnp.bfloat16))
            continue
        rows = encoded.shape[0] if name in Kept.states else most
        width = shards[9].shape[1] if name in Kept.wide else shards[1].shape[1]
        saved.append(((rows, width), jnp.float32 if name in Kept.exact else jnp.bfloat16))
    shapes += [jax.ShapeDtypeStruct(*s) for s in saved]
    down = shapes[count - 1]
    down = jax.ShapeDtypeStruct((down.shape[1] // 256, down.shape[0], 256), down.dtype)
    square = shards[1].shape[1]
    return pl.pallas_call(
        functools.partial(forward_kernel, count),
        out_shape=shapes + [down],
        in_specs=[vmem] * (count + 5),
        out_specs=[anywhere] * (len(shapes) + 1),
        scratch_shapes=[pltpu.VMEM(*s) for s in saved]
        + [
            pltpu.VMEM(down.shape, down.dtype),
            pltpu.VMEM(shapes[0].shape, jnp.float32),
            pltpu.VMEM((8, square), jnp.float32),
            pltpu.VMEM((total, square), jnp.bfloat16),
            pltpu.VMEM((total, square), jnp.bfloat16),
            pltpu.VMEM((square, square), jnp.bfloat16),
            pltpu.VMEM((square, shards[9].shape[1]), jnp.bfloat16),
            pltpu.SemaphoreType.DMA((count, 9)),
            pltpu.SemaphoreType.DMA((count, 9)),
            pltpu.SemaphoreType.DMA((count,)),
            pltpu.SemaphoreType.DMA((2, DOCS - 1)),
            pltpu.SemaphoreType.DMA((2, DOCS - 1)),
            pltpu.SemaphoreType.DMA((2,)),
            pltpu.SemaphoreType.DMA((count,)),
            pltpu.SemaphoreType.DMA((len(saved) + 1,)),
        ],
        compiler_params=pltpu.CompilerParams(
            collective_id=1, has_side_effects=True, vmem_limit_bytes=60 * 2**20
        ),
        name="forward",
    )(*shards, tokens, cotangent, chosen, encoded, spread)


def add_rows(target, source):
    rows = target.shape[1]
    step = math.gcd(rows, 64)

    def one(index):
        at = pl.ds(pl.multiple_of(index * step, step), step)
        target[:, at, :] = target[:, at, :] + source[:, at, :]

    each(rows // step, one)


class Reduce:
    def __init__(self, pieces, buffers, load, send_sems, recv_sems, local_sems):
        rank, core, along_x, along_y, depth = place()
        self.pieces, self.buffers, self.load = pieces, buffers, load
        self.send_sems, self.recv_sems, self.local_sems = send_sems, recv_sems, local_sems
        self.core, self.along_x, self.along_y = core, along_x, along_y
        self.block = 2 * along_y + along_x
        self.to_x = (rank + 2 - 4 * along_x, depth)
        self.to_y = (rank + 4 - 8 * along_y, depth)
        self.to_core = (rank + 1 - 2 * core, depth)
        self.inner = (depth == 1) | (depth == 2)
        self.to_line = (rank, depth + 1 - 2 * lax.rem(depth, 2))
        self.to_middle = (rank, 3 - depth)
        self.partners = [self.to_x, self.to_y, self.to_core, self.to_line, self.to_middle]

    def copy(self, number, kind, source, target, device):
        return remote(
            source,
            target,
            self.send_sems.at[number, kind],
            self.recv_sems.at[number, kind],
            device,
        )

    def halves(self, number):
        size = self.pieces[number].rows // 2
        return (pl.ds(0, size), pl.ds(size, size))

    def core_copies(self, number):
        piece, both = self.pieces[number], self.buffers[number][0]
        return [
            self.copy(number, q, piece.slot(2 * q + 1 - self.core), both.at[q], self.to_core)
            for q in range(4)
        ]

    def own_load(self, number, q):
        return pltpu.make_async_copy(
            self.pieces[number].slot(2 * q + self.core),
            self.load[number].at[q % 2],
            self.local_sems.at[number, q],
        )

    def first_copies(self, number):
        both, from_x, from_y = self.buffers[number][:3]
        low, high = self.halves(number)
        copies = []
        for other in range(2):
            copies.append(
                self.copy(
                    number,
                    4 + other,
                    both.at[2 * other + 1 - self.along_x, :, low],
                    from_x.at[other],
                    self.to_x,
                )
            )
        for other in range(2):
            copies.append(
                self.copy(
                    number,
                    6 + other,
                    both.at[2 * (1 - self.along_y) + other, :, high],
                    from_y.at[other],
                    self.to_y,
                )
            )
        return copies

    def second_copies(self, number):
        both, unused_x, unused_y, late_x, late_y = self.buffers[number][:5]
        low, high = self.halves(number)
        return [
            self.copy(
                number,
                8,
                both.at[2 * (1 - self.along_y) + self.along_x, :, low],
                late_y,
                self.to_y,
            ),
            self.copy(
                number,
                9,
                both.at[2 * self.along_y + 1 - self.along_x, :, high],
                late_x,
                self.to_x,
            ),
        ]

    def line_copy(self, number):
        return self.copy(
            number,
            10,
            self.buffers[number][0].at[self.block],
            self.buffers[number][5],
            self.to_line,
        )

    def middle_copy(self, number):
        return self.copy(
            number,
            11,
            self.buffers[number][0].at[self.block],
            self.buffers[number][6],
            self.to_middle,
        )

    def return_copy(self, number):
        return self.copy(
            number,
            10,
            self.buffers[number][5],
            self.buffers[number][5],
            self.to_line,
        )

    def write(self, number):
        return pltpu.make_async_copy(
            self.buffers[number][5],
            self.pieces[number].out.at[self.pieces[number].tiles],
            self.local_sems.at[number, 4],
        )

    def stage(self, number, level):
        both, from_x, from_y, late_x, late_y, on_line, on_middle = self.buffers[number]
        low, high = self.halves(number)
        if level == 0:
            for copy in self.core_copies(number):
                copy.start()
            self.own_load(number, 0).start()
            self.own_load(number, 1).start()
        elif level == 1:
            for q, copy in enumerate(self.core_copies(number)):
                copy.wait_recv()
                self.own_load(number, q).wait()
                add_rows(both.at[q], self.load[number].at[q % 2])
                if q < 2:
                    self.own_load(number, q + 2).start()
            for copy in self.first_copies(number):
                copy.start()
        elif level == 2:
            copies = self.first_copies(number)
            for other in range(2):
                copies[other].wait_recv()
                copies[other].wait_send()
                add_rows(both.at[2 * other + self.along_x, :, low], from_x.at[other])
            for other in range(2):
                copies[2 + other].wait_recv()
                copies[2 + other].wait_send()
                add_rows(both.at[2 * self.along_y + other, :, high], from_y.at[other])
            for copy in self.second_copies(number):
                copy.start()
        elif level == 3:
            to_y, to_x = self.second_copies(number)
            to_y.wait_recv()
            add_rows(both.at[self.block, :, low], late_y)
            to_x.wait_recv()
            add_rows(both.at[self.block, :, high], late_x)
            to_y.wait_send()
            to_x.wait_send()

            @pl.when(jnp.logical_not(self.inner))
            def _():
                self.line_copy(number).start()
        elif level == 4:

            @pl.when(self.inner)
            def _():
                self.line_copy(number).wait_recv()
                add_rows(both.at[self.block], on_line)
                self.middle_copy(number).start()
        elif level == 5:

            @pl.when(self.inner)
            def _():
                middle = self.middle_copy(number)
                middle.wait_recv()
                rows = on_line.shape[1]
                step = math.gcd(rows, 64)

                def one(index):
                    at = pl.ds(pl.multiple_of(index * step, step), step)
                    on_line[:, at, :] = both[self.block, :, at, :] + on_middle[:, at, :]

                each(rows // step, one)
                middle.wait_send()
                self.return_copy(number).start()
        else:
            line = self.line_copy(number)

            @pl.when(jnp.logical_not(self.inner))
            def _():
                line.wait_send()
                line.wait_recv()

            @pl.when(self.inner)
            def _():
                self.return_copy(number).wait_send()

            for copy in self.core_copies(number):
                copy.wait_send()
            self.write(number).start()

    levels = 7


def buffer_shapes(tiles, rows, width, dtype):
    return [
        pltpu.VMEM((4, tiles, rows, width), dtype),
        pltpu.VMEM((2, tiles, rows // 2, width), dtype),
        pltpu.VMEM((2, tiles, rows // 2, width), dtype),
        pltpu.VMEM((tiles, rows // 2, width), dtype),
        pltpu.VMEM((tiles, rows // 2, width), dtype),
        pltpu.VMEM((tiles, rows, width), dtype),
        pltpu.VMEM((tiles, rows, width), dtype),
    ]


class Piece:
    def __init__(self, grad, out, start, tiles):
        self.grad, self.out = grad, out
        self.tiles = pl.ds(start, tiles)
        self.rows = grad.shape[2]

    def slot(self, index):
        return self.grad.at[self.tiles, index]


def pieces_of(shape):
    most = 1 if shape[2] > 256 else 4
    return [(start, min(most, shape[0] - start)) for start in range(0, shape[0], most)]


def piece_order(shapes):
    parts = [[(number,) + p for p in pieces_of(shape)] for number, shape in enumerate(shapes)]
    turns = [p for both in zip(parts[1], parts[2]) for p in both]
    return parts[0] + turns + [p for part in parts[3:] for p in part]


class Pipeline:
    gaps = (0, 1, 2, 2, 2, 2, 2)

    def __init__(self, reduce, count):
        self.reduce, self.count = reduce, count
        self.done, self.ready = [0] * reduce.levels, 0

    def tick(self):
        before = [self.ready] + list(self.done)
        for level, gap in enumerate(self.gaps):
            limit = before[level]
            if level and limit < self.count:
                limit = limit - gap + 1
            if self.done[level] < limit:
                self.reduce.stage(self.done[level], level)
                self.done[level] += 1

    def drain(self):
        while self.done[-1] < self.count:
            self.tick()


def rms_back(values, cotangent, gain, carry, out, gain_grad):
    def one(index):
        at = tile(index, 32)
        v, gz = values[at, :], cotangent[at, :]
        root = lax.rsqrt(jnp.mean(v * v, axis=-1, keepdims=True) + epsilon)
        scaled = gain * gz
        inner = jnp.mean(scaled * v, axis=-1, keepdims=True)
        gain_grad[...] += jnp.sum(gz * v * root, axis=0, keepdims=True)
        result = carry[at, :].astype(jnp.float32) + root * scaled - v * (root * root * root * inner)
        out[at, :] = result.astype(out.dtype)

    gain_grad[...] = jnp.zeros_like(gain_grad)
    each(values.shape[0] // 32, one)


def diagonal_sums(grad):
    size = grad.shape[1]
    total = grad[0:8]
    for group in range(1, grad.shape[0] // 8):
        part = grad[8 * group : 8 * group + 8]
        total = total + pltpu.roll(part, size - 8 * group, 1)
    row = lax.broadcasted_iota(jnp.int32, total.shape, 0)
    line = jnp.where(row == 0, total, 0.0)
    for step in range(1, 8):
        line = line + jnp.where(row == step, pltpu.roll(total, size - step, 1), 0.0)
    return jnp.sum(line, axis=0, keepdims=True)


def attend_back_heads(
    first, last, queries, flipped, keys, values, grad, grad_flipped, grad_q, grad_k, grad_v, bias_of, bias_grad
):
    masks = half_masks()
    row = lax.broadcasted_iota(jnp.int32, (2 * HD, 1), 0)
    low = (row < HD).astype(jnp.float32)
    sides = (low.astype(jnp.bfloat16), (1.0 - low).astype(jnp.bfloat16))

    def pair(index):
        at = tile(index + first, 2 * HD)
        q, k, v, g = queries[:, at], keys[:, at], values[:, at], grad[:, at]
        qt, gt = flipped[at, :], grad_flipped[at, :]
        total_q = jnp.zeros(q.shape, jnp.float32)
        total_k = jnp.zeros((2 * HD, k.shape[0]), jnp.float32)
        total_v = jnp.zeros((2 * HD, k.shape[0]), jnp.float32)
        for half in range(2):
            scores = product_right(q * masks[half], k)
            if bias_of is not None:
                scores = scores + bias_of(index + first, half)
            weights = softmax_rows(scores)
            grad_w = product_right(g * masks[half], v)
            inner = jnp.sum(weights * grad_w, axis=-1, keepdims=True)
            grad_s = weights * (grad_w - inner)
            if bias_grad is not None:
                bias_grad(index + first, half, grad_s)
            rounded = grad_s.astype(jnp.bfloat16)
            total_q = total_q + product(rounded, k * masks[half])
            total_k = total_k + product(qt * sides[half], rounded)
            total_v = total_v + product(gt * sides[half], weights.astype(jnp.bfloat16))
        grad_q[:, at] = total_q.astype(jnp.bfloat16)
        grad_k[at, :] = total_k.astype(jnp.bfloat16)
        grad_v[at, :] = total_v.astype(jnp.bfloat16)

    each(last - first, pair)


def turn(source, target):
    step = min(256, source.shape[0])

    def one(index):
        at = tile(index, step)
        target[:, at] = source[at, :].T

    each(source.shape[0] // step, one)


class Given:
    inputs, normed_t, q, q_t, k, u, o1_t, after, normed2_t = range(9)
    cq, cq_t, ck, cv, o2_t, after2, normed3_t, w, slope, gelu, cot = range(9, 20)
    states_t, chosen_t, spread, smalls = range(20, 24)
    w_ck, w_cv, w_sq, w_sk, w_sv, w_so, w_cq, w_co, w_fg, w_fu, w_fd = range(24, 35)
    grad_fd = 35
    count = 36


def backward_kernel(shared, *refs):
    given, refs = refs[: Given.count], refs[Given.count :]
    grads, refs = (given[Given.grad_fd],) + refs[:11], refs[11:]
    kept_states, refs = refs[0], refs[1:]
    outs, refs = refs[:12], refs[12:]
    (encoder_out, layer_out, hidden_out), refs = refs[:3], refs[3:]
    order = piece_order([g.shape for g in grads])
    pieces = [Piece(grads[n], outs[n], start, tiles) for n, start, tiles in order]
    count = len(pieces)
    buffers, refs = [refs[7 * i : 7 * i + 7] for i in range(count)], refs[7 * count :]
    loads = [refs[shared[i]] for i in range(count)]
    refs = refs[max(shared) + 1 :]
    (
        one_w,
        two_w,
        three_w,
        backs,
        stage,
        state_stage,
        grad_x,
        grad_n,
        value,
        other,
        cot,
        half_a,
        half_b,
        half_c,
        half_d,
        left,
        turned_q,
        turned_g,
        chosen_t,
        spread,
        smalls,
        gains,
        gain_grad,
        small_grads,
        landing,
        send_sems,
        recv_sems,
        local_sems,
        line_send,
        line_recv,
        load_sems,
        stage_sems,
        out_sems,
    ) = refs
    rank, core, along_x, along_y, depth = place()
    reduce = Reduce(pieces, buffers, loads, send_sems, recv_sems, local_sems)
    column = column_partners(rank, depth)
    greet([reduce.to_x, reduce.to_y, reduce.to_core] + column)
    pipeline = Pipeline(reduce, count)
    tick = pipeline.tick
    numbers = [n for n, unused_start, unused_tiles in order]
    pipeline.ready = numbers.count(0)
    turn_of = iter(range(1 << 20))

    def begin(*pairs):
        copies = []
        for source, target in pairs:
            sem = load_sems.at[next(turn_of) % load_sems.shape[0]]
            copies.append(pltpu.make_async_copy(source, target, sem))
            copies[-1].start()
        return copies

    def end(copies):
        for copy in copies:
            copy.wait()

    def staged(buffers_of, target_of, values, tiles):
        slots = buffers_of.shape[0]

        def copy(index):
            slot = lax.rem(index, slots)
            return pltpu.make_async_copy(buffers_of.at[slot], target_of(index), stage_sems.at[slot])

        def one(index):
            @pl.when(index >= slots)
            def _():
                copy(index - slots).wait()

            buffers_of[lax.rem(index, slots)] = values(tile(index))
            copy(index).start()

        each(tiles, one)
        for index in range(max(0, tiles - slots), tiles):
            copy(jnp.int32(index)).wait()

    def weight_grad(number, right, start=0):
        def values(at):
            result = product(left[...], right[:, at])
            return result.astype(jnp.bfloat16).reshape(stage.shape[1:])

        staged(stage, lambda index: grads[number].at[start + index], values, right.shape[1] // 256)
        pipeline.ready += 1

    def send_back(number, rows):
        def write(index):
            at = tile(index)
            result = product(chosen_t[...], rows[:, at]).astype(jnp.bfloat16)
            backs[number, :, :, at] = result.reshape(backs.shape[1:3] + (256,))

        each(rows.shape[1] // 256, write)
        for step, (unused, partner) in enumerate(column):
            back_copy(number, step, partner).start()

    def back_copy(number, step, partner):
        return remote(
            backs.at[number, partner],
            landing.at[number, step],
            line_send.at[number, step],
            line_recv.at[number, step],
            (rank, partner),
        )

    def receive_back(number, out):
        for step, (unused, partner) in enumerate(column):
            copy = back_copy(number, step, partner)
            copy.wait_recv()
            copy.wait_send()

        def one(index):
            at = tile(index, 32)
            total = backs[number, depth, at, :].astype(jnp.float32)
            for step in range(DOCS - 1):
                total = total + landing[number, step, at, :].astype(jnp.float32)
            out[at, :] = total.astype(jnp.bfloat16)

        each(out.shape[0] // 32, one)

    def norm_grad(values, gain, carry, out):
        rms_back(values, grad_n, gains[gain : gain + 1, :], carry, out, gain_grad)
        for slot in range(8):
            small_grads[0, slot, gain : gain + 1, :] = gain_grad[:, 128 * slot : 128 * slot + 128]

    def round_rows(source, target):
        def one(index):
            at = tile(index, 32)
            target[at, :] = source[at, :].astype(jnp.bfloat16)

        each(source.shape[0] // 32, one)

    def through(right_rows, weights, write):
        def one(index):
            at = tile(index)
            write(at, product_right(right_rows[...], weights[at, :]))

        each(weights.shape[0] // 256, one)

    def head_grads(weights):
        through(half_a, weights, store_as(half_b))

        def one(index):
            at = tile(index)
            turned_g[at, :] = product_right(weights[at, :], half_a[...]).astype(jnp.bfloat16)

        each(weights.shape[0] // 256, one)

    def feed_loads(start, tiles):
        at = pl.ds(256 * start, 256 * tiles)
        width = 256 * tiles
        return begin(
            (given[Given.w_fd].at[at], one_w.at[0:width]),
            (given[Given.slope].at[:, at], value.at[:, 0:width]),
            (given[Given.gelu].at[:, at], other.at[:, 0:width]),
            (given[Given.w].at[:, at], half_a.at[:, 0:width]),
            (given[Given.w_fg].at[:, at], two_w.at[:, 0:width]),
            (given[Given.w_fu].at[:, at], three_w.at[:, 0:width]),
        )

    tick()
    first = begin(
        (given[Given.cot], cot),
        (given[Given.smalls], smalls),
        (given[Given.chosen_t], chosen_t),
        (given[Given.spread], spread),
        (given[Given.normed3_t], left),
    )
    feeds = pieces_of(grads[1].shape)
    loaded = feed_loads(*feeds[0])
    tick()
    end(first)
    for slot in range(8):
        gains[0:3, 128 * slot : 128 * slot + 128] = smalls[16 * slot : 16 * slot + 3, :]
    small_grads[...] = jnp.zeros_like(small_grads)
    for turn_number, (start, tiles) in enumerate(feeds):
        width = 256 * tiles
        down, gate, up = one_w.at[0:width], two_w.at[:, 0:width], three_w.at[:, 0:width]
        part = half_a.at[:, 0:width]
        slope, gelu = value.at[:, 0:width], other.at[:, 0:width]
        gate_grad, up_grad = half_b.at[:, 0:width], half_c.at[:, 0:width]
        end(loaded)

        def split(at, grad_w):
            gate_grad[:, at] = (grad_w * slope[:, at]).astype(jnp.bfloat16)
            up_grad[:, at] = (grad_w * gelu[:, at]).astype(jnp.bfloat16)

        through(cot, down, split)

        def add(index):
            at = tile(index)
            forward = product(part[...], down[:, at])
            back = product_right(gate_grad[...], gate[at, :]) + product_right(up_grad[...], up[at, :])
            if start:
                forward, back = forward + grad_x[:, at], back + grad_n[:, at]
            grad_x[:, at] = forward
            grad_n[:, at] = back

        each(grad_x.shape[1] // 256, add)
        if turn_number + 1 < len(feeds):
            loaded = feed_loads(*feeds[turn_number + 1])
        else:
            loaded = begin(
                (given[Given.after2], value),
                (given[Given.w_co], one_w),
                (given[Given.cq_t], turned_q),
                (given[Given.ck], two_w.at[0:512]),
                (given[Given.cv], two_w.at[512:1024]),
            )
        tick()
        weight_grad(1, gate_grad, start)
        weight_grad(2, up_grad, start)
        tick()

    loaded += begin((given[Given.o2_t], left), (given[Given.cq], half_c))
    end(loaded)

    def last(index):
        at = tile(index, 32)
        half_a[at, :] = (value[at, :] + grad_x[at, :]).astype(jnp.bfloat16)

    each(value.shape[0] // 32, last)
    send_back(0, half_a)
    norm_grad(value, 2, cot, grad_x)
    round_rows(grad_x, half_a)
    tick()
    weight_grad(3, half_a)
    head_grads(one_w)
    tick()
    keys_grad, values_grad = three_w.at[:, 0:512], three_w.at[:, 512:1024]
    states = one_w.at[:, 0:512]
    loaded = begin(
        (given[Given.states_t], states), (given[Given.normed2_t], left), (given[Given.after], value)
    )

    def cross(first, last):
        attend_back_heads(
            first,
            last,
            half_c,
            turned_q,
            two_w.at[0:512],
            two_w.at[512:1024],
            half_b,
            turned_g,
            half_d,
            keys_grad,
            values_grad,
            None,
            None,
        )

    cross(0, 3)
    tick()
    cross(3, 6)
    tick()
    cross(6, 8)
    end(loaded)

    def state_grad(number, right):
        def values(at):
            result = product_right(states[...], right[at, :])
            return result.astype(jnp.bfloat16).reshape(stage.shape[1:])

        staged(stage, lambda index: grads[number].at[index], values, 4)
        pipeline.ready += 1

    state_grad(4, keys_grad)
    state_grad(5, values_grad)
    tick()
    turn(keys_grad, two_w.at[0:512])
    turn(values_grad, two_w.at[512:1024])
    kept = pltpu.make_async_copy(two_w, kept_states, out_sems.at[0])
    kept.start()
    loaded = begin(
        (given[Given.w_cq], one_w),
        (given[Given.w_so], three_w),
        (given[Given.q], half_c),
        (given[Given.q_t], turned_q),
    )
    weight_grad(6, half_d)
    kept.wait()
    end(loaded)
    loaded = begin((given[Given.k], two_w.at[0:256]), (given[Given.u], two_w.at[256:512]))
    through(half_d, one_w, store_as(grad_n))
    loaded += begin((given[Given.o1_t], left))
    norm_grad(value, 1, grad_x, grad_x)
    round_rows(grad_x, half_a)
    end(loaded)
    loaded = begin((given[Given.inputs], value), (given[Given.w_sq], one_w))
    tick()
    weight_grad(7, half_a)
    head_grads(three_w)
    loaded += begin((given[Given.normed_t], left))
    tick()

    def table_grad(index, half, grad_s):
        line = jnp.broadcast_to(diagonal_sums(grad_s), (8, grad_s.shape[1]))
        table = lax.dot_general(
            line,
            spread[half].astype(jnp.float32),
            (((1,), (1,)), ((), ())),
            precision=highest,
            preferred_element_type=jnp.float32,
        )
        small_grads[0, index, 3:4, :] = small_grads[0, index, 3:4, :] + table[0:1]

    keys_grad, values_grad = three_w.at[:, 0:256], three_w.at[:, 256:512]

    def own(first, last):
        attend_back_heads(
            first,
            last,
            half_c,
            turned_q,
            two_w.at[0:256],
            two_w.at[256:512],
            half_b,
            turned_g,
            half_d,
            keys_grad,
            values_grad,
            functools.partial(causal_bias, smalls, spread),
            table_grad,
        )

    own(0, 4)
    tick()
    own(4, 8)
    turn(keys_grad, half_a)
    turn(values_grad, half_b)
    end(loaded)
    loaded = begin((given[Given.w_sk], two_w), (given[Given.w_sv], three_w))
    tick()
    weight_grad(8, half_d)
    weight_grad(9, half_a)
    weight_grad(10, half_b)
    tick()
    end(loaded)

    def sum_three(index):
        at = tile(index)
        grad_n[:, at] = (
            product_right(half_d[...], one_w[at, :])
            + product_right(half_a[...], two_w[at, :])
            + product_right(half_b[...], three_w[at, :])
        )

    each(grad_n.shape[1] // 256, sum_three)
    loaded = begin((given[Given.w_ck], one_w), (given[Given.w_cv], three_w), (kept_states, two_w))
    norm_grad(value, 0, grad_x, half_c)
    small_copy = pltpu.make_async_copy(small_grads, grads[11], out_sems.at[1])
    small_copy.start()
    small_copy.wait()
    pipeline.ready += 1
    tick()
    send_back(1, half_c)
    tick()
    end(loaded)
    staged(
        state_stage,
        lambda index: encoder_out.at[:, tile(index)],
        lambda at: product_right(two_w[0:512], one_w[at, :])
        + product_right(two_w[512:1024], three_w[at, :]),
        4,
    )
    receive_back(0, layer_out)
    pipeline.drain()
    receive_back(1, hidden_out)
    for number in range(count):
        reduce.write(number).wait()


def backward_call(operands, rows):
    count = Given.count
    anywhere = pl.BlockSpec(memory_space=pl.ANY)
    vmem = pl.BlockSpec(memory_space=pltpu.VMEM)
    bf16, f32 = jnp.bfloat16, jnp.float32
    grad_fd = operands[Given.grad_fd]
    width, wide = operands[Given.w_fg].shape
    square = jax.ShapeDtypeStruct((width // 256, 8, width // 8, 256), bf16)
    broad = jax.ShapeDtypeStruct((wide // 256, 8, width // 8, 256), bf16)
    small = jax.ShapeDtypeStruct((1, 8, 16, 128), f32)
    full = [jax.ShapeDtypeStruct(grad_fd.shape, grad_fd.dtype), broad, broad] + [square] * 8 + [small]
    outs = [jax.ShapeDtypeStruct(g.shape[:1] + g.shape[2:], g.dtype) for g in full]
    most = operands[Given.inputs].shape[0]
    states = operands[Given.ck].shape[0]
    total = operands[Given.chosen_t].shape[0]
    kept_states = jax.ShapeDtypeStruct((2 * states, width), bf16)
    tail = [
        jax.ShapeDtypeStruct((states, width), f32),
        jax.ShapeDtypeStruct((rows, width), bf16),
        jax.ShapeDtypeStruct((rows, width), bf16),
    ]
    scratch, load_shapes, shared = [], [], []
    order = piece_order([g.shape for g in full])
    for number, unused, tiles in order:
        shape = (tiles,) + full[number].shape[2:]
        scratch += buffer_shapes(*shape, full[number].dtype)
        key = ((2,) + shape, full[number].dtype)
        held = [i for i, s in enumerate(load_shapes) if s == key]
        if len(held) < 2:
            shared.append(len(load_shapes))
            load_shapes.append(key)
        else:
            last = [i for i in shared if i in held][-1]
            shared.append(held[0] if last == held[1] else held[1])
    scratch += [pltpu.VMEM(*s) for s in load_shapes]
    pieces = len(order)
    scratch += [pltpu.VMEM((width, width), bf16)] * 3
    scratch += [
        pltpu.VMEM((2, DOCS, total // DOCS, width), bf16),
        pltpu.VMEM((3, 8, width // 8, 256), bf16),
        pltpu.VMEM((2, states, 256), f32),
    ]
    scratch += [pltpu.VMEM((most, width), f32)] * 4
    scratch += [pltpu.VMEM((most, width), bf16)] * 5
    scratch += [pltpu.VMEM((width, most), bf16)] * 3
    scratch += [
        pltpu.VMEM((total, most), bf16),
        pltpu.VMEM((2, 128, most), bf16),
        pltpu.VMEM((128, 128), f32),
        pltpu.VMEM((8, width), f32),
        pltpu.VMEM((1, width), f32),
        pltpu.VMEM((1, 8, 16, 128), f32),
        pltpu.VMEM((2, DOCS - 1, rows, width), bf16),
        pltpu.SemaphoreType.DMA((pieces, 12)),
        pltpu.SemaphoreType.DMA((pieces, 12)),
        pltpu.SemaphoreType.DMA((pieces, 5)),
        pltpu.SemaphoreType.DMA((2, DOCS - 1)),
        pltpu.SemaphoreType.DMA((2, DOCS - 1)),
        pltpu.SemaphoreType.DMA((16,)),
        pltpu.SemaphoreType.DMA((3,)),
        pltpu.SemaphoreType.DMA((2,)),
    ]
    results = pl.pallas_call(
        functools.partial(backward_kernel, shared),
        out_shape=full[1:] + [kept_states] + outs + tail,
        in_specs=[anywhere] * count,
        out_specs=[anywhere] * (len(full) + len(outs) + 1) + [vmem] * 2,
        scratch_shapes=scratch,
        compiler_params=pltpu.CompilerParams(
            collective_id=2, has_side_effects=True, vmem_limit_bytes=67043328
        ),
        name="backward",
    )(*operands)
    return results[len(full) :]


def widen_kernel(*refs):
    half = len(refs) // 2
    for source, target in zip(refs[:half], refs[half:]):
        if len(source.shape) == 2:
            target[...] = source[...].astype(target.dtype)
            continue
        for part in range(source.shape[0]):
            target[:, 256 * part : 256 * part + 256] = source[part].astype(target.dtype)


def widen_call(sums, layer_out, hidden_grad):
    operands = list(sums) + [layer_out, hidden_grad]
    shapes = [jax.ShapeDtypeStruct((s.shape[1], s.shape[0] * s.shape[2]), jnp.float32) for s in sums]
    shapes.append(jax.ShapeDtypeStruct(layer_out.shape, layer_out.dtype))
    shapes.append(jax.ShapeDtypeStruct(hidden_grad.shape, jnp.float32))
    vmem = pl.BlockSpec(memory_space=pltpu.VMEM)
    return pl.pallas_call(
        widen_kernel,
        out_shape=shapes,
        in_specs=[vmem] * len(operands),
        out_specs=[vmem] * len(operands),
        name="widen",
    )(*operands)


def pack_small(norms, table):
    rows = [n.astype(jnp.float32) for n in norms]
    rows.append(jnp.pad(table.astype(jnp.float32), (0, 128 - table.shape[0])))
    return jnp.pad(jnp.stack(rows), ((0, 12), (0, 0)))


def by_document(
    hidden_in,
    encoder_states,
    segment_ids,
    encoder_docs,
    self_query,
    self_key,
    self_value,
    self_out,
    cross_query,
    cross_key,
    cross_value,
    cross_out,
    feed_gate,
    feed_up,
    feed_down,
    norm_self,
    norm_cross,
    norm_feed,
    bias_table,
    out_grad,
):
    width = hidden_in.shape[2]
    total = segment_ids.shape[1]
    most = total // 2
    encoded = encoder_states[0]
    small = pack_small((norm_self, norm_cross, norm_feed), bias_table)
    document = lax.dynamic_slice_in_dim(
        encoder_docs[0], lax.axis_index("ctx") * encoded.shape[0], 1, 0
    )
    segments = segment_ids[0]
    start = jnp.sum((segments < document).astype(jnp.int32))
    length = jnp.sum((segments == document).astype(jnp.int32))
    row = lax.broadcasted_iota(jnp.int32, (most, total), 0)
    column = lax.broadcasted_iota(jnp.int32, (most, total), 1)
    chosen = ((row + start == column) & (row < length)).astype(jnp.bfloat16)

    slot = jnp.arange(2 * HD, dtype=jnp.int32)
    position = jnp.arange(most, dtype=jnp.int32)
    bucket = bucket_of(lax.rem(most - position, most))
    spread = jnp.stack(
        [(slot[:, None] == bucket[None] + BUCKETS * half) for half in range(2)]
    ).astype(jnp.bfloat16)
    results = forward_call(
        (
            small,
            cross_key,
            cross_value,
            self_query,
            self_key,
            self_value,
            self_out,
            cross_query,
            cross_out,
            feed_gate,
            feed_up,
            feed_down,
        ),
        hidden_in[0],
        out_grad[0],
        chosen,
        encoded,
        spread,
    )
    kept = results[12:]
    grad_fd = results[-1].reshape(width // 256, 8, -1, 256)
    forward_side = [
        kept[i]
        for i in (
            Kept.inputs,
            Kept.normed_t,
            Kept.q,
            Kept.q_t,
            Kept.k,
            Kept.u,
            Kept.o1_t,
            Kept.after,
            Kept.normed2_t,
            Kept.cq,
            Kept.cq_t,
            Kept.ck,
            Kept.cv,
            Kept.o2_t,
            Kept.after2,
            Kept.normed3_t,
            Kept.w,
            Kept.slope,
            Kept.gelu,
            Kept.cot,
            Kept.states_t,
        )
    ]
    results = backward_call(
        forward_side + [chosen.T, spread] + list(results[:12]) + [grad_fd], hidden_in.shape[1]
    )
    smalls, encoder_grad, layer_out, hidden_grad = results[11:]
    fd, fg, fu, co, ck, cv, cq, so, sq, sk, sv, layer_out, hidden_grad = widen_call(
        results[:11], layer_out, hidden_grad
    )
    smalls = smalls[0]
    return (
        layer_out[None],
        hidden_grad[None],
        encoder_grad[None],
        sq,
        sk,
        sv,
        so,
        cq,
        ck,
        cv,
        co,
        fg,
        fu,
        fd,
        smalls[0],
        smalls[1],
        smalls[2],
        smalls[3, : bias_table.shape[0]],
    )


def layer(sizes, *args):
    encoder_states, encoder_docs = args[1], args[3]
    whole_document = encoder_states.shape[1] * DOCS == encoder_docs.shape[1]
    if whole_document and sizes["fsdp"] == 8 and sizes["ctx"] == DOCS:
        return by_document(*args)
    return on_device(*args)


def solution(mesh):
    in_specs = (
        P("fsdp", "ctx", None),
        P("fsdp", "ctx", None),
        P("fsdp", None),
        P("fsdp", None),
        P("fsdp", None),
        P("fsdp", None),
        P("fsdp", None),
        P("fsdp", None),
        P("fsdp", None),
        P("fsdp", None),
        P("fsdp", None),
        P("fsdp", None),
        P("fsdp", None),
        P("fsdp", None),
        P("fsdp", None),
        P("fsdp"),
        P("fsdp"),
        P("fsdp"),
        P("fsdp"),
        P("fsdp", "ctx", None),
    )
    out_specs = (
        P("fsdp", "ctx", None),
        P("fsdp", "ctx", None),
        P("fsdp", "ctx", None),
        P("fsdp", None),
        P("fsdp", None),
        P("fsdp", None),
        P("fsdp", None),
        P("fsdp", None),
        P("fsdp", None),
        P("fsdp", None),
        P("fsdp", None),
        P("fsdp", None),
        P("fsdp", None),
        P("fsdp", None),
        P("fsdp"),
        P("fsdp"),
        P("fsdp"),
        P("fsdp"),
    )
    return jax.shard_map(
        functools.partial(layer, dict(mesh.shape)), mesh=mesh, in_specs=in_specs, out_specs=out_specs, check_vma=False
    )
```

```python
import functools
import math

import jax
import jax.numpy as jnp
from jax import lax
from jax.experimental import pallas as pl
from jax.experimental.pallas import tpu as pltpu
from jax.sharding import PartitionSpec as P

H = 16
HD = 64
BUCKETS = 32
DOCS = 4
MESH = pl.DeviceIdType.MESH


bucket_edges = (19, 21, 24, 27, 31, 35, 40, 46, 52, 59, 67, 77, 87, 99, 113)
epsilon = 1e-06
masked_value = -1e30
highest = lax.Precision.HIGHEST


def normalize(values, gain_vector):
    inverse_root = lax.rsqrt(jnp.mean(values * values, axis=-1, keepdims=True) + epsilon)
    return values * inverse_root * gain_vector


def norm_back(values, gain_vector, grad_normed):
    unused, pullback = jax.vjp(normalize, values, gain_vector)
    return pullback(grad_normed)


def product(left_side, right_side):
    return jnp.dot(left_side, right_side, preferred_element_type=jnp.float32)


def product_left(left_side, right_side):
    return lax.dot_general(
        left_side, right_side, (((0,), (0,)), ((), ())), preferred_element_type=jnp.float32
    )


def product_right(left_side, right_side):
    return lax.dot_general(
        left_side, right_side, (((1,), (1,)), ((), ())), preferred_element_type=jnp.float32
    )


def bucket_of(distance):
    bucket_index = jnp.minimum(distance, 16)
    for threshold in bucket_edges:
        bucket_index = bucket_index + (distance >= threshold).astype(jnp.int32)
    return bucket_index


def bucket_onehot(distance):
    return (bucket_of(distance)[:, :, None] == jnp.arange(BUCKETS, dtype=jnp.int32)).astype(jnp.bfloat16)


def split_blocks(rows_all):
    total_rows = rows_all.shape[0]
    block_rows = math.gcd(total_rows, 512)
    return (block_rows, rows_all.reshape(total_rows // block_rows, block_rows, H, HD))


def block_logits(query_heads, key_part, allowed, distance, table_rows):
    scores = jnp.einsum("qhd,khd->hqk", query_heads, key_part, preferred_element_type=jnp.float32)
    onehot = None
    if table_rows is not None:
        onehot = bucket_onehot(distance)
        scores = scores + jnp.einsum(
            "qkb,hb->hqk", onehot, table_rows, preferred_element_type=jnp.float32
        )
    return (jnp.where(allowed[None], scores, masked_value), onehot)


def attention_forward(query_heads, key_rows, value_rows, mask_of, table_rows):
    block_rows, key_blocks = split_blocks(key_rows)
    unused, value_blocks = split_blocks(value_rows)
    numbers = jnp.arange(key_blocks.shape[0], dtype=jnp.int32)
    query_count = query_heads.shape[0]

    def total_step(carried, element):
        number, key_part = element
        allowed, distance = mask_of(number, block_rows)

        def total_live_branch(state):
            running, summed = state
            scores, unused_hot = block_logits(query_heads, key_part, allowed, distance, table_rows)
            newest = jnp.maximum(running, jnp.max(scores, axis=-1))
            exp_terms = jnp.where(allowed[None], jnp.exp(scores - newest[..., None]), 0.0)
            return (newest, summed * jnp.exp(running - newest) + jnp.sum(exp_terms, axis=-1))

        return (lax.cond(jnp.any(allowed), total_live_branch, lambda state: state, carried), None)

    start_state = (
        jnp.full((H, query_count), masked_value, jnp.float32),
        jnp.zeros((H, query_count), jnp.float32),
    )
    (running, summed), unused_out = lax.scan(total_step, start_state, (numbers, key_blocks))
    logsum = running + jnp.log(summed)

    def output_step(carried, element):
        number, key_part, value_part = element
        allowed, distance = mask_of(number, block_rows)

        def output_live_branch(state):
            scores, unused_hot = block_logits(query_heads, key_part, allowed, distance, table_rows)
            weights = jnp.where(allowed[None], jnp.exp(scores - logsum[..., None]), 0.0).astype(
                jnp.bfloat16
            )
            return state + jnp.einsum(
                "hqk,khd->qhd", weights, value_part, preferred_element_type=jnp.float32
            )

        return (lax.cond(jnp.any(allowed), output_live_branch, lambda state: state, carried), None)

    output, unused_out = lax.scan(
        output_step,
        jnp.zeros((query_count, H, HD), jnp.float32),
        (numbers, key_blocks, value_blocks),
    )
    return (output, logsum)


def attention_delta(query_heads, key_rows, value_rows, grad_heads, logsum, mask_of, table_rows):
    block_rows, key_blocks = split_blocks(key_rows)
    unused, value_blocks = split_blocks(value_rows)
    numbers = jnp.arange(key_blocks.shape[0], dtype=jnp.int32)
    query_count = query_heads.shape[0]

    def delta_step(carried, element):
        number, key_part, value_part = element
        allowed, distance = mask_of(number, block_rows)

        def delta_live_branch(state):
            scores, unused_hot = block_logits(query_heads, key_part, allowed, distance, table_rows)
            weights = jnp.where(allowed[None], jnp.exp(scores - logsum[..., None]), 0.0)
            grad_weights = jnp.einsum(
                "qhd,khd->hqk", grad_heads, value_part, preferred_element_type=jnp.float32
            )
            return state + jnp.sum(weights * grad_weights, axis=-1)

        return (lax.cond(jnp.any(allowed), delta_live_branch, lambda state: state, carried), None)

    row_delta, unused_out = lax.scan(
        delta_step, jnp.zeros((H, query_count), jnp.float32), (numbers, key_blocks, value_blocks)
    )
    return row_delta


def attention_backward(
    query_heads, key_rows, value_rows, grad_heads, logsum, row_delta, mask_of, table_rows
):
    block_rows, key_blocks = split_blocks(key_rows)
    unused, value_blocks = split_blocks(value_rows)
    numbers = jnp.arange(key_blocks.shape[0], dtype=jnp.int32)
    query_count = query_heads.shape[0]
    part_shape = (block_rows, H, HD)

    def grad_step(carried, element):
        number, key_part, value_part = element
        allowed, distance = mask_of(number, block_rows)

        def grad_live_branch(state):
            grad_query, grad_table = state
            scores, onehot = block_logits(query_heads, key_part, allowed, distance, table_rows)
            weights = jnp.where(allowed[None], jnp.exp(scores - logsum[..., None]), 0.0)
            grad_weights = jnp.einsum(
                "qhd,khd->hqk", grad_heads, value_part, preferred_element_type=jnp.float32
            )
            grad_scores = weights * (grad_weights - row_delta[..., None])
            rounded = grad_scores.astype(jnp.bfloat16)
            grad_query = grad_query + jnp.einsum(
                "hqk,khd->qhd", rounded, key_part, preferred_element_type=jnp.float32
            )
            if table_rows is not None:
                grad_table = grad_table + jnp.einsum(
                    "hqk,qkb->hb", grad_scores, onehot.astype(jnp.float32), precision=highest
                )
            grad_key_part = jnp.einsum(
                "hqk,qhd->khd", rounded, query_heads, preferred_element_type=jnp.float32
            )
            grad_value_part = jnp.einsum(
                "hqk,qhd->khd",
                weights.astype(jnp.bfloat16),
                grad_heads,
                preferred_element_type=jnp.float32,
            )
            return ((grad_query, grad_table), (grad_key_part, grad_value_part))

        def dead_branch(state):
            return (state, (jnp.zeros(part_shape, jnp.float32), jnp.zeros(part_shape, jnp.float32)))

        return lax.cond(jnp.any(allowed), grad_live_branch, dead_branch, carried)

    table_shape = (H, BUCKETS) if table_rows is not None else (1, 1)
    start_state = (
        jnp.zeros((query_count, H, HD), jnp.float32),
        jnp.zeros(table_shape, jnp.float32),
    )
    (grad_query, grad_table), key_parts = lax.scan(
        grad_step, start_state, (numbers, key_blocks, value_blocks)
    )
    total_rows = key_rows.shape[0]
    return (
        grad_query,
        grad_table,
        key_parts[0].reshape(total_rows, H * HD),
        key_parts[1].reshape(total_rows, H * HD),
    )


def on_device(
    hidden_in,
    encoder_states,
    segment_ids,
    encoder_docs,
    self_query,
    self_key,
    self_value,
    self_out,
    cross_query,
    cross_key,
    cross_value,
    cross_out,
    feed_gate,
    feed_up,
    feed_down,
    norm_self,
    norm_cross,
    norm_feed,
    bias_table,
    out_grad,
):
    gathered = (
        lax.all_gather(self_query, "fsdp", axis=0, tiled=True),
        lax.all_gather(self_key, "fsdp", axis=0, tiled=True),
        lax.all_gather(self_value, "fsdp", axis=0, tiled=True),
        lax.all_gather(self_out, "fsdp", axis=0, tiled=True),
        lax.all_gather(cross_query, "fsdp", axis=0, tiled=True),
        lax.all_gather(cross_key, "fsdp", axis=0, tiled=True),
        lax.all_gather(cross_value, "fsdp", axis=0, tiled=True),
        lax.all_gather(cross_out, "fsdp", axis=0, tiled=True),
        lax.all_gather(feed_gate, "fsdp", axis=0, tiled=True),
        lax.all_gather(feed_up, "fsdp", axis=0, tiled=True),
        lax.all_gather(feed_down, "fsdp", axis=0, tiled=True),
        lax.all_gather(norm_self, "fsdp", axis=0, tiled=True),
        lax.all_gather(norm_cross, "fsdp", axis=0, tiled=True),
        lax.all_gather(norm_feed, "fsdp", axis=0, tiled=True),
        lax.all_gather(bias_table, "fsdp", axis=0, tiled=True),
    )
    tokens = hidden_in[0]
    encoded = encoder_states[0]
    segments = segment_ids[0]
    documents = encoder_docs[0]
    tok_rows = tokens.shape[0]
    first_row = lax.axis_index("ctx") * tok_rows
    query_pos = first_row + jnp.arange(tok_rows, dtype=jnp.int32)
    query_seg = lax.dynamic_slice_in_dim(segments, first_row, tok_rows, 0)

    def self_mask(number, block_rows):
        key_pos = number * block_rows + jnp.arange(block_rows, dtype=jnp.int32)
        key_seg = lax.dynamic_slice_in_dim(segments, number * block_rows, block_rows, 0)
        distance = query_pos[:, None] - key_pos[None, :]
        allowed = (distance >= 0) & (query_seg[:, None] == key_seg[None, :])
        return (allowed, jnp.maximum(distance, 0))

    def cross_mask(number, block_rows):
        key_doc = lax.dynamic_slice_in_dim(documents, number * block_rows, block_rows, 0)
        return (query_seg[:, None] == key_doc[None, :], None)

    inputs = tokens.astype(jnp.float32)
    self_normed = normalize(inputs, gathered[11].astype(jnp.float32)).astype(jnp.bfloat16)
    queries = product(self_normed, gathered[0]).astype(jnp.bfloat16)
    key_local = product(self_normed, gathered[1]).astype(jnp.bfloat16)
    value_local = product(self_normed, gathered[2]).astype(jnp.bfloat16)
    key_rows, value_rows = (
        lax.all_gather(key_local, "ctx", axis=0, tiled=True),
        lax.all_gather(value_local, "ctx", axis=0, tiled=True),
    )
    table_rows = gathered[14].reshape(H, BUCKETS)
    query_heads = queries.reshape(tok_rows, H, HD)
    key_heads = key_rows.reshape(-1, H, HD)
    value_heads = value_rows.reshape(-1, H, HD)
    self_heads, self_logsum = attention_forward(
        query_heads, key_heads, value_heads, self_mask, table_rows
    )
    self_attended = self_heads.reshape(tok_rows, H * HD).astype(jnp.bfloat16)
    after_self = inputs + product(self_attended, gathered[3])
    cross_normed = normalize(after_self, gathered[12].astype(jnp.float32)).astype(jnp.bfloat16)
    cross_queries = product(cross_normed, gathered[4]).astype(jnp.bfloat16)
    cross_key_local = product(encoded, gathered[5]).astype(jnp.bfloat16)
    cross_value_local = product(encoded, gathered[6]).astype(jnp.bfloat16)
    cross_keys, cross_values = (
        lax.all_gather(cross_key_local, "ctx", axis=0, tiled=True),
        lax.all_gather(cross_value_local, "ctx", axis=0, tiled=True),
    )
    cross_query_heads = cross_queries.reshape(tok_rows, H, HD)
    cross_key_heads = cross_keys.reshape(-1, H, HD)
    cross_value_heads = cross_values.reshape(-1, H, HD)
    cross_heads, cross_logsum = attention_forward(
        cross_query_heads, cross_key_heads, cross_value_heads, cross_mask, None
    )
    cross_attended = cross_heads.reshape(tok_rows, H * HD).astype(jnp.bfloat16)
    after_cross = after_self + product(cross_attended, gathered[7])
    feed_normed = normalize(after_cross, gathered[13].astype(jnp.float32)).astype(jnp.bfloat16)
    gate_value = product(feed_normed, gathered[8])
    up_value = product(feed_normed, gathered[9])
    hidden_units = (jax.nn.gelu(gate_value, approximate=True) * up_value).astype(jnp.bfloat16)
    layer_out = (after_cross + product(hidden_units, gathered[10])).astype(jnp.bfloat16)
    grad_after = out_grad[0].astype(jnp.float32)
    grad_round = grad_after.astype(jnp.bfloat16)
    grad_feed_down = product_left(hidden_units, grad_round)
    grad_hidden = product_right(grad_round, gathered[10])
    unused, pullback = jax.vjp(
        lambda gate_in, up_in: jax.nn.gelu(gate_in, approximate=True) * up_in, gate_value, up_value
    )
    grad_gate, grad_up = pullback(grad_hidden)
    gate_round = grad_gate.astype(jnp.bfloat16)
    up_round = grad_up.astype(jnp.bfloat16)
    grad_feed_gate = product_left(feed_normed, gate_round)
    grad_feed_up = product_left(feed_normed, up_round)
    grad_feed_normed = product_right(gate_round, gathered[8]) + product_right(up_round, gathered[9])
    grad_cross_side, grad_norm_feed = norm_back(
        after_cross, gathered[13].astype(jnp.float32), grad_feed_normed
    )
    grad_after_cross = grad_after + grad_cross_side
    cross_round = grad_after_cross.astype(jnp.bfloat16)
    grad_cross_out = product_left(cross_attended, cross_round)
    grad_cross_heads = (
        product_right(cross_round, gathered[7]).astype(jnp.bfloat16).reshape(tok_rows, H, HD)
    )
    cross_delta = attention_delta(
        cross_query_heads,
        cross_key_heads,
        cross_value_heads,
        grad_cross_heads,
        cross_logsum,
        cross_mask,
        None,
    )
    grad_cross_q, unused_table, grad_cross_k, grad_cross_v = attention_backward(
        cross_query_heads,
        cross_key_heads,
        cross_value_heads,
        grad_cross_heads,
        cross_logsum,
        cross_delta,
        cross_mask,
        None,
    )
    cross_key_grad, cross_value_grad = (
        lax.psum_scatter(
            grad_cross_k.astype(jnp.bfloat16), "ctx", scatter_dimension=0, tiled=True
        ).astype(jnp.float32),
        lax.psum_scatter(
            grad_cross_v.astype(jnp.bfloat16), "ctx", scatter_dimension=0, tiled=True
        ).astype(jnp.float32),
    )
    cross_key_round = cross_key_grad.astype(jnp.bfloat16)
    cross_value_round = cross_value_grad.astype(jnp.bfloat16)
    grad_cross_key = product_left(encoded, cross_key_round)
    grad_cross_value = product_left(encoded, cross_value_round)
    encoder_grad = product_right(cross_key_round, gathered[5]) + product_right(
        cross_value_round, gathered[6]
    )
    cross_query_round = grad_cross_q.reshape(tok_rows, H * HD).astype(jnp.bfloat16)
    grad_cross_query = product_left(cross_normed, cross_query_round)
    grad_cross_normed = product_right(cross_query_round, gathered[4])
    grad_self_side, grad_norm_cross = norm_back(
        after_self, gathered[12].astype(jnp.float32), grad_cross_normed
    )
    grad_after_self = grad_after_cross + grad_self_side
    self_round = grad_after_self.astype(jnp.bfloat16)
    grad_self_out = product_left(self_attended, self_round)
    grad_self_flat = product_right(self_round, gathered[3]).astype(jnp.bfloat16)
    grad_self_heads = grad_self_flat.reshape(tok_rows, H, HD)
    back_table = gathered[14].reshape(H, BUCKETS)
    self_delta = attention_delta(
        query_heads, key_heads, value_heads, grad_self_heads, self_logsum, self_mask, back_table
    )
    grad_self_q, grad_table, grad_self_k, grad_self_v = attention_backward(
        query_heads,
        key_heads,
        value_heads,
        grad_self_heads,
        self_logsum,
        self_delta,
        self_mask,
        back_table,
    )
    self_key_grad, self_value_grad = (
        lax.psum_scatter(
            grad_self_k.astype(jnp.bfloat16), "ctx", scatter_dimension=0, tiled=True
        ).astype(jnp.float32),
        lax.psum_scatter(
            grad_self_v.astype(jnp.bfloat16), "ctx", scatter_dimension=0, tiled=True
        ).astype(jnp.float32),
    )
    self_key_round = self_key_grad.astype(jnp.bfloat16)
    self_value_round = self_value_grad.astype(jnp.bfloat16)
    self_query_round = grad_self_q.reshape(tok_rows, H * HD).astype(jnp.bfloat16)
    grad_self_query = product_left(self_normed, self_query_round)
    grad_self_key = product_left(self_normed, self_key_round)
    grad_self_value = product_left(self_normed, self_value_round)
    grad_self_normed = (
        product_right(self_query_round, gathered[0])
        + product_right(self_key_round, gathered[1])
        + product_right(self_value_round, gathered[2])
    )
    grad_input_side, grad_norm_self = norm_back(
        inputs, gathered[11].astype(jnp.float32), grad_self_normed
    )
    hidden_grad = grad_after_self + grad_input_side
    grad_bias_table = grad_table.reshape(H * BUCKETS)
    pieces = (
        lax.psum_scatter(
            grad_self_query.astype(jnp.bfloat16), "fsdp", scatter_dimension=0, tiled=True
        ).astype(jnp.float32),
        lax.psum_scatter(
            grad_self_key.astype(jnp.bfloat16), "fsdp", scatter_dimension=0, tiled=True
        ).astype(jnp.float32),
        lax.psum_scatter(
            grad_self_value.astype(jnp.bfloat16), "fsdp", scatter_dimension=0, tiled=True
        ).astype(jnp.float32),
        lax.psum_scatter(
            grad_self_out.astype(jnp.bfloat16), "fsdp", scatter_dimension=0, tiled=True
        ).astype(jnp.float32),
        lax.psum_scatter(
            grad_cross_query.astype(jnp.bfloat16), "fsdp", scatter_dimension=0, tiled=True
        ).astype(jnp.float32),
        lax.psum_scatter(
            grad_cross_key.astype(jnp.bfloat16), "fsdp", scatter_dimension=0, tiled=True
        ).astype(jnp.float32),
        lax.psum_scatter(
            grad_cross_value.astype(jnp.bfloat16), "fsdp", scatter_dimension=0, tiled=True
        ).astype(jnp.float32),
        lax.psum_scatter(
            grad_cross_out.astype(jnp.bfloat16), "fsdp", scatter_dimension=0, tiled=True
        ).astype(jnp.float32),
        lax.psum_scatter(
            grad_feed_gate.astype(jnp.bfloat16), "fsdp", scatter_dimension=0, tiled=True
        ).astype(jnp.float32),
        lax.psum_scatter(
            grad_feed_up.astype(jnp.bfloat16), "fsdp", scatter_dimension=0, tiled=True
        ).astype(jnp.float32),
        lax.psum_scatter(
            grad_feed_down.astype(jnp.bfloat16), "fsdp", scatter_dimension=0, tiled=True
        ).astype(jnp.float32),
        lax.psum_scatter(
            grad_norm_self.astype(jnp.bfloat16), "fsdp", scatter_dimension=0, tiled=True
        ).astype(jnp.float32),
        lax.psum_scatter(
            grad_norm_cross.astype(jnp.bfloat16), "fsdp", scatter_dimension=0, tiled=True
        ).astype(jnp.float32),
        lax.psum_scatter(
            grad_norm_feed.astype(jnp.bfloat16), "fsdp", scatter_dimension=0, tiled=True
        ).astype(jnp.float32),
        lax.psum_scatter(
            grad_bias_table.astype(jnp.bfloat16), "fsdp", scatter_dimension=0, tiled=True
        ).astype(jnp.float32),
    )
    owned = (
        lax.psum(pieces[0].astype(jnp.bfloat16), "ctx").astype(jnp.float32),
        lax.psum(pieces[1].astype(jnp.bfloat16), "ctx").astype(jnp.float32),
        lax.psum(pieces[2].astype(jnp.bfloat16), "ctx").astype(jnp.float32),
        lax.psum(pieces[3].astype(jnp.bfloat16), "ctx").astype(jnp.float32),
        lax.psum(pieces[4].astype(jnp.bfloat16), "ctx").astype(jnp.float32),
        lax.psum(pieces[5].astype(jnp.bfloat16), "ctx").astype(jnp.float32),
        lax.psum(pieces[6].astype(jnp.bfloat16), "ctx").astype(jnp.float32),
        lax.psum(pieces[7].astype(jnp.bfloat16), "ctx").astype(jnp.float32),
        lax.psum(pieces[8].astype(jnp.bfloat16), "ctx").astype(jnp.float32),
        lax.psum(pieces[9].astype(jnp.bfloat16), "ctx").astype(jnp.float32),
        lax.psum(pieces[10].astype(jnp.bfloat16), "ctx").astype(jnp.float32),
        lax.psum(pieces[11].astype(jnp.bfloat16), "ctx").astype(jnp.float32),
        lax.psum(pieces[12].astype(jnp.bfloat16), "ctx").astype(jnp.float32),
        lax.psum(pieces[13].astype(jnp.bfloat16), "ctx").astype(jnp.float32),
        lax.psum(pieces[14].astype(jnp.bfloat16), "ctx").astype(jnp.float32),
    )
    return (
        layer_out[None],
        hidden_grad[None],
        encoder_grad[None],
        owned[0],
        owned[1],
        owned[2],
        owned[3],
        owned[4],
        owned[5],
        owned[6],
        owned[7],
        owned[8],
        owned[9],
        owned[10],
        owned[11],
        owned[12],
        owned[13],
        owned[14],
    )


def place():
    rank = lax.axis_index("fsdp")
    core = lax.rem(rank, 2)
    along_x = lax.rem(lax.div(rank, 2), 2)
    along_y = lax.div(rank, 4)
    return (rank, core, along_x, along_y, lax.axis_index("ctx"))


def greet(partners):
    barrier = pltpu.get_barrier_semaphore()
    for partner in partners:
        pl.semaphore_signal(barrier, inc=1, device_id=partner, device_id_type=MESH)
    pl.semaphore_wait(barrier, len(partners))


def remote(source, target, send_sem, recv_sem, device):
    return pltpu.make_async_remote_copy(
        src_ref=source,
        dst_ref=target,
        send_sem=send_sem,
        recv_sem=recv_sem,
        device_id=device,
        device_id_type=MESH,
    )


class Unit:
    def __init__(self, number, start, rows, flat, first, last):
        self.number, self.start, self.rows = number, start, rows
        self.flat, self.first, self.last = flat, first, last


def units_of(shapes, flat_count):
    units = []
    for number, (rows, columns) in enumerate(shapes):
        parts = max(1, rows * columns // (176 * 1024)) if number < len(shapes) - 1 else 4
        most = -(-rows // parts // 16) * 16
        starts = list(range(0, rows, most))
        for start in starts:
            size = min(most, rows - start)
            units.append(Unit(number, start, size, number < flat_count, start == 0, start == starts[-1]))
    return units


class Gather:
    def __init__(self, units, owns, fulls, send_sems, recv_sems, local_sems):
        rank, core, along_x, along_y, depth = place()
        self.units, self.owns, self.fulls = units, owns, fulls
        self.send_sems, self.recv_sems, self.local_sems = send_sems, recv_sems, local_sems
        self.rank = rank
        self.by_x = rank + 2 - 4 * along_x
        self.by_y = rank + 4 - 8 * along_y
        self.diag = self.by_x + 4 - 8 * along_y
        self.to_x = (self.by_x, depth)
        self.to_y = (self.by_y, depth)
        self.to_core = (rank + 1 - 2 * core, depth)
        self.shift = 1 - 2 * core
        odd = lax.rem(depth, 2)
        self.odd = odd == 1
        self.to_pair = (rank, depth + 1 - 2 * odd)
        self.second = self.by_x + odd * (self.diag - self.by_x)
        self.third = self.diag + odd * (self.by_x - self.diag)

    def rows(self, index, slot, half):
        unit = self.units[index]
        size = self.owns[unit.number].shape[0]
        start = pl.multiple_of(slot * size + unit.start, math.gcd(size, unit.start))
        rows = unit.rows
        if half is not None:
            rows = rows // 2
            start = pl.multiple_of(start + half * rows, math.gcd(size, unit.start, rows))
        return self.fulls[unit.number].at[pl.ds(start, rows)]

    def copy(self, index, kind, slot, half, device, own=False):
        target = self.rows(index, slot, half)
        unit = self.units[index]
        return remote(
            self.owns[unit.number].at[pl.ds(unit.start, unit.rows)] if own else target,
            target,
            self.send_sems.at[index, kind],
            self.recv_sems.at[index, kind],
            device,
        )

    def sent(self, index, kind):
        flat = (
            (self.rank, None, self.to_x),
            (self.rank, None, self.to_y),
            (self.rank, None, self.to_core),
            (self.by_x, 0, self.to_y),
            (self.by_y, 1, self.to_x),
            (self.by_x, None, self.to_core),
            (self.by_y, None, self.to_core),
            (self.diag, 0, self.to_core),
            (self.diag, 1, self.to_core),
        )
        line = (
            (self.rank, None, self.to_x),
            (self.rank, None, self.to_y),
            (self.rank, None, self.to_core),
            (self.by_y, None, self.to_x),
            (self.second, None, self.to_pair),
            (self.by_y, None, self.to_core),
            (self.second, None, self.to_core),
            (self.third, None, self.to_core),
        )
        slot, half, device = (flat if self.units[index].flat else line)[kind]
        return self.copy(index, kind, slot, half, device, kind < 3)

    def landed(self, index, kind):
        shift = self.shift
        flat = (
            (self.by_x, None, self.to_x),
            (self.by_y, None, self.to_y),
            (self.rank + shift, None, self.to_core),
            (self.diag, 0, self.to_y),
            (self.diag, 1, self.to_x),
            (self.by_x + shift, None, self.to_core),
            (self.by_y + shift, None, self.to_core),
            (self.diag + shift, 0, self.to_core),
            (self.diag + shift, 1, self.to_core),
        )
        line = (
            (self.by_x, None, self.to_x),
            (self.by_y, None, self.to_y),
            (self.rank + shift, None, self.to_core),
            (self.diag, None, self.to_x),
            (self.third, None, self.to_pair),
            (self.by_y + shift, None, self.to_core),
            (self.second + shift, None, self.to_core),
            (self.third + shift, None, self.to_core),
        )
        slot, half, device = (flat if self.units[index].flat else line)[kind]
        return self.copy(index, kind, slot, half, device)

    def local(self, number):
        size = self.owns[number].shape[0]
        start = pl.multiple_of(self.rank * size, size)
        target = self.fulls[number].at[pl.ds(start, size)]
        return pltpu.make_async_copy(self.owns[number], target, self.local_sems.at[number])

    def by_pair(self, even, odd):
        pl.when(jnp.logical_not(self.odd))(even)
        pl.when(self.odd)(odd)

    def issue(self, index):
        unit = self.units[index]
        self.sent(index, 1).start()
        if unit.flat:
            self.sent(index, 0).start()
        else:
            pl.when(jnp.logical_not(self.odd))(lambda: self.sent(index, 0).start())
        self.sent(index, 2).start()
        if unit.first:
            self.local(unit.number).start()

    def relay(self, index):
        if self.units[index].flat:
            self.landed(index, 0).wait_recv()
            self.sent(index, 3).start()
            self.landed(index, 1).wait_recv()
            self.sent(index, 4).start()
            self.sent(index, 5).start()
            self.sent(index, 6).start()
            return
        self.landed(index, 1).wait_recv()
        pl.when(self.odd)(lambda: self.sent(index, 3).start())
        self.sent(index, 5).start()

    def spread(self, index):
        if self.units[index].flat:
            self.landed(index, 3).wait_recv()
            self.sent(index, 7).start()
            self.landed(index, 4).wait_recv()
            self.sent(index, 8).start()
            return
        self.by_pair(
            lambda: self.landed(index, 0).wait_recv(), lambda: self.landed(index, 3).wait_recv()
        )
        self.sent(index, 4).start()
        self.sent(index, 6).start()

    def close(self, index):
        if not self.units[index].flat:
            self.landed(index, 4).wait_recv()
            self.sent(index, 7).start()

    def finish(self, index):
        unit = self.units[index]
        for kind in (2, 5, 6, 7, 8) if unit.flat else (2, 5, 6, 7):
            self.landed(index, kind).wait_recv()
        if unit.flat:
            for kind in range(9):
                self.sent(index, kind).wait_send()
        else:
            self.by_pair(
                lambda: self.sent(index, 0).wait_send(), lambda: self.sent(index, 3).wait_send()
            )
            for kind in (1, 2, 4, 5, 6, 7):
                self.sent(index, kind).wait_send()
        if unit.last:
            self.local(unit.number).wait()


def column_partners(rank, depth):
    return [(rank, lax.rem(depth + step, DOCS)) for step in range(1, DOCS)]


def tile(index, size=256):
    return pl.ds(pl.multiple_of(index * size, size), size)


def each(count, body):
    def one(index, unused):
        body(index)
        return unused

    lax.fori_loop(0, count, one, 0)


def by_columns(left, right, write):
    def one(index):
        at = tile(index)
        write(at, product(left[...], right[:, at]))

    each(right.shape[1] // 256, one)


def store_as(target):
    def write(at, value):
        target[:, at] = value.astype(target.dtype)

    return write


def rms_rows(values, gain, normed):
    def one(index):
        at = tile(index, 32)
        v = values[at, :]
        root = lax.rsqrt(jnp.mean(v * v, axis=-1, keepdims=True) + epsilon)
        normed[at, :] = (v * root * gain).astype(jnp.bfloat16)

    each(values.shape[0] // 32, one)


def half_masks():
    lane = lax.broadcasted_iota(jnp.int32, (1, 2 * HD), 1)
    low = (lane < HD).astype(jnp.float32)
    return (low.astype(jnp.bfloat16), (1.0 - low).astype(jnp.bfloat16))


def causal_bias(smalls, spread, pair, half):
    row = smalls[tile(pair, 16), :][3:4]
    size = spread.shape[2]
    row = jnp.broadcast_to(row, (8, 128)).astype(jnp.bfloat16)
    line = product(row, spread[half])[0:1]
    bias = pltpu.roll(jnp.broadcast_to(line, (size, size)), 0, 1, stride=1, stride_axis=0)
    here = lax.broadcasted_iota(jnp.int32, (size, size), 0)
    there = lax.broadcasted_iota(jnp.int32, (size, size), 1)
    return jnp.where(there <= here, bias, masked_value)


def softmax_rows(scores):
    terms = jnp.exp(scores - jnp.max(scores, axis=-1, keepdims=True))
    return terms * (1.0 / jnp.sum(terms, axis=-1, keepdims=True))


def attend_heads(queries, keys, values, out, bias_of):
    masks = half_masks()

    def pair(index):
        at = tile(index, 2 * HD)
        q, k, v = queries[:, at], keys[:, at], values[:, at]
        total = jnp.zeros(q.shape, jnp.float32)
        for half in range(2):
            scores = product_right(q * masks[half], k)
            if bias_of is not None:
                scores = scores + bias_of(index, half)
            weights = softmax_rows(scores).astype(jnp.bfloat16)
            total = total + product(weights, v * masks[half])
        out[:, at] = total.astype(jnp.bfloat16)

    each(H // 2, pair)


def column_partners(rank, depth):
    return [(rank, lax.rem(depth + step, DOCS)) for step in range(1, DOCS)]


class Kept:
    inputs, normed, q, k, u, o1, after, normed2, cq = range(9)
    ck, cv, o2, after2, normed3, w, slope, gelu, cot = range(9, 18)
    normed_t, q_t, o1_t, normed2_t, cq_t, o2_t, normed3_t, states_t = range(18, 26)
    count = 26
    wide = (14, 15, 16)
    exact = (0, 6, 12, 15, 16)
    states = (9, 10)
    flipped = tuple(range(18, 26))
    inside = (1, 5, 7, 11, 13)


class Steps:
    lags = (0, 3, 5, 7, 8)

    def __init__(self, gather):
        self.gather, self.step, self.finished = gather, 0, 0

    def advance(self):
        gather, count = self.gather, len(self.gather.units)
        stages = (gather.issue, gather.relay, gather.spread, gather.close, gather.finish)
        for stage, lag in zip(stages, self.lags):
            if 0 <= self.step - lag < count:
                stage(self.step - lag)
        self.step += 1
        self.finished = min(max(0, self.step - self.lags[-1]), count)


def forward_kernel(count, units, *refs):
    owns, refs = refs[:count], refs[count:]
    (tokens, cotangent, chosen, encoded, spread), refs = refs[:5], refs[5:]
    fulls, refs = refs[:count], refs[count:]
    n = Kept.count
    outs, refs = refs[:n], refs[n:]
    grad_out, refs = refs[0], refs[1:]
    keep, refs = refs[:n], refs[n:]
    (
        grad_fd,
        smalls,
        gains,
        all_tokens,
        all_cotangent,
        square,
        wide,
        send_sems,
        recv_sems,
        local_sems,
        line_send,
        line_recv,
        line_local,
        load_sems,
        save_sems,
    ) = refs
    rank, core, along_x, along_y, depth = place()
    gather = Gather(units, owns, fulls, send_sems, recv_sems, local_sems)
    column = column_partners(rank, depth)
    greet([gather.to_x, gather.to_y, gather.to_core] + column)

    def line_copies(number):
        own, whole = ((tokens, all_tokens), (cotangent, all_cotangent))[number]
        rows = own.shape[0]
        at = whole.at[pl.ds(pl.multiple_of(depth * rows, rows), rows)]
        here = pltpu.make_async_copy(own, at, line_local.at[number])
        sends, receives = [], []
        for step, partner in enumerate(column):
            sems = (line_send.at[number, step], line_recv.at[number, step])
            sends.append(remote(own, at, sems[0], sems[1], partner))
            origin = lax.rem(depth + DOCS - 1 - step, DOCS)
            landing = whole.at[pl.ds(pl.multiple_of(origin * rows, rows), rows)]
            receives.append(remote(own, landing, sems[0], sems[1], partner))
        return (here, sends, receives)

    def line_finish(number):
        here, sends, receives = line_copies(number)
        here.wait()
        for copy in receives:
            copy.wait_recv()
        for copy in sends:
            copy.wait_send()

    steps = Steps(gather)
    advance = steps.advance
    lasts = [index for index, unit in enumerate(units) if unit.last]
    advance()
    for number in range(2):
        here, sends, unused = line_copies(number)
        here.start()
        for copy in sends:
            copy.start()

    def flip(source, name):
        turn(source, keep[name])
        save(name)

    def save(name):
        if name in Kept.inside:
            return
        pltpu.make_async_copy(keep[name], outs[name], save_sems.at[name]).start()

    def load(number):
        if number == 0:
            buffer = smalls
        else:
            buffer = (square if fulls[number].shape[1] == square.shape[2] else wide).at[number % 2]
        return (pltpu.make_async_copy(fulls[number], buffer, load_sems.at[number]), buffer)

    def loaded(number):
        copy, buffer = load(number)
        copy.wait()
        return buffer

    def project(left, number, name):
        by_columns(left, loaded(number), store_as(keep[name]))
        save(name)

    def residual(before, left, number, name, gain, normed, turned):
        weight = loaded(number)

        def write(at, value):
            keep[name][:, at] = keep[before][:, at] + value

        by_columns(keep[left], weight, write)
        save(name)
        rms_rows(keep[name], gains[gain : gain + 1, :], keep[normed])
        flip(keep[normed], turned)

    def start():
        loaded(0)
        for slot in range(8):
            gains[0:3, 128 * slot : 128 * slot + 128] = smalls[16 * slot : 16 * slot + 3, :]
        flip(encoded, Kept.states_t)

    def values_and_tokens():
        project(encoded, 2, Kept.cv)
        line_finish(0)
        by_columns(chosen, all_tokens, store_as(keep[Kept.inputs]))
        save(Kept.inputs)
        rms_rows(keep[Kept.inputs], gains[0:1, :], keep[Kept.normed])
        flip(keep[Kept.normed], Kept.normed_t)

    def keys():
        flip(keep[Kept.q], Kept.q_t)
        project(keep[Kept.normed], 4, Kept.k)

    def self_heads():
        project(keep[Kept.normed], 5, Kept.u)
        advance()
        attend_heads(
            keep[Kept.q], keep[Kept.k], keep[Kept.u], keep[Kept.o1], functools.partial(causal_bias, smalls, spread)
        )
        flip(keep[Kept.o1], Kept.o1_t)

    def cross_heads():
        project(keep[Kept.normed2], 7, Kept.cq)
        flip(keep[Kept.cq], Kept.cq_t)
        advance()
        attend_heads(keep[Kept.cq], keep[Kept.ck], keep[Kept.cv], keep[Kept.o2], None)
        flip(keep[Kept.o2], Kept.o2_t)
        line_finish(1)
        by_columns(chosen, all_cotangent, store_as(keep[Kept.cot]))
        save(Kept.cot)

    def gate():
        by_columns(keep[Kept.normed3], loaded(9), store_as(keep[Kept.slope]))

    def up():
        weight = loaded(10)
        scale = math.sqrt(2.0 / math.pi)

        def write(at, b):
            a = keep[Kept.slope][:, at]
            t = jnp.tanh(scale * (a + 0.044715 * (a * a * a)))
            gelu = 0.5 * a * (1.0 + t)
            slope = 0.5 * (1.0 + t) + 0.5 * a * (1.0 - t * t) * scale * (
                1.0 + 3 * 0.044715 * (a * a)
            )
            keep[Kept.gelu][:, at] = gelu
            keep[Kept.slope][:, at] = slope * b
            w = (gelu * b).astype(jnp.bfloat16)
            keep[Kept.w][:, at] = w
            grad = product_left(w, keep[Kept.cot][...]).astype(jnp.bfloat16)
            for part in range(grad_fd.shape[0]):
                grad_fd[part, at, :] = grad[:, 256 * part : 256 * part + 256]

        def one(index):
            at = tile(index)
            write(at, product(keep[Kept.normed3][...], weight[:, at]))

        tiles = weight.shape[1] // 256
        for part in range(0, tiles, 3):
            lax.fori_loop(part, min(part + 3, tiles), lambda index, unused: one(index), None)
            advance()
        for name in (Kept.gelu, Kept.slope, Kept.w):
            save(name)
        pltpu.make_async_copy(grad_fd, grad_out, save_sems.at[n]).start()

    compute = (
        start,
        lambda: project(encoded, 1, Kept.ck),
        values_and_tokens,
        lambda: project(keep[Kept.normed], 3, Kept.q),
        keys,
        self_heads,
        lambda: residual(Kept.inputs, Kept.o1, 6, Kept.after, 1, Kept.normed2, Kept.normed2_t),
        cross_heads,
        lambda: residual(Kept.after, Kept.o2, 8, Kept.after2, 2, Kept.normed3, Kept.normed3_t),
        gate,
        up,
    )
    for number in range(count - 1):
        while steps.finished <= lasts[number]:
            advance()
        load(number)[0].start()
        if number:
            compute[number - 1]()
    compute[count - 2]()
    while steps.finished < len(units):
        advance()
    for name in range(n):
        if name not in Kept.inside:
            pltpu.make_async_copy(keep[name], outs[name], save_sems.at[name]).wait()
    pltpu.make_async_copy(grad_fd, grad_out, save_sems.at[n]).wait()


def forward_call(shards, tokens, cotangent, chosen, encoded, spread):
    count = len(shards)
    vmem = pl.BlockSpec(memory_space=pltpu.VMEM)
    anywhere = pl.BlockSpec(memory_space=pl.ANY)
    most, total = chosen.shape
    shapes = [jax.ShapeDtypeStruct((8 * s.shape[0], s.shape[1]), s.dtype) for s in shards]
    saved = []
    for name in range(Kept.count):
        if name in Kept.flipped:
            rows = encoded.shape[0] if name == Kept.states_t else most
            saved.append(((shards[1].shape[1], rows), jnp.bfloat16))
            continue
        rows = encoded.shape[0] if name in Kept.states else most
        width = shards[9].shape[1] if name in Kept.wide else shards[1].shape[1]
        saved.append(((rows, width), jnp.float32 if name in Kept.exact else jnp.bfloat16))
    shapes += [jax.ShapeDtypeStruct(*s) for s in saved]
    down = shapes[count - 1]
    down = jax.ShapeDtypeStruct((down.shape[1] // 256, down.shape[0], 256), down.dtype)
    square = shards[1].shape[1]
    units = units_of([s.shape for s in shards], 3)
    return pl.pallas_call(
        functools.partial(forward_kernel, count, units),
        out_shape=shapes + [down],
        in_specs=[vmem] * (count + 5),
        out_specs=[anywhere] * (len(shapes) + 1),
        scratch_shapes=[pltpu.VMEM(*s) for s in saved]
        + [
            pltpu.VMEM(down.shape, down.dtype),
            pltpu.VMEM(shapes[0].shape, jnp.float32),
            pltpu.VMEM((8, square), jnp.float32),
            pltpu.VMEM((total, square), jnp.bfloat16),
            pltpu.VMEM((total, square), jnp.bfloat16),
            pltpu.VMEM((2, square, square), jnp.bfloat16),
            pltpu.VMEM((2, square, shards[9].shape[1]), jnp.bfloat16),
            pltpu.SemaphoreType.DMA((len(units), 9)),
            pltpu.SemaphoreType.DMA((len(units), 9)),
            pltpu.SemaphoreType.DMA((count,)),
            pltpu.SemaphoreType.DMA((2, DOCS - 1)),
            pltpu.SemaphoreType.DMA((2, DOCS - 1)),
            pltpu.SemaphoreType.DMA((2,)),
            pltpu.SemaphoreType.DMA((count,)),
            pltpu.SemaphoreType.DMA((len(saved) + 1,)),
        ],
        compiler_params=pltpu.CompilerParams(
            collective_id=1, has_side_effects=True, vmem_limit_bytes=60 * 2**20
        ),
        name="forward",
    )(*shards, tokens, cotangent, chosen, encoded, spread)


def add_rows(target, source):
    rows = target.shape[1]
    step = math.gcd(rows, 64)

    def one(index):
        at = pl.ds(pl.multiple_of(index * step, step), step)
        target[:, at, :] = target[:, at, :] + source[:, at, :]

    each(rows // step, one)


class Reduce:
    def __init__(self, pieces, buffers, load, send_sems, recv_sems, local_sems):
        rank, core, along_x, along_y, depth = place()
        self.pieces, self.buffers, self.load = pieces, buffers, load
        self.send_sems, self.recv_sems, self.local_sems = send_sems, recv_sems, local_sems
        self.core, self.along_x, self.along_y = core, along_x, along_y
        self.block = 2 * along_y + along_x
        self.to_x = (rank + 2 - 4 * along_x, depth)
        self.to_y = (rank + 4 - 8 * along_y, depth)
        self.to_core = (rank + 1 - 2 * core, depth)
        self.inner = (depth == 1) | (depth == 2)
        self.to_line = (rank, depth + 1 - 2 * lax.rem(depth, 2))
        self.to_middle = (rank, 3 - depth)
        self.partners = [self.to_x, self.to_y, self.to_core, self.to_line, self.to_middle]

    def copy(self, number, kind, source, target, device):
        return remote(
            source,
            target,
            self.send_sems.at[number, kind],
            self.recv_sems.at[number, kind],
            device,
        )

    def halves(self, number):
        size = self.pieces[number].rows // 2
        return (pl.ds(0, size), pl.ds(size, size))

    def core_copies(self, number):
        piece, both = self.pieces[number], self.buffers[number][0]
        return [
            self.copy(number, q, piece.slot(2 * q + 1 - self.core), both.at[q], self.to_core)
            for q in range(4)
        ]

    def own_load(self, number, q):
        return pltpu.make_async_copy(
            self.pieces[number].slot(2 * q + self.core),
            self.load[number].at[q % 2],
            self.local_sems.at[number, q],
        )

    def first_copies(self, number):
        both, from_x, from_y = self.buffers[number][:3]
        low, high = self.halves(number)
        copies = []
        for other in range(2):
            copies.append(
                self.copy(
                    number,
                    4 + other,
                    both.at[2 * other + 1 - self.along_x, :, low],
                    from_x.at[other],
                    self.to_x,
                )
            )
        for other in range(2):
            copies.append(
                self.copy(
                    number,
                    6 + other,
                    both.at[2 * (1 - self.along_y) + other, :, high],
                    from_y.at[other],
                    self.to_y,
                )
            )
        return copies

    def second_copies(self, number):
        both, unused_x, unused_y, late_x, late_y = self.buffers[number][:5]
        low, high = self.halves(number)
        return [
            self.copy(
                number,
                8,
                both.at[2 * (1 - self.along_y) + self.along_x, :, low],
                late_y,
                self.to_y,
            ),
            self.copy(
                number,
                9,
                both.at[2 * self.along_y + 1 - self.along_x, :, high],
                late_x,
                self.to_x,
            ),
        ]

    def line_copy(self, number):
        return self.copy(
            number,
            10,
            self.buffers[number][0].at[self.block],
            self.buffers[number][5],
            self.to_line,
        )

    def middle_copy(self, number):
        return self.copy(
            number,
            11,
            self.buffers[number][0].at[self.block],
            self.buffers[number][6],
            self.to_middle,
        )

    def return_copy(self, number):
        return self.copy(
            number,
            10,
            self.buffers[number][5],
            self.buffers[number][5],
            self.to_line,
        )

    def write(self, number):
        return pltpu.make_async_copy(
            self.buffers[number][5],
            self.pieces[number].out.at[self.pieces[number].tiles],
            self.local_sems.at[number, 4],
        )

    def stage(self, number, level):
        both, from_x, from_y, late_x, late_y, on_line, on_middle = self.buffers[number]
        low, high = self.halves(number)
        if level == 0:
            for copy in self.core_copies(number):
                copy.start()
            self.own_load(number, 0).start()
            self.own_load(number, 1).start()
        elif level == 1:
            for q, copy in enumerate(self.core_copies(number)):
                copy.wait_recv()
                self.own_load(number, q).wait()
                add_rows(both.at[q], self.load[number].at[q % 2])
                if q < 2:
                    self.own_load(number, q + 2).start()
            for copy in self.first_copies(number):
                copy.start()
        elif level == 2:
            copies = self.first_copies(number)
            for other in range(2):
                copies[other].wait_recv()
                copies[other].wait_send()
                add_rows(both.at[2 * other + self.along_x, :, low], from_x.at[other])
            for other in range(2):
                copies[2 + other].wait_recv()
                copies[2 + other].wait_send()
                add_rows(both.at[2 * self.along_y + other, :, high], from_y.at[other])
            for copy in self.second_copies(number):
                copy.start()
        elif level == 3:
            to_y, to_x = self.second_copies(number)
            to_y.wait_recv()
            add_rows(both.at[self.block, :, low], late_y)
            to_x.wait_recv()
            add_rows(both.at[self.block, :, high], late_x)
            to_y.wait_send()
            to_x.wait_send()

            @pl.when(jnp.logical_not(self.inner))
            def _():
                self.line_copy(number).start()
        elif level == 4:

            @pl.when(self.inner)
            def _():
                self.line_copy(number).wait_recv()
                add_rows(both.at[self.block], on_line)
                self.middle_copy(number).start()
        elif level == 5:

            @pl.when(self.inner)
            def _():
                middle = self.middle_copy(number)
                middle.wait_recv()
                rows = on_line.shape[1]
                step = math.gcd(rows, 64)

                def one(index):
                    at = pl.ds(pl.multiple_of(index * step, step), step)
                    on_line[:, at, :] = both[self.block, :, at, :] + on_middle[:, at, :]

                each(rows // step, one)
                middle.wait_send()
                self.return_copy(number).start()
        else:
            line = self.line_copy(number)

            @pl.when(jnp.logical_not(self.inner))
            def _():
                line.wait_send()
                line.wait_recv()

            @pl.when(self.inner)
            def _():
                self.return_copy(number).wait_send()

            for copy in self.core_copies(number):
                copy.wait_send()
            self.write(number).start()

    levels = 7


def buffer_shapes(tiles, rows, width, dtype):
    return [
        pltpu.VMEM((4, tiles, rows, width), dtype),
        pltpu.VMEM((2, tiles, rows // 2, width), dtype),
        pltpu.VMEM((2, tiles, rows // 2, width), dtype),
        pltpu.VMEM((tiles, rows // 2, width), dtype),
        pltpu.VMEM((tiles, rows // 2, width), dtype),
        pltpu.VMEM((tiles, rows, width), dtype),
        pltpu.VMEM((tiles, rows, width), dtype),
    ]


class Piece:
    def __init__(self, grad, out, start, tiles):
        self.grad, self.out = grad, out
        self.tiles = pl.ds(start, tiles)
        self.rows = grad.shape[2]

    def slot(self, index):
        return self.grad.at[self.tiles, index]


def pieces_of(shape):
    most = 1 if shape[2] > 256 else 4
    return [(start, min(most, shape[0] - start)) for start in range(0, shape[0], most)]


def piece_order(shapes):
    parts = [[(number,) + p for p in pieces_of(shape)] for number, shape in enumerate(shapes)]
    turns = [p for both in zip(parts[1], parts[2]) for p in both]
    return parts[0] + turns + [p for part in parts[3:] for p in part]


class Pipeline:
    gaps = (0, 1, 2, 2, 2, 2, 2)

    def __init__(self, reduce, count):
        self.reduce, self.count = reduce, count
        self.done, self.ready = [0] * reduce.levels, 0

    def tick(self):
        before = [self.ready] + list(self.done)
        for level, gap in enumerate(self.gaps):
            limit = before[level]
            if level and limit < self.count:
                limit = limit - gap + 1
            if self.done[level] < limit:
                self.reduce.stage(self.done[level], level)
                self.done[level] += 1

    def drain(self):
        while self.done[-1] < self.count:
            self.tick()


def rms_back(values, cotangent, gain, carry, out, gain_grad):
    def one(index):
        at = tile(index, 32)
        v, gz = values[at, :], cotangent[at, :]
        root = lax.rsqrt(jnp.mean(v * v, axis=-1, keepdims=True) + epsilon)
        scaled = gain * gz
        inner = jnp.mean(scaled * v, axis=-1, keepdims=True)
        gain_grad[...] += jnp.sum(gz * v * root, axis=0, keepdims=True)
        result = carry[at, :].astype(jnp.float32) + root * scaled - v * (root * root * root * inner)
        out[at, :] = result.astype(out.dtype)

    gain_grad[...] = jnp.zeros_like(gain_grad)
    each(values.shape[0] // 32, one)


def diagonal_sums(grad):
    size = grad.shape[1]
    total = grad[0:8]
    for group in range(1, grad.shape[0] // 8):
        part = grad[8 * group : 8 * group + 8]
        total = total + pltpu.roll(part, size - 8 * group, 1)
    row = lax.broadcasted_iota(jnp.int32, total.shape, 0)
    line = jnp.where(row == 0, total, 0.0)
    for step in range(1, 8):
        line = line + jnp.where(row == step, pltpu.roll(total, size - step, 1), 0.0)
    return jnp.sum(line, axis=0, keepdims=True)


def attend_back_heads(
    first, last, queries, flipped, keys, values, grad, grad_flipped, grad_q, grad_k, grad_v, bias_of, bias_grad
):
    masks = half_masks()
    row = lax.broadcasted_iota(jnp.int32, (2 * HD, 1), 0)
    low = (row < HD).astype(jnp.float32)
    sides = (low.astype(jnp.bfloat16), (1.0 - low).astype(jnp.bfloat16))

    def pair(index):
        at = tile(index + first, 2 * HD)
        q, k, v, g = queries[:, at], keys[:, at], values[:, at], grad[:, at]
        qt, gt = flipped[at, :], grad_flipped[at, :]
        total_q = jnp.zeros(q.shape, jnp.float32)
        total_k = jnp.zeros((2 * HD, k.shape[0]), jnp.float32)
        total_v = jnp.zeros((2 * HD, k.shape[0]), jnp.float32)
        for half in range(2):
            scores = product_right(q * masks[half], k)
            if bias_of is not None:
                scores = scores + bias_of(index + first, half)
            weights = softmax_rows(scores)
            grad_w = product_right(g * masks[half], v)
            inner = jnp.sum(weights * grad_w, axis=-1, keepdims=True)
            grad_s = weights * (grad_w - inner)
            if bias_grad is not None:
                bias_grad(index + first, half, grad_s)
            rounded = grad_s.astype(jnp.bfloat16)
            total_q = total_q + product(rounded, k * masks[half])
            total_k = total_k + product(qt * sides[half], rounded)
            total_v = total_v + product(gt * sides[half], weights.astype(jnp.bfloat16))
        grad_q[:, at] = total_q.astype(jnp.bfloat16)
        grad_k[at, :] = total_k.astype(jnp.bfloat16)
        grad_v[at, :] = total_v.astype(jnp.bfloat16)

    each(last - first, pair)


def turn(source, target):
    step = min(256, source.shape[0])

    def one(index):
        at = tile(index, step)
        target[:, at] = source[at, :].T

    each(source.shape[0] // step, one)


class Given:
    inputs, normed_t, q, q_t, k, u, o1_t, after, normed2_t = range(9)
    cq, cq_t, ck, cv, o2_t, after2, normed3_t, w, slope, gelu, cot = range(9, 20)
    states_t, chosen_t, spread, smalls = range(20, 24)
    w_ck, w_cv, w_sq, w_sk, w_sv, w_so, w_cq, w_co, w_fg, w_fu, w_fd = range(24, 35)
    grad_fd = 35
    count = 36


def backward_kernel(shared, *refs):
    given, refs = refs[: Given.count], refs[Given.count :]
    grads, refs = (given[Given.grad_fd],) + refs[:11], refs[11:]
    kept_states, refs = refs[0], refs[1:]
    outs, refs = refs[:12], refs[12:]
    (encoder_out, layer_out, hidden_out), refs = refs[:3], refs[3:]
    order = piece_order([g.shape for g in grads])
    pieces = [Piece(grads[n], outs[n], start, tiles) for n, start, tiles in order]
    count = len(pieces)
    buffers, refs = [refs[7 * i : 7 * i + 7] for i in range(count)], refs[7 * count :]
    loads = [refs[shared[i]] for i in range(count)]
    refs = refs[max(shared) + 1 :]
    (
        one_w,
        two_w,
        three_w,
        backs,
        stage,
        state_stage,
        grad_x,
        grad_n,
        value,
        other,
        cot,
        half_a,
        half_b,
        half_c,
        half_d,
        left,
        turned_q,
        turned_g,
        chosen_t,
        spread,
        smalls,
        gains,
        gain_grad,
        small_grads,
        landing,
        send_sems,
        recv_sems,
        local_sems,
        line_send,
        line_recv,
        load_sems,
        stage_sems,
        out_sems,
    ) = refs
    rank, core, along_x, along_y, depth = place()
    reduce = Reduce(pieces, buffers, loads, send_sems, recv_sems, local_sems)
    column = column_partners(rank, depth)
    greet([reduce.to_x, reduce.to_y, reduce.to_core] + column)
    pipeline = Pipeline(reduce, count)
    tick = pipeline.tick
    numbers = [n for n, unused_start, unused_tiles in order]
    pipeline.ready = numbers.count(0)
    turn_of = iter(range(1 << 20))

    def begin(*pairs):
        copies = []
        for source, target in pairs:
            sem = load_sems.at[next(turn_of) % load_sems.shape[0]]
            copies.append(pltpu.make_async_copy(source, target, sem))
            copies[-1].start()
        return copies

    def end(copies):
        for copy in copies:
            copy.wait()

    def staged(buffers_of, target_of, values, tiles):
        slots = buffers_of.shape[0]

        def copy(index):
            slot = lax.rem(index, slots)
            return pltpu.make_async_copy(buffers_of.at[slot], target_of(index), stage_sems.at[slot])

        def one(index):
            @pl.when(index >= slots)
            def _():
                copy(index - slots).wait()

            buffers_of[lax.rem(index, slots)] = values(tile(index))
            copy(index).start()

        each(tiles, one)
        for index in range(max(0, tiles - slots), tiles):
            copy(jnp.int32(index)).wait()

    def weight_grad(number, right, start=0):
        def values(at):
            result = product(left[...], right[:, at])
            return result.astype(jnp.bfloat16).reshape(stage.shape[1:])

        staged(stage, lambda index: grads[number].at[start + index], values, right.shape[1] // 256)
        pipeline.ready += 1

    def send_back(number, rows):
        def write(index):
            at = tile(index)
            result = product(chosen_t[...], rows[:, at]).astype(jnp.bfloat16)
            backs[number, :, :, at] = result.reshape(backs.shape[1:3] + (256,))

        each(rows.shape[1] // 256, write)
        for step, (unused, partner) in enumerate(column):
            back_copy(number, step, partner).start()

    def back_copy(number, step, partner):
        return remote(
            backs.at[number, partner],
            landing.at[number, step],
            line_send.at[number, step],
            line_recv.at[number, step],
            (rank, partner),
        )

    def receive_back(number, out):
        for step, (unused, partner) in enumerate(column):
            copy = back_copy(number, step, partner)
            copy.wait_recv()
            copy.wait_send()

        def one(index):
            at = tile(index, 32)
            total = backs[number, depth, at, :].astype(jnp.float32)
            for step in range(DOCS - 1):
                total = total + landing[number, step, at, :].astype(jnp.float32)
            out[at, :] = total.astype(jnp.bfloat16)

        each(out.shape[0] // 32, one)

    def norm_grad(values, gain, carry, out):
        rms_back(values, grad_n, gains[gain : gain + 1, :], carry, out, gain_grad)
        for slot in range(8):
            small_grads[0, slot, gain : gain + 1, :] = gain_grad[:, 128 * slot : 128 * slot + 128]

    def round_rows(source, target):
        def one(index):
            at = tile(index, 32)
            target[at, :] = source[at, :].astype(jnp.bfloat16)

        each(source.shape[0] // 32, one)

    def through(right_rows, weights, write):
        def one(index):
            at = tile(index)
            write(at, product_right(right_rows[...], weights[at, :]))

        each(weights.shape[0] // 256, one)

    def head_grads(weights):
        through(half_a, weights, store_as(half_b))

        def one(index):
            at = tile(index)
            turned_g[at, :] = product_right(weights[at, :], half_a[...]).astype(jnp.bfloat16)

        each(weights.shape[0] // 256, one)

    def feed_loads(start, tiles):
        at = pl.ds(256 * start, 256 * tiles)
        width = 256 * tiles
        return begin(
            (given[Given.w_fd].at[at], one_w.at[0:width]),
            (given[Given.slope].at[:, at], value.at[:, 0:width]),
            (given[Given.gelu].at[:, at], other.at[:, 0:width]),
            (given[Given.w].at[:, at], half_a.at[:, 0:width]),
            (given[Given.w_fg].at[:, at], two_w.at[:, 0:width]),
            (given[Given.w_fu].at[:, at], three_w.at[:, 0:width]),
        )

    tick()
    first = begin(
        (given[Given.cot], cot),
        (given[Given.smalls], smalls),
        (given[Given.chosen_t], chosen_t),
        (given[Given.spread], spread),
        (given[Given.normed3_t], left),
    )
    feeds = pieces_of(grads[1].shape)
    loaded = feed_loads(*feeds[0])
    tick()
    end(first)
    for slot in range(8):
        gains[0:3, 128 * slot : 128 * slot + 128] = smalls[16 * slot : 16 * slot + 3, :]
    small_grads[...] = jnp.zeros_like(small_grads)
    for turn_number, (start, tiles) in enumerate(feeds):
        width = 256 * tiles
        down, gate, up = one_w.at[0:width], two_w.at[:, 0:width], three_w.at[:, 0:width]
        part = half_a.at[:, 0:width]
        slope, gelu = value.at[:, 0:width], other.at[:, 0:width]
        gate_grad, up_grad = half_b.at[:, 0:width], half_c.at[:, 0:width]
        end(loaded)

        def split(at, grad_w):
            gate_grad[:, at] = (grad_w * slope[:, at]).astype(jnp.bfloat16)
            up_grad[:, at] = (grad_w * gelu[:, at]).astype(jnp.bfloat16)

        through(cot, down, split)

        def add(index):
            at = tile(index)
            forward = product(part[...], down[:, at])
            back = product_right(gate_grad[...], gate[at, :]) + product_right(up_grad[...], up[at, :])
            if start:
                forward, back = forward + grad_x[:, at], back + grad_n[:, at]
            grad_x[:, at] = forward
            grad_n[:, at] = back

        each(grad_x.shape[1] // 256, add)
        if turn_number + 1 < len(feeds):
            loaded = feed_loads(*feeds[turn_number + 1])
        else:
            loaded = begin(
                (given[Given.after2], value),
                (given[Given.w_co], one_w),
                (given[Given.cq_t], turned_q),
                (given[Given.ck], two_w.at[0:512]),
                (given[Given.cv], two_w.at[512:1024]),
            )
        tick()
        weight_grad(1, gate_grad, start)
        weight_grad(2, up_grad, start)
        tick()

    loaded += begin((given[Given.o2_t], left), (given[Given.cq], half_c))
    end(loaded)

    def last(index):
        at = tile(index, 32)
        half_a[at, :] = (value[at, :] + grad_x[at, :]).astype(jnp.bfloat16)

    each(value.shape[0] // 32, last)
    send_back(0, half_a)
    norm_grad(value, 2, cot, grad_x)
    round_rows(grad_x, half_a)
    tick()
    weight_grad(3, half_a)
    head_grads(one_w)
    tick()
    keys_grad, values_grad = three_w.at[:, 0:512], three_w.at[:, 512:1024]
    states = one_w.at[:, 0:512]
    loaded = begin(
        (given[Given.states_t], states), (given[Given.normed2_t], left), (given[Given.after], value)
    )

    def cross(first, last):
        attend_back_heads(
            first,
            last,
            half_c,
            turned_q,
            two_w.at[0:512],
            two_w.at[512:1024],
            half_b,
            turned_g,
            half_d,
            keys_grad,
            values_grad,
            None,
            None,
        )

    cross(0, 3)
    tick()
    cross(3, 6)
    tick()
    cross(6, 8)
    end(loaded)

    def state_grad(number, right):
        def values(at):
            result = product_right(states[...], right[at, :])
            return result.astype(jnp.bfloat16).reshape(stage.shape[1:])

        staged(stage, lambda index: grads[number].at[index], values, 4)
        pipeline.ready += 1

    state_grad(4, keys_grad)
    state_grad(5, values_grad)
    tick()
    turn(keys_grad, two_w.at[0:512])
    turn(values_grad, two_w.at[512:1024])
    kept = pltpu.make_async_copy(two_w, kept_states, out_sems.at[0])
    kept.start()
    loaded = begin(
        (given[Given.w_cq], one_w),
        (given[Given.w_so], three_w),
        (given[Given.q], half_c),
        (given[Given.q_t], turned_q),
    )
    weight_grad(6, half_d)
    kept.wait()
    end(loaded)
    loaded = begin((given[Given.k], two_w.at[0:256]), (given[Given.u], two_w.at[256:512]))
    through(half_d, one_w, store_as(grad_n))
    loaded += begin((given[Given.o1_t], left))
    norm_grad(value, 1, grad_x, grad_x)
    round_rows(grad_x, half_a)
    end(loaded)
    loaded = begin((given[Given.inputs], value), (given[Given.w_sq], one_w))
    tick()
    weight_grad(7, half_a)
    head_grads(three_w)
    loaded += begin((given[Given.normed_t], left))
    tick()

    def table_grad(index, half, grad_s):
        line = jnp.broadcast_to(diagonal_sums(grad_s), (8, grad_s.shape[1]))
        table = lax.dot_general(
            line,
            spread[half].astype(jnp.float32),
            (((1,), (1,)), ((), ())),
            precision=highest,
            preferred_element_type=jnp.float32,
        )
        small_grads[0, index, 3:4, :] = small_grads[0, index, 3:4, :] + table[0:1]

    keys_grad, values_grad = three_w.at[:, 0:256], three_w.at[:, 256:512]

    def own(first, last):
        attend_back_heads(
            first,
            last,
            half_c,
            turned_q,
            two_w.at[0:256],
            two_w.at[256:512],
            half_b,
            turned_g,
            half_d,
            keys_grad,
            values_grad,
            functools.partial(causal_bias, smalls, spread),
            table_grad,
        )

    own(0, 4)
    tick()
    own(4, 8)
    turn(keys_grad, half_a)
    turn(values_grad, half_b)
    end(loaded)
    loaded = begin((given[Given.w_sk], two_w), (given[Given.w_sv], three_w))
    tick()
    weight_grad(8, half_d)
    weight_grad(9, half_a)
    weight_grad(10, half_b)
    tick()
    end(loaded)

    def sum_three(index):
        at = tile(index)
        grad_n[:, at] = (
            product_right(half_d[...], one_w[at, :])
            + product_right(half_a[...], two_w[at, :])
            + product_right(half_b[...], three_w[at, :])
        )

    each(grad_n.shape[1] // 256, sum_three)
    loaded = begin((given[Given.w_ck], one_w), (given[Given.w_cv], three_w), (kept_states, two_w))
    norm_grad(value, 0, grad_x, half_c)
    small_copy = pltpu.make_async_copy(small_grads, grads[11], out_sems.at[1])
    small_copy.start()
    small_copy.wait()
    pipeline.ready += 1
    tick()
    send_back(1, half_c)
    tick()
    end(loaded)
    staged(
        state_stage,
        lambda index: encoder_out.at[:, tile(index)],
        lambda at: product_right(two_w[0:512], one_w[at, :])
        + product_right(two_w[512:1024], three_w[at, :]),
        4,
    )
    receive_back(0, layer_out)
    pipeline.drain()
    receive_back(1, hidden_out)
    for number in range(count):
        reduce.write(number).wait()


def backward_call(operands, rows):
    count = Given.count
    anywhere = pl.BlockSpec(memory_space=pl.ANY)
    vmem = pl.BlockSpec(memory_space=pltpu.VMEM)
    bf16, f32 = jnp.bfloat16, jnp.float32
    grad_fd = operands[Given.grad_fd]
    width, wide = operands[Given.w_fg].shape
    square = jax.ShapeDtypeStruct((width // 256, 8, width // 8, 256), bf16)
    broad = jax.ShapeDtypeStruct((wide // 256, 8, width // 8, 256), bf16)
    small = jax.ShapeDtypeStruct((1, 8, 16, 128), f32)
    full = [jax.ShapeDtypeStruct(grad_fd.shape, grad_fd.dtype), broad, broad] + [square] * 8 + [small]
    outs = [jax.ShapeDtypeStruct(g.shape[:1] + g.shape[2:], g.dtype) for g in full]
    most = operands[Given.inputs].shape[0]
    states = operands[Given.ck].shape[0]
    total = operands[Given.chosen_t].shape[0]
    kept_states = jax.ShapeDtypeStruct((2 * states, width), bf16)
    tail = [
        jax.ShapeDtypeStruct((states, width), f32),
        jax.ShapeDtypeStruct((rows, width), bf16),
        jax.ShapeDtypeStruct((rows, width), bf16),
    ]
    scratch, load_shapes, shared = [], [], []
    order = piece_order([g.shape for g in full])
    for number, unused, tiles in order:
        shape = (tiles,) + full[number].shape[2:]
        scratch += buffer_shapes(*shape, full[number].dtype)
        key = ((2,) + shape, full[number].dtype)
        held = [i for i, s in enumerate(load_shapes) if s == key]
        if len(held) < 2:
            shared.append(len(load_shapes))
            load_shapes.append(key)
        else:
            last = [i for i in shared if i in held][-1]
            shared.append(held[0] if last == held[1] else held[1])
    scratch += [pltpu.VMEM(*s) for s in load_shapes]
    pieces = len(order)
    scratch += [pltpu.VMEM((width, width), bf16)] * 3
    scratch += [
        pltpu.VMEM((2, DOCS, total // DOCS, width), bf16),
        pltpu.VMEM((3, 8, width // 8, 256), bf16),
        pltpu.VMEM((2, states, 256), f32),
    ]
    scratch += [pltpu.VMEM((most, width), f32)] * 4
    scratch += [pltpu.VMEM((most, width), bf16)] * 5
    scratch += [pltpu.VMEM((width, most), bf16)] * 3
    scratch += [
        pltpu.VMEM((total, most), bf16),
        pltpu.VMEM((2, 128, most), bf16),
        pltpu.VMEM((128, 128), f32),
        pltpu.VMEM((8, width), f32),
        pltpu.VMEM((1, width), f32),
        pltpu.VMEM((1, 8, 16, 128), f32),
        pltpu.VMEM((2, DOCS - 1, rows, width), bf16),
        pltpu.SemaphoreType.DMA((pieces, 12)),
        pltpu.SemaphoreType.DMA((pieces, 12)),
        pltpu.SemaphoreType.DMA((pieces, 5)),
        pltpu.SemaphoreType.DMA((2, DOCS - 1)),
        pltpu.SemaphoreType.DMA((2, DOCS - 1)),
        pltpu.SemaphoreType.DMA((16,)),
        pltpu.SemaphoreType.DMA((3,)),
        pltpu.SemaphoreType.DMA((2,)),
    ]
    results = pl.pallas_call(
        functools.partial(backward_kernel, shared),
        out_shape=full[1:] + [kept_states] + outs + tail,
        in_specs=[anywhere] * count,
        out_specs=[anywhere] * (len(full) + len(outs) + 1) + [vmem] * 2,
        scratch_shapes=scratch,
        compiler_params=pltpu.CompilerParams(
            collective_id=2, has_side_effects=True, vmem_limit_bytes=67043328
        ),
        name="backward",
    )(*operands)
    return results[len(full) :]


def widen_kernel(*refs):
    half = (len(refs) - 5) // 2
    smalls, lines = refs[half], refs[-4:]
    for index, line in enumerate(lines):
        line[...] = smalls[0, index : index + 1, 0 : line.shape[0]].reshape(line.shape)
    for source, target in zip(refs[:half], refs[half + 1 : -4]):
        if len(source.shape) == 2:
            target[...] = source[...].astype(target.dtype)
            continue
        for part in range(source.shape[0]):
            target[:, 256 * part : 256 * part + 256] = source[part].astype(target.dtype)


def widen_call(sums, layer_out, hidden_grad, smalls, entries):
    operands = list(sums) + [layer_out, hidden_grad, smalls]
    shapes = [jax.ShapeDtypeStruct((s.shape[1], s.shape[0] * s.shape[2]), jnp.float32) for s in sums]
    shapes.append(jax.ShapeDtypeStruct(layer_out.shape, layer_out.dtype))
    shapes.append(jax.ShapeDtypeStruct(hidden_grad.shape, jnp.float32))
    shapes += [jax.ShapeDtypeStruct((size,), jnp.float32) for size in (smalls.shape[2],) * 3 + (entries,)]
    vmem = pl.BlockSpec(memory_space=pltpu.VMEM)
    return pl.pallas_call(
        widen_kernel,
        out_shape=shapes,
        in_specs=[vmem] * len(operands),
        out_specs=[vmem] * len(shapes),
        name="widen",
    )(*operands)


def prepare_kernel(rows, norms, table, segments, docs, small, chosen, chosen_t, spread):
    small[...] = jnp.zeros_like(small)
    for index, norm in enumerate(norms):
        small[index : index + 1, :] = norm[...].reshape(1, norm.shape[0]).astype(jnp.float32)
    entries = table.shape[0]
    small[3:4, 0:entries] = table[...].reshape(1, entries).astype(jnp.float32)
    first = pl.multiple_of(lax.axis_index("ctx") * rows, rows)
    document = docs[:, pl.ds(first, 128)][:, 0:1]
    ids = segments[...]
    start = jnp.sum((ids < document).astype(jnp.int32), axis=1, keepdims=True)
    length = jnp.sum((ids == document).astype(jnp.int32), axis=1, keepdims=True)
    for target, axis in ((chosen, 0), (chosen_t, 1)):
        row = lax.broadcasted_iota(jnp.int32, target.shape, axis)
        column = lax.broadcasted_iota(jnp.int32, target.shape, 1 - axis)
        here = jnp.where(row < length, row + start, -1)
        target[...] = (here == column).astype(jnp.float32).astype(jnp.bfloat16)
    most = spread.shape[2]
    position = lax.broadcasted_iota(jnp.int32, (1, most), 1)
    bucket = bucket_of(jnp.where(position == 0, 0, most - position))
    slot = lax.broadcasted_iota(jnp.int32, spread.shape[1:], 0)
    for half in range(2):
        found = (slot == bucket + BUCKETS * half).astype(jnp.float32)
        spread[half] = found.astype(jnp.bfloat16)


def prepare_call(norms, table, segment_ids, encoder_docs, rows):
    total = segment_ids.shape[1]
    most = total // 2
    count = len(norms)

    def kernel(*refs):
        prepare_kernel(rows, refs[:count], *refs[count:])

    vmem = pl.BlockSpec(memory_space=pltpu.VMEM)
    return pl.pallas_call(
        kernel,
        out_shape=[
            jax.ShapeDtypeStruct((16, norms[0].shape[0]), jnp.float32),
            jax.ShapeDtypeStruct((most, total), jnp.bfloat16),
            jax.ShapeDtypeStruct((total, most), jnp.bfloat16),
            jax.ShapeDtypeStruct((2, 2 * HD, most), jnp.bfloat16),
        ],
        in_specs=[vmem] * (count + 3),
        out_specs=[vmem] * 4,
        name="prepare",
    )(*norms, table, segment_ids, encoder_docs)


def by_document(
    hidden_in,
    encoder_states,
    segment_ids,
    encoder_docs,
    self_query,
    self_key,
    self_value,
    self_out,
    cross_query,
    cross_key,
    cross_value,
    cross_out,
    feed_gate,
    feed_up,
    feed_down,
    norm_self,
    norm_cross,
    norm_feed,
    bias_table,
    out_grad,
):
    width = hidden_in.shape[2]
    encoded = encoder_states[0]
    small, chosen, chosen_t, spread = prepare_call(
        (norm_self, norm_cross, norm_feed), bias_table, segment_ids, encoder_docs, encoded.shape[0]
    )
    results = forward_call(
        (
            small,
            cross_key,
            cross_value,
            self_query,
            self_key,
            self_value,
            self_out,
            cross_query,
            cross_out,
            feed_gate,
            feed_up,
            feed_down,
        ),
        hidden_in[0],
        out_grad[0],
        chosen,
        encoded,
        spread,
    )
    kept = results[12:]
    grad_fd = results[-1].reshape(width // 256, 8, -1, 256)
    forward_side = [
        kept[i]
        for i in (
            Kept.inputs,
            Kept.normed_t,
            Kept.q,
            Kept.q_t,
            Kept.k,
            Kept.u,
            Kept.o1_t,
            Kept.after,
            Kept.normed2_t,
            Kept.cq,
            Kept.cq_t,
            Kept.ck,
            Kept.cv,
            Kept.o2_t,
            Kept.after2,
            Kept.normed3_t,
            Kept.w,
            Kept.slope,
            Kept.gelu,
            Kept.cot,
            Kept.states_t,
        )
    ]
    results = backward_call(
        forward_side + [chosen_t, spread] + list(results[:12]) + [grad_fd], hidden_in.shape[1]
    )
    smalls, encoder_grad, layer_out, hidden_grad = results[11:]
    fd, fg, fu, co, ck, cv, cq, so, sq, sk, sv, layer_out, hidden_grad, *lines = widen_call(
        results[:11], layer_out, hidden_grad, smalls, bias_table.shape[0]
    )
    return (
        layer_out[None],
        hidden_grad[None],
        encoder_grad[None],
        sq,
        sk,
        sv,
        so,
        cq,
        ck,
        cv,
        co,
        fg,
        fu,
        fd,
        *lines,
    )


def layer(sizes, *args):
    encoder_states, encoder_docs = args[1], args[3]
    whole_document = encoder_states.shape[1] * DOCS == encoder_docs.shape[1]
    if whole_document and sizes["fsdp"] == 8 and sizes["ctx"] == DOCS:
        return by_document(*args)
    return on_device(*args)


def solution(mesh):
    in_specs = (
        P("fsdp", "ctx", None),
        P("fsdp", "ctx", None),
        P("fsdp", None),
        P("fsdp", None),
        P("fsdp", None),
        P("fsdp", None),
        P("fsdp", None),
        P("fsdp", None),
        P("fsdp", None),
        P("fsdp", None),
        P("fsdp", None),
        P("fsdp", None),
        P("fsdp", None),
        P("fsdp", None),
        P("fsdp", None),
        P("fsdp"),
        P("fsdp"),
        P("fsdp"),
        P("fsdp"),
        P("fsdp", "ctx", None),
    )
    out_specs = (
        P("fsdp", "ctx", None),
        P("fsdp", "ctx", None),
        P("fsdp", "ctx", None),
        P("fsdp", None),
        P("fsdp", None),
        P("fsdp", None),
        P("fsdp", None),
        P("fsdp", None),
        P("fsdp", None),
        P("fsdp", None),
        P("fsdp", None),
        P("fsdp", None),
        P("fsdp", None),
        P("fsdp", None),
        P("fsdp"),
        P("fsdp"),
        P("fsdp"),
        P("fsdp"),
    )
    return jax.shard_map(
        functools.partial(layer, dict(mesh.shape)), mesh=mesh, in_specs=in_specs, out_specs=out_specs, check_vma=False
    )
```

```python
import functools
import math

import jax
import jax.numpy as jnp
from jax import lax
from jax.experimental import pallas as pl
from jax.experimental.pallas import tpu as pltpu
from jax.sharding import PartitionSpec as P

H = 16
HD = 64
BUCKETS = 32
DOCS = 4
MESH = pl.DeviceIdType.MESH


bucket_edges = (19, 21, 24, 27, 31, 35, 40, 46, 52, 59, 67, 77, 87, 99, 113)
epsilon = 1e-06
masked_value = -1e30
highest = lax.Precision.HIGHEST


def normalize(values, gain_vector):
    inverse_root = lax.rsqrt(jnp.mean(values * values, axis=-1, keepdims=True) + epsilon)
    return values * inverse_root * gain_vector


def norm_back(values, gain_vector, grad_normed):
    unused, pullback = jax.vjp(normalize, values, gain_vector)
    return pullback(grad_normed)


def product(left_side, right_side):
    return jnp.dot(left_side, right_side, preferred_element_type=jnp.float32)


def product_left(left_side, right_side):
    return lax.dot_general(
        left_side, right_side, (((0,), (0,)), ((), ())), preferred_element_type=jnp.float32
    )


def product_right(left_side, right_side):
    return lax.dot_general(
        left_side, right_side, (((1,), (1,)), ((), ())), preferred_element_type=jnp.float32
    )


def bucket_of(distance):
    bucket_index = jnp.minimum(distance, 16)
    for threshold in bucket_edges:
        bucket_index = bucket_index + (distance >= threshold).astype(jnp.int32)
    return bucket_index


def bucket_onehot(distance):
    return (bucket_of(distance)[:, :, None] == jnp.arange(BUCKETS, dtype=jnp.int32)).astype(jnp.bfloat16)


def split_blocks(rows_all):
    total_rows = rows_all.shape[0]
    block_rows = math.gcd(total_rows, 512)
    return (block_rows, rows_all.reshape(total_rows // block_rows, block_rows, H, HD))


def block_logits(query_heads, key_part, allowed, distance, table_rows):
    scores = jnp.einsum("qhd,khd->hqk", query_heads, key_part, preferred_element_type=jnp.float32)
    onehot = None
    if table_rows is not None:
        onehot = bucket_onehot(distance)
        scores = scores + jnp.einsum(
            "qkb,hb->hqk", onehot, table_rows, preferred_element_type=jnp.float32
        )
    return (jnp.where(allowed[None], scores, masked_value), onehot)


def attention_forward(query_heads, key_rows, value_rows, mask_of, table_rows):
    block_rows, key_blocks = split_blocks(key_rows)
    unused, value_blocks = split_blocks(value_rows)
    numbers = jnp.arange(key_blocks.shape[0], dtype=jnp.int32)
    query_count = query_heads.shape[0]

    def total_step(carried, element):
        number, key_part = element
        allowed, distance = mask_of(number, block_rows)

        def total_live_branch(state):
            running, summed = state
            scores, unused_hot = block_logits(query_heads, key_part, allowed, distance, table_rows)
            newest = jnp.maximum(running, jnp.max(scores, axis=-1))
            exp_terms = jnp.where(allowed[None], jnp.exp(scores - newest[..., None]), 0.0)
            return (newest, summed * jnp.exp(running - newest) + jnp.sum(exp_terms, axis=-1))

        return (lax.cond(jnp.any(allowed), total_live_branch, lambda state: state, carried), None)

    start_state = (
        jnp.full((H, query_count), masked_value, jnp.float32),
        jnp.zeros((H, query_count), jnp.float32),
    )
    (running, summed), unused_out = lax.scan(total_step, start_state, (numbers, key_blocks))
    logsum = running + jnp.log(summed)

    def output_step(carried, element):
        number, key_part, value_part = element
        allowed, distance = mask_of(number, block_rows)

        def output_live_branch(state):
            scores, unused_hot = block_logits(query_heads, key_part, allowed, distance, table_rows)
            weights = jnp.where(allowed[None], jnp.exp(scores - logsum[..., None]), 0.0).astype(
                jnp.bfloat16
            )
            return state + jnp.einsum(
                "hqk,khd->qhd", weights, value_part, preferred_element_type=jnp.float32
            )

        return (lax.cond(jnp.any(allowed), output_live_branch, lambda state: state, carried), None)

    output, unused_out = lax.scan(
        output_step,
        jnp.zeros((query_count, H, HD), jnp.float32),
        (numbers, key_blocks, value_blocks),
    )
    return (output, logsum)


def attention_delta(query_heads, key_rows, value_rows, grad_heads, logsum, mask_of, table_rows):
    block_rows, key_blocks = split_blocks(key_rows)
    unused, value_blocks = split_blocks(value_rows)
    numbers = jnp.arange(key_blocks.shape[0], dtype=jnp.int32)
    query_count = query_heads.shape[0]

    def delta_step(carried, element):
        number, key_part, value_part = element
        allowed, distance = mask_of(number, block_rows)

        def delta_live_branch(state):
            scores, unused_hot = block_logits(query_heads, key_part, allowed, distance, table_rows)
            weights = jnp.where(allowed[None], jnp.exp(scores - logsum[..., None]), 0.0)
            grad_weights = jnp.einsum(
                "qhd,khd->hqk", grad_heads, value_part, preferred_element_type=jnp.float32
            )
            return state + jnp.sum(weights * grad_weights, axis=-1)

        return (lax.cond(jnp.any(allowed), delta_live_branch, lambda state: state, carried), None)

    row_delta, unused_out = lax.scan(
        delta_step, jnp.zeros((H, query_count), jnp.float32), (numbers, key_blocks, value_blocks)
    )
    return row_delta


def attention_backward(
    query_heads, key_rows, value_rows, grad_heads, logsum, row_delta, mask_of, table_rows
):
    block_rows, key_blocks = split_blocks(key_rows)
    unused, value_blocks = split_blocks(value_rows)
    numbers = jnp.arange(key_blocks.shape[0], dtype=jnp.int32)
    query_count = query_heads.shape[0]
    part_shape = (block_rows, H, HD)

    def grad_step(carried, element):
        number, key_part, value_part = element
        allowed, distance = mask_of(number, block_rows)

        def grad_live_branch(state):
            grad_query, grad_table = state
            scores, onehot = block_logits(query_heads, key_part, allowed, distance, table_rows)
            weights = jnp.where(allowed[None], jnp.exp(scores - logsum[..., None]), 0.0)
            grad_weights = jnp.einsum(
                "qhd,khd->hqk", grad_heads, value_part, preferred_element_type=jnp.float32
            )
            grad_scores = weights * (grad_weights - row_delta[..., None])
            rounded = grad_scores.astype(jnp.bfloat16)
            grad_query = grad_query + jnp.einsum(
                "hqk,khd->qhd", rounded, key_part, preferred_element_type=jnp.float32
            )
            if table_rows is not None:
                grad_table = grad_table + jnp.einsum(
                    "hqk,qkb->hb", grad_scores, onehot.astype(jnp.float32), precision=highest
                )
            grad_key_part = jnp.einsum(
                "hqk,qhd->khd", rounded, query_heads, preferred_element_type=jnp.float32
            )
            grad_value_part = jnp.einsum(
                "hqk,qhd->khd",
                weights.astype(jnp.bfloat16),
                grad_heads,
                preferred_element_type=jnp.float32,
            )
            return ((grad_query, grad_table), (grad_key_part, grad_value_part))

        def dead_branch(state):
            return (state, (jnp.zeros(part_shape, jnp.float32), jnp.zeros(part_shape, jnp.float32)))

        return lax.cond(jnp.any(allowed), grad_live_branch, dead_branch, carried)

    table_shape = (H, BUCKETS) if table_rows is not None else (1, 1)
    start_state = (
        jnp.zeros((query_count, H, HD), jnp.float32),
        jnp.zeros(table_shape, jnp.float32),
    )
    (grad_query, grad_table), key_parts = lax.scan(
        grad_step, start_state, (numbers, key_blocks, value_blocks)
    )
    total_rows = key_rows.shape[0]
    return (
        grad_query,
        grad_table,
        key_parts[0].reshape(total_rows, H * HD),
        key_parts[1].reshape(total_rows, H * HD),
    )


def on_device(
    hidden_in,
    encoder_states,
    segment_ids,
    encoder_docs,
    self_query,
    self_key,
    self_value,
    self_out,
    cross_query,
    cross_key,
    cross_value,
    cross_out,
    feed_gate,
    feed_up,
    feed_down,
    norm_self,
    norm_cross,
    norm_feed,
    bias_table,
    out_grad,
):
    gathered = (
        lax.all_gather(self_query, "fsdp", axis=0, tiled=True),
        lax.all_gather(self_key, "fsdp", axis=0, tiled=True),
        lax.all_gather(self_value, "fsdp", axis=0, tiled=True),
        lax.all_gather(self_out, "fsdp", axis=0, tiled=True),
        lax.all_gather(cross_query, "fsdp", axis=0, tiled=True),
        lax.all_gather(cross_key, "fsdp", axis=0, tiled=True),
        lax.all_gather(cross_value, "fsdp", axis=0, tiled=True),
        lax.all_gather(cross_out, "fsdp", axis=0, tiled=True),
        lax.all_gather(feed_gate, "fsdp", axis=0, tiled=True),
        lax.all_gather(feed_up, "fsdp", axis=0, tiled=True),
        lax.all_gather(feed_down, "fsdp", axis=0, tiled=True),
        lax.all_gather(norm_self, "fsdp", axis=0, tiled=True),
        lax.all_gather(norm_cross, "fsdp", axis=0, tiled=True),
        lax.all_gather(norm_feed, "fsdp", axis=0, tiled=True),
        lax.all_gather(bias_table, "fsdp", axis=0, tiled=True),
    )
    tokens = hidden_in[0]
    encoded = encoder_states[0]
    segments = segment_ids[0]
    documents = encoder_docs[0]
    tok_rows = tokens.shape[0]
    first_row = lax.axis_index("ctx") * tok_rows
    query_pos = first_row + jnp.arange(tok_rows, dtype=jnp.int32)
    query_seg = lax.dynamic_slice_in_dim(segments, first_row, tok_rows, 0)

    def self_mask(number, block_rows):
        key_pos = number * block_rows + jnp.arange(block_rows, dtype=jnp.int32)
        key_seg = lax.dynamic_slice_in_dim(segments, number * block_rows, block_rows, 0)
        distance = query_pos[:, None] - key_pos[None, :]
        allowed = (distance >= 0) & (query_seg[:, None] == key_seg[None, :])
        return (allowed, jnp.maximum(distance, 0))

    def cross_mask(number, block_rows):
        key_doc = lax.dynamic_slice_in_dim(documents, number * block_rows, block_rows, 0)
        return (query_seg[:, None] == key_doc[None, :], None)

    inputs = tokens.astype(jnp.float32)
    self_normed = normalize(inputs, gathered[11].astype(jnp.float32)).astype(jnp.bfloat16)
    queries = product(self_normed, gathered[0]).astype(jnp.bfloat16)
    key_local = product(self_normed, gathered[1]).astype(jnp.bfloat16)
    value_local = product(self_normed, gathered[2]).astype(jnp.bfloat16)
    key_rows, value_rows = (
        lax.all_gather(key_local, "ctx", axis=0, tiled=True),
        lax.all_gather(value_local, "ctx", axis=0, tiled=True),
    )
    table_rows = gathered[14].reshape(H, BUCKETS)
    query_heads = queries.reshape(tok_rows, H, HD)
    key_heads = key_rows.reshape(-1, H, HD)
    value_heads = value_rows.reshape(-1, H, HD)
    self_heads, self_logsum = attention_forward(
        query_heads, key_heads, value_heads, self_mask, table_rows
    )
    self_attended = self_heads.reshape(tok_rows, H * HD).astype(jnp.bfloat16)
    after_self = inputs + product(self_attended, gathered[3])
    cross_normed = normalize(after_self, gathered[12].astype(jnp.float32)).astype(jnp.bfloat16)
    cross_queries = product(cross_normed, gathered[4]).astype(jnp.bfloat16)
    cross_key_local = product(encoded, gathered[5]).astype(jnp.bfloat16)
    cross_value_local = product(encoded, gathered[6]).astype(jnp.bfloat16)
    cross_keys, cross_values = (
        lax.all_gather(cross_key_local, "ctx", axis=0, tiled=True),
        lax.all_gather(cross_value_local, "ctx", axis=0, tiled=True),
    )
    cross_query_heads = cross_queries.reshape(tok_rows, H, HD)
    cross_key_heads = cross_keys.reshape(-1, H, HD)
    cross_value_heads = cross_values.reshape(-1, H, HD)
    cross_heads, cross_logsum = attention_forward(
        cross_query_heads, cross_key_heads, cross_value_heads, cross_mask, None
    )
    cross_attended = cross_heads.reshape(tok_rows, H * HD).astype(jnp.bfloat16)
    after_cross = after_self + product(cross_attended, gathered[7])
    feed_normed = normalize(after_cross, gathered[13].astype(jnp.float32)).astype(jnp.bfloat16)
    gate_value = product(feed_normed, gathered[8])
    up_value = product(feed_normed, gathered[9])
    hidden_units = (jax.nn.gelu(gate_value, approximate=True) * up_value).astype(jnp.bfloat16)
    layer_out = (after_cross + product(hidden_units, gathered[10])).astype(jnp.bfloat16)
    grad_after = out_grad[0].astype(jnp.float32)
    grad_round = grad_after.astype(jnp.bfloat16)
    grad_feed_down = product_left(hidden_units, grad_round)
    grad_hidden = product_right(grad_round, gathered[10])
    unused, pullback = jax.vjp(
        lambda gate_in, up_in: jax.nn.gelu(gate_in, approximate=True) * up_in, gate_value, up_value
    )
    grad_gate, grad_up = pullback(grad_hidden)
    gate_round = grad_gate.astype(jnp.bfloat16)
    up_round = grad_up.astype(jnp.bfloat16)
    grad_feed_gate = product_left(feed_normed, gate_round)
    grad_feed_up = product_left(feed_normed, up_round)
    grad_feed_normed = product_right(gate_round, gathered[8]) + product_right(up_round, gathered[9])
    grad_cross_side, grad_norm_feed = norm_back(
        after_cross, gathered[13].astype(jnp.float32), grad_feed_normed
    )
    grad_after_cross = grad_after + grad_cross_side
    cross_round = grad_after_cross.astype(jnp.bfloat16)
    grad_cross_out = product_left(cross_attended, cross_round)
    grad_cross_heads = (
        product_right(cross_round, gathered[7]).astype(jnp.bfloat16).reshape(tok_rows, H, HD)
    )
    cross_delta = attention_delta(
        cross_query_heads,
        cross_key_heads,
        cross_value_heads,
        grad_cross_heads,
        cross_logsum,
        cross_mask,
        None,
    )
    grad_cross_q, unused_table, grad_cross_k, grad_cross_v = attention_backward(
        cross_query_heads,
        cross_key_heads,
        cross_value_heads,
        grad_cross_heads,
        cross_logsum,
        cross_delta,
        cross_mask,
        None,
    )
    cross_key_grad, cross_value_grad = (
        lax.psum_scatter(
            grad_cross_k.astype(jnp.bfloat16), "ctx", scatter_dimension=0, tiled=True
        ).astype(jnp.float32),
        lax.psum_scatter(
            grad_cross_v.astype(jnp.bfloat16), "ctx", scatter_dimension=0, tiled=True
        ).astype(jnp.float32),
    )
    cross_key_round = cross_key_grad.astype(jnp.bfloat16)
    cross_value_round = cross_value_grad.astype(jnp.bfloat16)
    grad_cross_key = product_left(encoded, cross_key_round)
    grad_cross_value = product_left(encoded, cross_value_round)
    encoder_grad = product_right(cross_key_round, gathered[5]) + product_right(
        cross_value_round, gathered[6]
    )
    cross_query_round = grad_cross_q.reshape(tok_rows, H * HD).astype(jnp.bfloat16)
    grad_cross_query = product_left(cross_normed, cross_query_round)
    grad_cross_normed = product_right(cross_query_round, gathered[4])
    grad_self_side, grad_norm_cross = norm_back(
        after_self, gathered[12].astype(jnp.float32), grad_cross_normed
    )
    grad_after_self = grad_after_cross + grad_self_side
    self_round = grad_after_self.astype(jnp.bfloat16)
    grad_self_out = product_left(self_attended, self_round)
    grad_self_flat = product_right(self_round, gathered[3]).astype(jnp.bfloat16)
    grad_self_heads = grad_self_flat.reshape(tok_rows, H, HD)
    back_table = gathered[14].reshape(H, BUCKETS)
    self_delta = attention_delta(
        query_heads, key_heads, value_heads, grad_self_heads, self_logsum, self_mask, back_table
    )
    grad_self_q, grad_table, grad_self_k, grad_self_v = attention_backward(
        query_heads,
        key_heads,
        value_heads,
        grad_self_heads,
        self_logsum,
        self_delta,
        self_mask,
        back_table,
    )
    self_key_grad, self_value_grad = (
        lax.psum_scatter(
            grad_self_k.astype(jnp.bfloat16), "ctx", scatter_dimension=0, tiled=True
        ).astype(jnp.float32),
        lax.psum_scatter(
            grad_self_v.astype(jnp.bfloat16), "ctx", scatter_dimension=0, tiled=True
        ).astype(jnp.float32),
    )
    self_key_round = self_key_grad.astype(jnp.bfloat16)
    self_value_round = self_value_grad.astype(jnp.bfloat16)
    self_query_round = grad_self_q.reshape(tok_rows, H * HD).astype(jnp.bfloat16)
    grad_self_query = product_left(self_normed, self_query_round)
    grad_self_key = product_left(self_normed, self_key_round)
    grad_self_value = product_left(self_normed, self_value_round)
    grad_self_normed = (
        product_right(self_query_round, gathered[0])
        + product_right(self_key_round, gathered[1])
        + product_right(self_value_round, gathered[2])
    )
    grad_input_side, grad_norm_self = norm_back(
        inputs, gathered[11].astype(jnp.float32), grad_self_normed
    )
    hidden_grad = grad_after_self + grad_input_side
    grad_bias_table = grad_table.reshape(H * BUCKETS)
    pieces = (
        lax.psum_scatter(
            grad_self_query.astype(jnp.bfloat16), "fsdp", scatter_dimension=0, tiled=True
        ).astype(jnp.float32),
        lax.psum_scatter(
            grad_self_key.astype(jnp.bfloat16), "fsdp", scatter_dimension=0, tiled=True
        ).astype(jnp.float32),
        lax.psum_scatter(
            grad_self_value.astype(jnp.bfloat16), "fsdp", scatter_dimension=0, tiled=True
        ).astype(jnp.float32),
        lax.psum_scatter(
            grad_self_out.astype(jnp.bfloat16), "fsdp", scatter_dimension=0, tiled=True
        ).astype(jnp.float32),
        lax.psum_scatter(
            grad_cross_query.astype(jnp.bfloat16), "fsdp", scatter_dimension=0, tiled=True
        ).astype(jnp.float32),
        lax.psum_scatter(
            grad_cross_key.astype(jnp.bfloat16), "fsdp", scatter_dimension=0, tiled=True
        ).astype(jnp.float32),
        lax.psum_scatter(
            grad_cross_value.astype(jnp.bfloat16), "fsdp", scatter_dimension=0, tiled=True
        ).astype(jnp.float32),
        lax.psum_scatter(
            grad_cross_out.astype(jnp.bfloat16), "fsdp", scatter_dimension=0, tiled=True
        ).astype(jnp.float32),
        lax.psum_scatter(
            grad_feed_gate.astype(jnp.bfloat16), "fsdp", scatter_dimension=0, tiled=True
        ).astype(jnp.float32),
        lax.psum_scatter(
            grad_feed_up.astype(jnp.bfloat16), "fsdp", scatter_dimension=0, tiled=True
        ).astype(jnp.float32),
        lax.psum_scatter(
            grad_feed_down.astype(jnp.bfloat16), "fsdp", scatter_dimension=0, tiled=True
        ).astype(jnp.float32),
        lax.psum_scatter(
            grad_norm_self.astype(jnp.bfloat16), "fsdp", scatter_dimension=0, tiled=True
        ).astype(jnp.float32),
        lax.psum_scatter(
            grad_norm_cross.astype(jnp.bfloat16), "fsdp", scatter_dimension=0, tiled=True
        ).astype(jnp.float32),
        lax.psum_scatter(
            grad_norm_feed.astype(jnp.bfloat16), "fsdp", scatter_dimension=0, tiled=True
        ).astype(jnp.float32),
        lax.psum_scatter(
            grad_bias_table.astype(jnp.bfloat16), "fsdp", scatter_dimension=0, tiled=True
        ).astype(jnp.float32),
    )
    owned = (
        lax.psum(pieces[0].astype(jnp.bfloat16), "ctx").astype(jnp.float32),
        lax.psum(pieces[1].astype(jnp.bfloat16), "ctx").astype(jnp.float32),
        lax.psum(pieces[2].astype(jnp.bfloat16), "ctx").astype(jnp.float32),
        lax.psum(pieces[3].astype(jnp.bfloat16), "ctx").astype(jnp.float32),
        lax.psum(pieces[4].astype(jnp.bfloat16), "ctx").astype(jnp.float32),
        lax.psum(pieces[5].astype(jnp.bfloat16), "ctx").astype(jnp.float32),
        lax.psum(pieces[6].astype(jnp.bfloat16), "ctx").astype(jnp.float32),
        lax.psum(pieces[7].astype(jnp.bfloat16), "ctx").astype(jnp.float32),
        lax.psum(pieces[8].astype(jnp.bfloat16), "ctx").astype(jnp.float32),
        lax.psum(pieces[9].astype(jnp.bfloat16), "ctx").astype(jnp.float32),
        lax.psum(pieces[10].astype(jnp.bfloat16), "ctx").astype(jnp.float32),
        lax.psum(pieces[11].astype(jnp.bfloat16), "ctx").astype(jnp.float32),
        lax.psum(pieces[12].astype(jnp.bfloat16), "ctx").astype(jnp.float32),
        lax.psum(pieces[13].astype(jnp.bfloat16), "ctx").astype(jnp.float32),
        lax.psum(pieces[14].astype(jnp.bfloat16), "ctx").astype(jnp.float32),
    )
    return (
        layer_out[None],
        hidden_grad[None],
        encoder_grad[None],
        owned[0],
        owned[1],
        owned[2],
        owned[3],
        owned[4],
        owned[5],
        owned[6],
        owned[7],
        owned[8],
        owned[9],
        owned[10],
        owned[11],
        owned[12],
        owned[13],
        owned[14],
    )


def place():
    rank = lax.axis_index("fsdp")
    core = lax.rem(rank, 2)
    along_x = lax.rem(lax.div(rank, 2), 2)
    along_y = lax.div(rank, 4)
    return (rank, core, along_x, along_y, lax.axis_index("ctx"))


def greet(partners):
    barrier = pltpu.get_barrier_semaphore()
    for partner in partners:
        pl.semaphore_signal(barrier, inc=1, device_id=partner, device_id_type=MESH)
    pl.semaphore_wait(barrier, len(partners))


def remote(source, target, send_sem, recv_sem, device):
    return pltpu.make_async_remote_copy(
        src_ref=source,
        dst_ref=target,
        send_sem=send_sem,
        recv_sem=recv_sem,
        device_id=device,
        device_id_type=MESH,
    )


class Unit:
    def __init__(self, number, start, rows, flat, first, last):
        self.number, self.start, self.rows = number, start, rows
        self.flat, self.first, self.last = flat, first, last


def units_of(shapes, flat_count):
    units = []
    for number, (rows, columns) in enumerate(shapes):
        parts = max(1, rows * columns // (176 * 1024)) if number < len(shapes) - 1 else 4
        most = -(-rows // parts // 16) * 16
        starts = list(range(0, rows, most))
        for start in starts:
            size = min(most, rows - start)
            units.append(Unit(number, start, size, number < flat_count, start == 0, start == starts[-1]))
    return units


class Gather:
    def __init__(self, units, owns, fulls, send_sems, recv_sems, local_sems):
        rank, core, along_x, along_y, depth = place()
        self.units, self.owns, self.fulls = units, owns, fulls
        self.send_sems, self.recv_sems, self.local_sems = send_sems, recv_sems, local_sems
        self.rank = rank
        self.by_x = rank + 2 - 4 * along_x
        self.by_y = rank + 4 - 8 * along_y
        self.diag = self.by_x + 4 - 8 * along_y
        self.to_x = (self.by_x, depth)
        self.to_y = (self.by_y, depth)
        self.to_core = (rank + 1 - 2 * core, depth)
        self.shift = 1 - 2 * core
        odd = lax.rem(depth, 2)
        self.odd = odd == 1
        self.to_pair = (rank, depth + 1 - 2 * odd)
        self.second = self.by_x + odd * (self.diag - self.by_x)
        self.third = self.diag + odd * (self.by_x - self.diag)

    def rows(self, index, slot, half):
        unit = self.units[index]
        size = self.owns[unit.number].shape[0]
        start = pl.multiple_of(slot * size + unit.start, math.gcd(size, unit.start))
        rows = unit.rows
        if half is not None:
            rows = rows // 2
            start = pl.multiple_of(start + half * rows, math.gcd(size, unit.start, rows))
        return self.fulls[unit.number].at[pl.ds(start, rows)]

    def copy(self, index, kind, slot, half, device, own=False):
        target = self.rows(index, slot, half)
        unit = self.units[index]
        return remote(
            self.owns[unit.number].at[pl.ds(unit.start, unit.rows)] if own else target,
            target,
            self.send_sems.at[index, kind],
            self.recv_sems.at[index, kind],
            device,
        )

    def sent(self, index, kind):
        flat = (
            (self.rank, None, self.to_x),
            (self.rank, None, self.to_y),
            (self.rank, None, self.to_core),
            (self.by_x, 0, self.to_y),
            (self.by_y, 1, self.to_x),
            (self.by_x, None, self.to_core),
            (self.by_y, None, self.to_core),
            (self.diag, 0, self.to_core),
            (self.diag, 1, self.to_core),
        )
        line = (
            (self.rank, None, self.to_x),
            (self.rank, None, self.to_y),
            (self.rank, None, self.to_core),
            (self.by_y, None, self.to_x),
            (self.second, None, self.to_pair),
            (self.by_y, None, self.to_core),
            (self.second, None, self.to_core),
            (self.third, None, self.to_core),
        )
        slot, half, device = (flat if self.units[index].flat else line)[kind]
        return self.copy(index, kind, slot, half, device, kind < 3)

    def landed(self, index, kind):
        shift = self.shift
        flat = (
            (self.by_x, None, self.to_x),
            (self.by_y, None, self.to_y),
            (self.rank + shift, None, self.to_core),
            (self.diag, 0, self.to_y),
            (self.diag, 1, self.to_x),
            (self.by_x + shift, None, self.to_core),
            (self.by_y + shift, None, self.to_core),
            (self.diag + shift, 0, self.to_core),
            (self.diag + shift, 1, self.to_core),
        )
        line = (
            (self.by_x, None, self.to_x),
            (self.by_y, None, self.to_y),
            (self.rank + shift, None, self.to_core),
            (self.diag, None, self.to_x),
            (self.third, None, self.to_pair),
            (self.by_y + shift, None, self.to_core),
            (self.second + shift, None, self.to_core),
            (self.third + shift, None, self.to_core),
        )
        slot, half, device = (flat if self.units[index].flat else line)[kind]
        return self.copy(index, kind, slot, half, device)

    def local(self, number):
        size = self.owns[number].shape[0]
        start = pl.multiple_of(self.rank * size, size)
        target = self.fulls[number].at[pl.ds(start, size)]
        return pltpu.make_async_copy(self.owns[number], target, self.local_sems.at[number])

    def by_pair(self, even, odd):
        pl.when(jnp.logical_not(self.odd))(even)
        pl.when(self.odd)(odd)

    def issue(self, index):
        unit = self.units[index]
        self.sent(index, 1).start()
        if unit.flat:
            self.sent(index, 0).start()
        else:
            pl.when(jnp.logical_not(self.odd))(lambda: self.sent(index, 0).start())
        self.sent(index, 2).start()
        if unit.first:
            self.local(unit.number).start()

    def relay(self, index):
        if self.units[index].flat:
            self.landed(index, 0).wait_recv()
            self.sent(index, 3).start()
            self.landed(index, 1).wait_recv()
            self.sent(index, 4).start()
            self.sent(index, 5).start()
            self.sent(index, 6).start()
            return
        self.landed(index, 1).wait_recv()
        pl.when(self.odd)(lambda: self.sent(index, 3).start())
        self.sent(index, 5).start()

    def spread(self, index):
        if self.units[index].flat:
            self.landed(index, 3).wait_recv()
            self.sent(index, 7).start()
            self.landed(index, 4).wait_recv()
            self.sent(index, 8).start()
            return
        self.by_pair(
            lambda: self.landed(index, 0).wait_recv(), lambda: self.landed(index, 3).wait_recv()
        )
        self.sent(index, 4).start()
        self.sent(index, 6).start()

    def close(self, index):
        if not self.units[index].flat:
            self.landed(index, 4).wait_recv()
            self.sent(index, 7).start()

    def finish(self, index):
        unit = self.units[index]
        for kind in (2, 5, 6, 7, 8) if unit.flat else (2, 5, 6, 7):
            self.landed(index, kind).wait_recv()
        if unit.flat:
            for kind in range(9):
                self.sent(index, kind).wait_send()
        else:
            self.by_pair(
                lambda: self.sent(index, 0).wait_send(), lambda: self.sent(index, 3).wait_send()
            )
            for kind in (1, 2, 4, 5, 6, 7):
                self.sent(index, kind).wait_send()
        if unit.last:
            self.local(unit.number).wait()


def column_partners(rank, depth):
    return [(rank, lax.rem(depth + step, DOCS)) for step in range(1, DOCS)]


def tile(index, size=256):
    return pl.ds(pl.multiple_of(index * size, size), size)


def each(count, body):
    def one(index, unused):
        body(index)
        return unused

    lax.fori_loop(0, count, one, 0)


def by_columns(left, right, write):
    def one(index):
        at = tile(index)
        write(at, product(left[...], right[:, at]))

    each(right.shape[1] // 256, one)


def store_as(target):
    def write(at, value):
        target[:, at] = value.astype(target.dtype)

    return write


def rms_rows(values, gain, normed):
    def one(index):
        at = tile(index, 32)
        v = values[at, :]
        root = lax.rsqrt(jnp.mean(v * v, axis=-1, keepdims=True) + epsilon)
        normed[at, :] = (v * root * gain).astype(jnp.bfloat16)

    each(values.shape[0] // 32, one)


def half_masks():
    lane = lax.broadcasted_iota(jnp.int32, (1, 2 * HD), 1)
    low = (lane < HD).astype(jnp.float32)
    return (low.astype(jnp.bfloat16), (1.0 - low).astype(jnp.bfloat16))


def causal_bias(smalls, spread, pair, half):
    row = smalls[tile(pair, 16), :][3:4]
    size = spread.shape[2]
    row = jnp.broadcast_to(row, (8, 128)).astype(jnp.bfloat16)
    line = product(row, spread[half])[0:1]
    bias = pltpu.roll(jnp.broadcast_to(line, (size, size)), 0, 1, stride=1, stride_axis=0)
    here = lax.broadcasted_iota(jnp.int32, (size, size), 0)
    there = lax.broadcasted_iota(jnp.int32, (size, size), 1)
    return jnp.where(there <= here, bias, masked_value)


def softmax_rows(scores):
    terms = jnp.exp(scores - jnp.max(scores, axis=-1, keepdims=True))
    return terms * (1.0 / jnp.sum(terms, axis=-1, keepdims=True))


def attend_heads(queries, keys, values, out, bias_of):
    masks = half_masks()

    def pair(index):
        at = tile(index, 2 * HD)
        q, k, v = queries[:, at], keys[:, at], values[:, at]
        total = jnp.zeros(q.shape, jnp.float32)
        for half in range(2):
            scores = product_right(q * masks[half], k)
            if bias_of is not None:
                scores = scores + bias_of(index, half)
            weights = softmax_rows(scores).astype(jnp.bfloat16)
            total = total + product(weights, v * masks[half])
        out[:, at] = total.astype(jnp.bfloat16)

    each(H // 2, pair)


def column_partners(rank, depth):
    return [(rank, lax.rem(depth + step, DOCS)) for step in range(1, DOCS)]


class Kept:
    inputs, normed, q, k, u, o1, after, normed2, cq = range(9)
    ck, cv, o2, after2, normed3, w, slope, gelu, cot = range(9, 18)
    normed_t, q_t, o1_t, normed2_t, cq_t, o2_t, normed3_t, states_t = range(18, 26)
    count = 26
    wide = (14, 15, 16)
    exact = (0, 6, 12, 15, 16)
    states = (9, 10)
    flipped = tuple(range(18, 26))
    inside = (1, 5, 7, 11, 13)


class Steps:
    lags = (0, 3, 5, 7, 8)

    def __init__(self, gather):
        self.gather, self.step, self.finished = gather, 0, 0

    def advance(self):
        gather, count = self.gather, len(self.gather.units)
        stages = (gather.issue, gather.relay, gather.spread, gather.close, gather.finish)
        for stage, lag in zip(stages, self.lags):
            if 0 <= self.step - lag < count:
                stage(self.step - lag)
        self.step += 1
        self.finished = min(max(0, self.step - self.lags[-1]), count)


def forward_kernel(count, units, *refs):
    owns, refs = refs[:count], refs[count:]
    (tokens, cotangent, chosen, encoded, spread), refs = refs[:5], refs[5:]
    fulls, refs = refs[:count], refs[count:]
    n = Kept.count
    outs, refs = refs[:n], refs[n:]
    grad_out, refs = refs[0], refs[1:]
    keep, refs = refs[:n], refs[n:]
    (
        grad_fd,
        smalls,
        gains,
        all_tokens,
        all_cotangent,
        square,
        wide,
        send_sems,
        recv_sems,
        local_sems,
        line_send,
        line_recv,
        line_local,
        load_sems,
        save_sems,
    ) = refs
    rank, core, along_x, along_y, depth = place()
    gather = Gather(units, owns, fulls, send_sems, recv_sems, local_sems)
    column = column_partners(rank, depth)
    greet([gather.to_x, gather.to_y, gather.to_core] + column)

    def line_copies(number):
        own, whole = ((tokens, all_tokens), (cotangent, all_cotangent))[number]
        rows = own.shape[0]
        at = whole.at[pl.ds(pl.multiple_of(depth * rows, rows), rows)]
        here = pltpu.make_async_copy(own, at, line_local.at[number])
        sends, receives = [], []
        for step, partner in enumerate(column):
            sems = (line_send.at[number, step], line_recv.at[number, step])
            sends.append(remote(own, at, sems[0], sems[1], partner))
            origin = lax.rem(depth + DOCS - 1 - step, DOCS)
            landing = whole.at[pl.ds(pl.multiple_of(origin * rows, rows), rows)]
            receives.append(remote(own, landing, sems[0], sems[1], partner))
        return (here, sends, receives)

    def line_finish(number):
        here, sends, receives = line_copies(number)
        here.wait()
        for copy in receives:
            copy.wait_recv()
        for copy in sends:
            copy.wait_send()

    steps = Steps(gather)
    advance = steps.advance
    lasts = [index for index, unit in enumerate(units) if unit.last]
    advance()
    for number in range(2):
        here, sends, unused = line_copies(number)
        here.start()
        for copy in sends:
            copy.start()

    def flip(source, name):
        turn(source, keep[name])
        save(name)

    def save(name):
        if name in Kept.inside:
            return
        pltpu.make_async_copy(keep[name], outs[name], save_sems.at[name]).start()

    def load(number):
        if number == 0:
            buffer = smalls
        else:
            buffer = (square if fulls[number].shape[1] == square.shape[2] else wide).at[number % 2]
        return (pltpu.make_async_copy(fulls[number], buffer, load_sems.at[number]), buffer)

    def loaded(number):
        copy, buffer = load(number)
        copy.wait()
        return buffer

    def project(left, number, name):
        by_columns(left, loaded(number), store_as(keep[name]))
        save(name)

    def residual(before, left, number, name, gain, normed, turned):
        weight = loaded(number)

        def write(at, value):
            keep[name][:, at] = keep[before][:, at] + value

        by_columns(keep[left], weight, write)
        save(name)
        rms_rows(keep[name], gains[gain : gain + 1, :], keep[normed])
        flip(keep[normed], turned)

    def start():
        loaded(0)
        for slot in range(8):
            gains[0:3, 128 * slot : 128 * slot + 128] = smalls[16 * slot : 16 * slot + 3, :]
        flip(encoded, Kept.states_t)

    def values_and_tokens():
        project(encoded, 2, Kept.cv)
        line_finish(0)
        by_columns(chosen, all_tokens, store_as(keep[Kept.inputs]))
        save(Kept.inputs)
        rms_rows(keep[Kept.inputs], gains[0:1, :], keep[Kept.normed])
        flip(keep[Kept.normed], Kept.normed_t)

    def keys():
        flip(keep[Kept.q], Kept.q_t)
        project(keep[Kept.normed], 4, Kept.k)

    def self_heads():
        project(keep[Kept.normed], 5, Kept.u)
        advance()
        attend_heads(
            keep[Kept.q], keep[Kept.k], keep[Kept.u], keep[Kept.o1], functools.partial(causal_bias, smalls, spread)
        )
        flip(keep[Kept.o1], Kept.o1_t)

    def cross_heads():
        project(keep[Kept.normed2], 7, Kept.cq)
        flip(keep[Kept.cq], Kept.cq_t)
        advance()
        attend_heads(keep[Kept.cq], keep[Kept.ck], keep[Kept.cv], keep[Kept.o2], None)
        flip(keep[Kept.o2], Kept.o2_t)
        line_finish(1)
        by_columns(chosen, all_cotangent, store_as(keep[Kept.cot]))
        save(Kept.cot)

    def gate():
        by_columns(keep[Kept.normed3], loaded(9), store_as(keep[Kept.slope]))

    def up():
        weight = loaded(10)
        scale = math.sqrt(2.0 / math.pi)

        def write(at, b):
            a = keep[Kept.slope][:, at]
            t = jnp.tanh(scale * (a + 0.044715 * (a * a * a)))
            gelu = 0.5 * a * (1.0 + t)
            slope = 0.5 * (1.0 + t) + 0.5 * a * (1.0 - t * t) * scale * (
                1.0 + 3 * 0.044715 * (a * a)
            )
            keep[Kept.gelu][:, at] = gelu
            keep[Kept.slope][:, at] = slope * b
            w = (gelu * b).astype(jnp.bfloat16)
            keep[Kept.w][:, at] = w
            grad = product_left(w, keep[Kept.cot][...]).astype(jnp.bfloat16)
            for part in range(grad_fd.shape[0]):
                grad_fd[part, at, :] = grad[:, 256 * part : 256 * part + 256]

        def one(index):
            at = tile(index)
            write(at, product(keep[Kept.normed3][...], weight[:, at]))

        tiles = weight.shape[1] // 256
        for part in range(0, tiles, 3):
            lax.fori_loop(part, min(part + 3, tiles), lambda index, unused: one(index), None)
            advance()
        for name in (Kept.gelu, Kept.slope, Kept.w):
            save(name)
        pltpu.make_async_copy(grad_fd, grad_out, save_sems.at[n]).start()

    compute = (
        start,
        lambda: project(encoded, 1, Kept.ck),
        values_and_tokens,
        lambda: project(keep[Kept.normed], 3, Kept.q),
        keys,
        self_heads,
        lambda: residual(Kept.inputs, Kept.o1, 6, Kept.after, 1, Kept.normed2, Kept.normed2_t),
        cross_heads,
        lambda: residual(Kept.after, Kept.o2, 8, Kept.after2, 2, Kept.normed3, Kept.normed3_t),
        gate,
        up,
    )
    for number in range(count - 1):
        while steps.finished <= lasts[number]:
            advance()
        load(number)[0].start()
        if number:
            compute[number - 1]()
    compute[count - 2]()
    while steps.finished < len(units):
        advance()
    for name in range(n):
        if name not in Kept.inside:
            pltpu.make_async_copy(keep[name], outs[name], save_sems.at[name]).wait()
    pltpu.make_async_copy(grad_fd, grad_out, save_sems.at[n]).wait()


def forward_call(shards, tokens, cotangent, chosen, encoded, spread):
    count = len(shards)
    vmem = pl.BlockSpec(memory_space=pltpu.VMEM)
    anywhere = pl.BlockSpec(memory_space=pl.ANY)
    most, total = chosen.shape
    shapes = [jax.ShapeDtypeStruct((8 * s.shape[0], s.shape[1]), s.dtype) for s in shards]
    saved = []
    for name in range(Kept.count):
        if name in Kept.flipped:
            rows = encoded.shape[0] if name == Kept.states_t else most
            saved.append(((shards[1].shape[1], rows), jnp.bfloat16))
            continue
        rows = encoded.shape[0] if name in Kept.states else most
        width = shards[9].shape[1] if name in Kept.wide else shards[1].shape[1]
        saved.append(((rows, width), jnp.float32 if name in Kept.exact else jnp.bfloat16))
    shapes += [jax.ShapeDtypeStruct(*s) for s in saved]
    down = shapes[count - 1]
    down = jax.ShapeDtypeStruct((down.shape[1] // 256, down.shape[0], 256), down.dtype)
    square = shards[1].shape[1]
    units = units_of([s.shape for s in shards], 3)
    return pl.pallas_call(
        functools.partial(forward_kernel, count, units),
        out_shape=shapes + [down],
        in_specs=[vmem] * (count + 5),
        out_specs=[anywhere] * (len(shapes) + 1),
        scratch_shapes=[pltpu.VMEM(*s) for s in saved]
        + [
            pltpu.VMEM(down.shape, down.dtype),
            pltpu.VMEM(shapes[0].shape, jnp.float32),
            pltpu.VMEM((8, square), jnp.float32),
            pltpu.VMEM((total, square), jnp.bfloat16),
            pltpu.VMEM((total, square), jnp.bfloat16),
            pltpu.VMEM((2, square, square), jnp.bfloat16),
            pltpu.VMEM((2, square, shards[9].shape[1]), jnp.bfloat16),
            pltpu.SemaphoreType.DMA((len(units), 9)),
            pltpu.SemaphoreType.DMA((len(units), 9)),
            pltpu.SemaphoreType.DMA((count,)),
            pltpu.SemaphoreType.DMA((2, DOCS - 1)),
            pltpu.SemaphoreType.DMA((2, DOCS - 1)),
            pltpu.SemaphoreType.DMA((2,)),
            pltpu.SemaphoreType.DMA((count,)),
            pltpu.SemaphoreType.DMA((len(saved) + 1,)),
        ],
        compiler_params=pltpu.CompilerParams(
            collective_id=1, has_side_effects=True, vmem_limit_bytes=60 * 2**20
        ),
        name="forward",
    )(*shards, tokens, cotangent, chosen, encoded, spread)


def add_rows(target, source):
    rows = target.shape[1]
    step = math.gcd(rows, 64)

    def one(index):
        at = pl.ds(pl.multiple_of(index * step, step), step)
        target[:, at, :] = target[:, at, :] + source[:, at, :]

    each(rows // step, one)


class Reduce:
    def __init__(self, pieces, buffers, load, send_sems, recv_sems, local_sems):
        rank, core, along_x, along_y, depth = place()
        self.pieces, self.buffers, self.load = pieces, buffers, load
        self.send_sems, self.recv_sems, self.local_sems = send_sems, recv_sems, local_sems
        self.core, self.along_x, self.along_y = core, along_x, along_y
        self.block = 2 * along_y + along_x
        self.to_x = (rank + 2 - 4 * along_x, depth)
        self.to_y = (rank + 4 - 8 * along_y, depth)
        self.to_core = (rank + 1 - 2 * core, depth)
        self.inner = (depth == 1) | (depth == 2)
        self.to_line = (rank, depth + 1 - 2 * lax.rem(depth, 2))
        self.to_middle = (rank, 3 - depth)
        self.partners = [self.to_x, self.to_y, self.to_core, self.to_line, self.to_middle]

    def copy(self, number, kind, source, target, device):
        return remote(
            source,
            target,
            self.send_sems.at[number, kind],
            self.recv_sems.at[number, kind],
            device,
        )

    def halves(self, number):
        size = self.pieces[number].rows // 2
        return (pl.ds(0, size), pl.ds(size, size))

    def core_copies(self, number):
        piece, both = self.pieces[number], self.buffers[number][0]
        return [
            self.copy(number, q, piece.slot(2 * q + 1 - self.core), both.at[q // 2, q % 2], self.to_core)
            for q in range(4)
        ]

    def own_load(self, number, q):
        return pltpu.make_async_copy(
            self.pieces[number].slot(2 * q + self.core),
            self.load[number].at[q % 2],
            self.local_sems.at[number, q],
        )

    def first_copies(self, number):
        both, from_x, from_y = self.buffers[number][:3]
        low, high = self.halves(number)
        return [
            self.copy(number, 4, both.at[:, 1 - self.along_x, :, low], from_x, self.to_x),
            self.copy(number, 6, both.at[1 - self.along_y, :, :, high], from_y, self.to_y),
        ]

    def second_copies(self, number):
        both, unused_x, unused_y, late_x, late_y = self.buffers[number][:5]
        low, high = self.halves(number)
        return [
            self.copy(
                number,
                8,
                both.at[1 - self.along_y, self.along_x, :, low],
                late_y,
                self.to_y,
            ),
            self.copy(
                number,
                9,
                both.at[self.along_y, 1 - self.along_x, :, high],
                late_x,
                self.to_x,
            ),
        ]

    def line_copy(self, number):
        return self.copy(
            number,
            10,
            self.buffers[number][0].at[self.along_y, self.along_x],
            self.buffers[number][5],
            self.to_line,
        )

    def middle_copy(self, number):
        return self.copy(
            number,
            11,
            self.buffers[number][0].at[self.along_y, self.along_x],
            self.buffers[number][6],
            self.to_middle,
        )

    def return_copy(self, number):
        return self.copy(
            number,
            10,
            self.buffers[number][5],
            self.buffers[number][5],
            self.to_line,
        )

    def write(self, number):
        return pltpu.make_async_copy(
            self.buffers[number][5],
            self.pieces[number].out.at[self.pieces[number].tiles],
            self.local_sems.at[number, 4],
        )

    def stage(self, number, level):
        both, from_x, from_y, late_x, late_y, on_line, on_middle = self.buffers[number]
        low, high = self.halves(number)
        if level == 0:
            for copy in self.core_copies(number):
                copy.start()
            self.own_load(number, 0).start()
            self.own_load(number, 1).start()
        elif level == 1:
            for q, copy in enumerate(self.core_copies(number)):
                copy.wait_recv()
                self.own_load(number, q).wait()
                add_rows(both.at[q // 2, q % 2], self.load[number].at[q % 2])
                if q < 2:
                    self.own_load(number, q + 2).start()
            for copy in self.first_copies(number):
                copy.start()
        elif level == 2:
            copies = self.first_copies(number)
            for copy in copies:
                copy.wait_recv()
                copy.wait_send()
            for other in range(2):
                add_rows(both.at[other, self.along_x, :, low], from_x.at[other])
            for other in range(2):
                add_rows(both.at[self.along_y, other, :, high], from_y.at[other])
            for copy in self.second_copies(number):
                copy.start()
        elif level == 3:
            to_y, to_x = self.second_copies(number)
            to_y.wait_recv()
            add_rows(both.at[self.along_y, self.along_x, :, low], late_y)
            to_x.wait_recv()
            add_rows(both.at[self.along_y, self.along_x, :, high], late_x)
            to_y.wait_send()
            to_x.wait_send()

            @pl.when(jnp.logical_not(self.inner))
            def _():
                self.line_copy(number).start()
        elif level == 4:

            @pl.when(self.inner)
            def _():
                self.line_copy(number).wait_recv()
                add_rows(both.at[self.along_y, self.along_x], on_line)
                self.middle_copy(number).start()
        elif level == 5:

            @pl.when(self.inner)
            def _():
                middle = self.middle_copy(number)
                middle.wait_recv()
                rows = on_line.shape[1]
                step = math.gcd(rows, 64)

                def one(index):
                    at = pl.ds(pl.multiple_of(index * step, step), step)
                    on_line[:, at, :] = both[self.along_y, self.along_x, :, at, :] + on_middle[:, at, :]

                each(rows // step, one)
                middle.wait_send()
                self.return_copy(number).start()
        else:
            line = self.line_copy(number)

            @pl.when(jnp.logical_not(self.inner))
            def _():
                line.wait_send()
                line.wait_recv()

            @pl.when(self.inner)
            def _():
                self.return_copy(number).wait_send()

            for copy in self.core_copies(number):
                copy.wait_send()
            self.write(number).start()

    levels = 7


def buffer_shapes(tiles, rows, width, dtype):
    return [
        pltpu.VMEM((2, 2, tiles, rows, width), dtype),
        pltpu.VMEM((2, tiles, rows // 2, width), dtype),
        pltpu.VMEM((2, tiles, rows // 2, width), dtype),
        pltpu.VMEM((tiles, rows // 2, width), dtype),
        pltpu.VMEM((tiles, rows // 2, width), dtype),
        pltpu.VMEM((tiles, rows, width), dtype),
        pltpu.VMEM((tiles, rows, width), dtype),
    ]


class Piece:
    def __init__(self, grad, out, start, tiles):
        self.grad, self.out = grad, out
        self.tiles = pl.ds(start, tiles)
        self.rows = grad.shape[2]

    def slot(self, index):
        return self.grad.at[self.tiles, index]


def pieces_of(shape):
    most = 1 if shape[2] > 256 else 4
    return [(start, min(most, shape[0] - start)) for start in range(0, shape[0], most)]


def piece_order(shapes):
    parts = [[(number,) + p for p in pieces_of(shape)] for number, shape in enumerate(shapes)]
    turns = [p for both in zip(parts[1], parts[2]) for p in both]
    return parts[0] + turns + [p for part in parts[3:] for p in part]


class Pipeline:
    gaps = (0, 1, 2, 2, 2, 2, 2)

    def __init__(self, reduce, count):
        self.reduce, self.count = reduce, count
        self.done, self.ready = [0] * reduce.levels, 0

    def tick(self):
        before = [self.ready] + list(self.done)
        for level in reversed(range(len(self.gaps))):
            gap = self.gaps[level]
            limit = before[level]
            if level and limit < self.count:
                limit = limit - gap + 1
            if self.done[level] < limit:
                self.reduce.stage(self.done[level], level)
                self.done[level] += 1

    def drain(self):
        while self.done[-1] < self.count:
            self.tick()


def rms_back(values, cotangent, gain, carry, out, gain_grad):
    def one(index):
        at = tile(index, 32)
        v, gz = values[at, :], cotangent[at, :]
        root = lax.rsqrt(jnp.mean(v * v, axis=-1, keepdims=True) + epsilon)
        scaled = gain * gz
        inner = jnp.mean(scaled * v, axis=-1, keepdims=True)
        gain_grad[...] += jnp.sum(gz * v * root, axis=0, keepdims=True)
        result = carry[at, :].astype(jnp.float32) + root * scaled - v * (root * root * root * inner)
        out[at, :] = result.astype(out.dtype)

    gain_grad[...] = jnp.zeros_like(gain_grad)
    each(values.shape[0] // 32, one)


def diagonal_sums(grad):
    size = grad.shape[1]
    total = grad[0:8]
    for group in range(1, grad.shape[0] // 8):
        part = grad[8 * group : 8 * group + 8]
        total = total + pltpu.roll(part, size - 8 * group, 1)
    row = lax.broadcasted_iota(jnp.int32, total.shape, 0)
    line = jnp.where(row == 0, total, 0.0)
    for step in range(1, 8):
        line = line + jnp.where(row == step, pltpu.roll(total, size - step, 1), 0.0)
    return jnp.sum(line, axis=0, keepdims=True)


def attend_back_heads(
    first, last, queries, flipped, keys, values, grad, grad_flipped, grad_q, grad_k, grad_v, bias_of, bias_grad
):
    masks = half_masks()
    row = lax.broadcasted_iota(jnp.int32, (2 * HD, 1), 0)
    low = (row < HD).astype(jnp.float32)
    sides = (low.astype(jnp.bfloat16), (1.0 - low).astype(jnp.bfloat16))

    def pair(index):
        at = tile(index + first, 2 * HD)
        q, k, v, g = queries[:, at], keys[:, at], values[:, at], grad[:, at]
        qt, gt = flipped[at, :], grad_flipped[at, :]
        total_q = jnp.zeros(q.shape, jnp.float32)
        total_k = jnp.zeros((2 * HD, k.shape[0]), jnp.float32)
        total_v = jnp.zeros((2 * HD, k.shape[0]), jnp.float32)
        for half in range(2):
            scores = product_right(q * masks[half], k)
            if bias_of is not None:
                scores = scores + bias_of(index + first, half)
            weights = softmax_rows(scores)
            grad_w = product_right(g * masks[half], v)
            inner = jnp.sum(weights * grad_w, axis=-1, keepdims=True)
            grad_s = weights * (grad_w - inner)
            if bias_grad is not None:
                bias_grad(index + first, half, grad_s)
            rounded = grad_s.astype(jnp.bfloat16)
            total_q = total_q + product(rounded, k * masks[half])
            total_k = total_k + product(qt * sides[half], rounded)
            total_v = total_v + product(gt * sides[half], weights.astype(jnp.bfloat16))
        grad_q[:, at] = total_q.astype(jnp.bfloat16)
        grad_k[at, :] = total_k.astype(jnp.bfloat16)
        grad_v[at, :] = total_v.astype(jnp.bfloat16)

    each(last - first, pair)


def turn(source, target):
    step = min(256, source.shape[0])

    def one(index):
        at = tile(index, step)
        target[:, at] = source[at, :].T

    each(source.shape[0] // step, one)


class Given:
    inputs, normed_t, q, q_t, k, u, o1_t, after, normed2_t = range(9)
    cq, cq_t, ck, cv, o2_t, after2, normed3_t, w, slope, gelu, cot = range(9, 20)
    states_t, chosen_t, spread, smalls = range(20, 24)
    w_ck, w_cv, w_sq, w_sk, w_sv, w_so, w_cq, w_co, w_fg, w_fu, w_fd = range(24, 35)
    grad_fd = 35
    count = 36


def backward_kernel(shared, *refs):
    given, refs = refs[: Given.count], refs[Given.count :]
    grads, refs = (given[Given.grad_fd],) + refs[:11], refs[11:]
    kept_states, refs = refs[0], refs[1:]
    outs, refs = refs[:12], refs[12:]
    (encoder_out, layer_out, hidden_out), refs = refs[:3], refs[3:]
    order = piece_order([g.shape for g in grads])
    pieces = [Piece(grads[n], outs[n], start, tiles) for n, start, tiles in order]
    count = len(pieces)
    buffers, refs = [refs[7 * i : 7 * i + 7] for i in range(count)], refs[7 * count :]
    loads = [refs[shared[i]] for i in range(count)]
    refs = refs[max(shared) + 1 :]
    (
        one_w,
        two_w,
        three_w,
        backs,
        stage,
        state_stage,
        grad_x,
        grad_n,
        value,
        other,
        cot,
        half_a,
        half_b,
        half_c,
        half_d,
        left,
        turned_q,
        turned_g,
        chosen_t,
        spread,
        smalls,
        gains,
        gain_grad,
        small_grads,
        landing,
        send_sems,
        recv_sems,
        local_sems,
        line_send,
        line_recv,
        load_sems,
        stage_sems,
        out_sems,
    ) = refs
    rank, core, along_x, along_y, depth = place()
    reduce = Reduce(pieces, buffers, loads, send_sems, recv_sems, local_sems)
    column = column_partners(rank, depth)
    greet([reduce.to_x, reduce.to_y, reduce.to_core] + column)
    pipeline = Pipeline(reduce, count)
    tick = pipeline.tick
    numbers = [n for n, unused_start, unused_tiles in order]
    pipeline.ready = numbers.count(0)
    turn_of = iter(range(1 << 20))

    def begin(*pairs):
        copies = []
        for source, target in pairs:
            sem = load_sems.at[next(turn_of) % load_sems.shape[0]]
            copies.append(pltpu.make_async_copy(source, target, sem))
            copies[-1].start()
        return copies

    def end(copies):
        for copy in copies:
            copy.wait()

    def staged(buffers_of, target_of, values, tiles):
        slots = buffers_of.shape[0]

        def copy(index):
            slot = lax.rem(index, slots)
            return pltpu.make_async_copy(buffers_of.at[slot], target_of(index), stage_sems.at[slot])

        def one(index):
            @pl.when(index >= slots)
            def _():
                copy(index - slots).wait()

            buffers_of[lax.rem(index, slots)] = values(tile(index))
            copy(index).start()

        each(tiles, one)
        for index in range(max(0, tiles - slots), tiles):
            copy(jnp.int32(index)).wait()

    def weight_grad(number, right, start=0):
        def values(at):
            result = product(left[...], right[:, at])
            return result.astype(jnp.bfloat16).reshape(stage.shape[1:])

        staged(stage, lambda index: grads[number].at[start + index], values, right.shape[1] // 256)
        pipeline.ready += 1

    def send_back(number, rows):
        def write(index):
            at = tile(index)
            result = product(chosen_t[...], rows[:, at]).astype(jnp.bfloat16)
            backs[number, :, :, at] = result.reshape(backs.shape[1:3] + (256,))

        each(rows.shape[1] // 256, write)
        for step, (unused, partner) in enumerate(column):
            back_copy(number, step, partner).start()

    def back_copy(number, step, partner):
        return remote(
            backs.at[number, partner],
            landing.at[number, step],
            line_send.at[number, step],
            line_recv.at[number, step],
            (rank, partner),
        )

    def receive_back(number, out):
        for step, (unused, partner) in enumerate(column):
            copy = back_copy(number, step, partner)
            copy.wait_recv()
            copy.wait_send()

        def one(index):
            at = tile(index, 32)
            total = backs[number, depth, at, :].astype(jnp.float32)
            for step in range(DOCS - 1):
                total = total + landing[number, step, at, :].astype(jnp.float32)
            out[at, :] = total.astype(jnp.bfloat16)

        each(out.shape[0] // 32, one)

    def norm_grad(values, gain, carry, out):
        rms_back(values, grad_n, gains[gain : gain + 1, :], carry, out, gain_grad)
        for slot in range(8):
            small_grads[0, slot, gain : gain + 1, :] = gain_grad[:, 128 * slot : 128 * slot + 128]

    def round_rows(source, target):
        def one(index):
            at = tile(index, 32)
            target[at, :] = source[at, :].astype(jnp.bfloat16)

        each(source.shape[0] // 32, one)

    def through(right_rows, weights, write):
        def one(index):
            at = tile(index)
            write(at, product_right(right_rows[...], weights[at, :]))

        each(weights.shape[0] // 256, one)

    def head_grads(weights):
        through(half_a, weights, store_as(half_b))

        def one(index):
            at = tile(index)
            turned_g[at, :] = product_right(weights[at, :], half_a[...]).astype(jnp.bfloat16)

        each(weights.shape[0] // 256, one)

    def feed_loads(start, tiles):
        at = pl.ds(256 * start, 256 * tiles)
        width = 256 * tiles
        return begin(
            (given[Given.w_fd].at[at], one_w.at[0:width]),
            (given[Given.slope].at[:, at], value.at[:, 0:width]),
            (given[Given.gelu].at[:, at], other.at[:, 0:width]),
            (given[Given.w].at[:, at], half_a.at[:, 0:width]),
            (given[Given.w_fg].at[:, at], two_w.at[:, 0:width]),
            (given[Given.w_fu].at[:, at], three_w.at[:, 0:width]),
        )

    tick()
    first = begin(
        (given[Given.cot], cot),
        (given[Given.smalls], smalls),
        (given[Given.chosen_t], chosen_t),
        (given[Given.spread], spread),
        (given[Given.normed3_t], left),
    )
    feeds = pieces_of(grads[1].shape)
    loaded = feed_loads(*feeds[0])
    tick()
    end(first)
    for slot in range(8):
        gains[0:3, 128 * slot : 128 * slot + 128] = smalls[16 * slot : 16 * slot + 3, :]
    small_grads[...] = jnp.zeros_like(small_grads)
    for turn_number, (start, tiles) in enumerate(feeds):
        width = 256 * tiles
        down, gate, up = one_w.at[0:width], two_w.at[:, 0:width], three_w.at[:, 0:width]
        part = half_a.at[:, 0:width]
        slope, gelu = value.at[:, 0:width], other.at[:, 0:width]
        gate_grad, up_grad = half_b.at[:, 0:width], half_c.at[:, 0:width]
        end(loaded)

        def split(at, grad_w):
            gate_grad[:, at] = (grad_w * slope[:, at]).astype(jnp.bfloat16)
            up_grad[:, at] = (grad_w * gelu[:, at]).astype(jnp.bfloat16)

        through(cot, down, split)

        def add(index):
            at = tile(index)
            forward = product(part[...], down[:, at])
            back = product_right(gate_grad[...], gate[at, :]) + product_right(up_grad[...], up[at, :])
            if start:
                forward, back = forward + grad_x[:, at], back + grad_n[:, at]
            grad_x[:, at] = forward
            grad_n[:, at] = back

        each(grad_x.shape[1] // 256, add)
        if turn_number + 1 < len(feeds):
            loaded = feed_loads(*feeds[turn_number + 1])
        else:
            loaded = begin(
                (given[Given.after2], value),
                (given[Given.w_co], one_w),
                (given[Given.cq_t], turned_q),
                (given[Given.ck], two_w.at[0:512]),
                (given[Given.cv], two_w.at[512:1024]),
            )
        tick()
        weight_grad(1, gate_grad, start)
        weight_grad(2, up_grad, start)
        tick()

    loaded += begin((given[Given.o2_t], left), (given[Given.cq], half_c))
    end(loaded)

    def last(index):
        at = tile(index, 32)
        half_a[at, :] = (value[at, :] + grad_x[at, :]).astype(jnp.bfloat16)

    each(value.shape[0] // 32, last)
    send_back(0, half_a)
    norm_grad(value, 2, cot, grad_x)
    round_rows(grad_x, half_a)
    tick()
    weight_grad(3, half_a)
    head_grads(one_w)
    tick()
    keys_grad, values_grad = three_w.at[:, 0:512], three_w.at[:, 512:1024]
    states = one_w.at[:, 0:512]
    loaded = begin(
        (given[Given.states_t], states), (given[Given.normed2_t], left), (given[Given.after], value)
    )

    def cross(first, last):
        attend_back_heads(
            first,
            last,
            half_c,
            turned_q,
            two_w.at[0:512],
            two_w.at[512:1024],
            half_b,
            turned_g,
            half_d,
            keys_grad,
            values_grad,
            None,
            None,
        )

    cross(0, 3)
    tick()
    cross(3, 6)
    tick()
    cross(6, 8)
    end(loaded)

    def state_grad(number, right):
        def values(at):
            result = product_right(states[...], right[at, :])
            return result.astype(jnp.bfloat16).reshape(stage.shape[1:])

        staged(stage, lambda index: grads[number].at[index], values, 4)
        pipeline.ready += 1

    state_grad(4, keys_grad)
    state_grad(5, values_grad)
    tick()
    turn(keys_grad, two_w.at[0:512])
    turn(values_grad, two_w.at[512:1024])
    kept = pltpu.make_async_copy(two_w, kept_states, out_sems.at[0])
    kept.start()
    loaded = begin(
        (given[Given.w_cq], one_w),
        (given[Given.w_so], three_w),
        (given[Given.q], half_c),
        (given[Given.q_t], turned_q),
    )
    weight_grad(6, half_d)
    kept.wait()
    end(loaded)
    loaded = begin((given[Given.k], two_w.at[0:256]), (given[Given.u], two_w.at[256:512]))
    through(half_d, one_w, store_as(grad_n))
    loaded += begin((given[Given.o1_t], left))
    norm_grad(value, 1, grad_x, grad_x)
    round_rows(grad_x, half_a)
    end(loaded)
    loaded = begin((given[Given.inputs], value), (given[Given.w_sq], one_w))
    tick()
    weight_grad(7, half_a)
    head_grads(three_w)
    loaded += begin((given[Given.normed_t], left))
    tick()

    def table_grad(index, half, grad_s):
        line = jnp.broadcast_to(diagonal_sums(grad_s), (8, grad_s.shape[1]))
        table = lax.dot_general(
            line,
            spread[half].astype(jnp.float32),
            (((1,), (1,)), ((), ())),
            precision=highest,
            preferred_element_type=jnp.float32,
        )
        small_grads[0, index, 3:4, :] = small_grads[0, index, 3:4, :] + table[0:1]

    keys_grad, values_grad = three_w.at[:, 0:256], three_w.at[:, 256:512]

    def own(first, last):
        attend_back_heads(
            first,
            last,
            half_c,
            turned_q,
            two_w.at[0:256],
            two_w.at[256:512],
            half_b,
            turned_g,
            half_d,
            keys_grad,
            values_grad,
            functools.partial(causal_bias, smalls, spread),
            table_grad,
        )

    own(0, 4)
    tick()
    own(4, 8)
    turn(keys_grad, half_a)
    turn(values_grad, half_b)
    end(loaded)
    loaded = begin((given[Given.w_sk], two_w), (given[Given.w_sv], three_w))
    tick()
    weight_grad(8, half_d)
    weight_grad(9, half_a)
    weight_grad(10, half_b)
    tick()
    end(loaded)

    def sum_three(index):
        at = tile(index)
        grad_n[:, at] = (
            product_right(half_d[...], one_w[at, :])
            + product_right(half_a[...], two_w[at, :])
            + product_right(half_b[...], three_w[at, :])
        )

    each(grad_n.shape[1] // 256, sum_three)
    loaded = begin((given[Given.w_ck], one_w), (given[Given.w_cv], three_w), (kept_states, two_w))
    norm_grad(value, 0, grad_x, half_c)
    small_copy = pltpu.make_async_copy(small_grads, grads[11], out_sems.at[1])
    small_copy.start()
    small_copy.wait()
    pipeline.ready += 1
    tick()
    send_back(1, half_c)
    tick()
    end(loaded)
    staged(
        state_stage,
        lambda index: encoder_out.at[:, tile(index)],
        lambda at: product_right(two_w[0:512], one_w[at, :])
        + product_right(two_w[512:1024], three_w[at, :]),
        4,
    )
    receive_back(0, layer_out)
    pipeline.drain()
    receive_back(1, hidden_out)
    for number in range(count):
        reduce.write(number).wait()


def backward_call(operands, rows):
    count = Given.count
    anywhere = pl.BlockSpec(memory_space=pl.ANY)
    vmem = pl.BlockSpec(memory_space=pltpu.VMEM)
    bf16, f32 = jnp.bfloat16, jnp.float32
    grad_fd = operands[Given.grad_fd]
    width, wide = operands[Given.w_fg].shape
    square = jax.ShapeDtypeStruct((width // 256, 8, width // 8, 256), bf16)
    broad = jax.ShapeDtypeStruct((wide // 256, 8, width // 8, 256), bf16)
    small = jax.ShapeDtypeStruct((1, 8, 16, 128), f32)
    full = [jax.ShapeDtypeStruct(grad_fd.shape, grad_fd.dtype), broad, broad] + [square] * 8 + [small]
    outs = [jax.ShapeDtypeStruct(g.shape[:1] + g.shape[2:], g.dtype) for g in full]
    most = operands[Given.inputs].shape[0]
    states = operands[Given.ck].shape[0]
    total = operands[Given.chosen_t].shape[0]
    kept_states = jax.ShapeDtypeStruct((2 * states, width), bf16)
    tail = [
        jax.ShapeDtypeStruct((states, width), f32),
        jax.ShapeDtypeStruct((rows, width), bf16),
        jax.ShapeDtypeStruct((rows, width), bf16),
    ]
    scratch, load_shapes, shared = [], [], []
    order = piece_order([g.shape for g in full])
    for number, unused, tiles in order:
        shape = (tiles,) + full[number].shape[2:]
        scratch += buffer_shapes(*shape, full[number].dtype)
        key = ((2,) + shape, full[number].dtype)
        held = [i for i, s in enumerate(load_shapes) if s == key]
        if len(held) < 2:
            shared.append(len(load_shapes))
            load_shapes.append(key)
        else:
            last = [i for i in shared if i in held][-1]
            shared.append(held[0] if last == held[1] else held[1])
    scratch += [pltpu.VMEM(*s) for s in load_shapes]
    pieces = len(order)
    scratch += [pltpu.VMEM((width, width), bf16)] * 3
    scratch += [
        pltpu.VMEM((2, DOCS, total // DOCS, width), bf16),
        pltpu.VMEM((3, 8, width // 8, 256), bf16),
        pltpu.VMEM((2, states, 256), f32),
    ]
    scratch += [pltpu.VMEM((most, width), f32)] * 4
    scratch += [pltpu.VMEM((most, width), bf16)] * 5
    scratch += [pltpu.VMEM((width, most), bf16)] * 3
    scratch += [
        pltpu.VMEM((total, most), bf16),
        pltpu.VMEM((2, 128, most), bf16),
        pltpu.VMEM((128, 128), f32),
        pltpu.VMEM((8, width), f32),
        pltpu.VMEM((1, width), f32),
        pltpu.VMEM((1, 8, 16, 128), f32),
        pltpu.VMEM((2, DOCS - 1, rows, width), bf16),
        pltpu.SemaphoreType.DMA((pieces, 12)),
        pltpu.SemaphoreType.DMA((pieces, 12)),
        pltpu.SemaphoreType.DMA((pieces, 5)),
        pltpu.SemaphoreType.DMA((2, DOCS - 1)),
        pltpu.SemaphoreType.DMA((2, DOCS - 1)),
        pltpu.SemaphoreType.DMA((16,)),
        pltpu.SemaphoreType.DMA((3,)),
        pltpu.SemaphoreType.DMA((2,)),
    ]
    results = pl.pallas_call(
        functools.partial(backward_kernel, shared),
        out_shape=full[1:] + [kept_states] + outs + tail,
        in_specs=[anywhere] * count,
        out_specs=[anywhere] * (len(full) + len(outs) + 1) + [vmem] * 2,
        scratch_shapes=scratch,
        compiler_params=pltpu.CompilerParams(
            collective_id=2, has_side_effects=True, vmem_limit_bytes=67043328
        ),
        name="backward",
    )(*operands)
    return results[len(full) :]


def widen_kernel(*refs):
    half = (len(refs) - 5) // 2
    smalls, lines = refs[half], refs[-4:]
    for index, line in enumerate(lines):
        line[...] = smalls[0, index : index + 1, 0 : line.shape[0]].reshape(line.shape)
    for source, target in zip(refs[:half], refs[half + 1 : -4]):
        if len(source.shape) == 2:
            target[...] = source[...].astype(target.dtype)
            continue
        for part in range(source.shape[0]):
            target[:, 256 * part : 256 * part + 256] = source[part].astype(target.dtype)


def widen_call(sums, layer_out, hidden_grad, smalls, entries):
    operands = list(sums) + [layer_out, hidden_grad, smalls]
    shapes = [jax.ShapeDtypeStruct((s.shape[1], s.shape[0] * s.shape[2]), jnp.float32) for s in sums]
    shapes.append(jax.ShapeDtypeStruct(layer_out.shape, layer_out.dtype))
    shapes.append(jax.ShapeDtypeStruct(hidden_grad.shape, jnp.float32))
    shapes += [jax.ShapeDtypeStruct((size,), jnp.float32) for size in (smalls.shape[2],) * 3 + (entries,)]
    vmem = pl.BlockSpec(memory_space=pltpu.VMEM)
    return pl.pallas_call(
        widen_kernel,
        out_shape=shapes,
        in_specs=[vmem] * len(operands),
        out_specs=[vmem] * len(shapes),
        name="widen",
    )(*operands)


def prepare_kernel(rows, norms, table, segments, docs, small, chosen, chosen_t, spread):
    small[...] = jnp.zeros_like(small)
    for index, norm in enumerate(norms):
        small[index : index + 1, :] = norm[...].reshape(1, norm.shape[0]).astype(jnp.float32)
    entries = table.shape[0]
    small[3:4, 0:entries] = table[...].reshape(1, entries).astype(jnp.float32)
    first = pl.multiple_of(lax.axis_index("ctx") * rows, rows)
    document = docs[:, pl.ds(first, 128)][:, 0:1]
    ids = segments[...]
    start = jnp.sum((ids < document).astype(jnp.int32), axis=1, keepdims=True)
    length = jnp.sum((ids == document).astype(jnp.int32), axis=1, keepdims=True)
    for target, axis in ((chosen, 0), (chosen_t, 1)):
        row = lax.broadcasted_iota(jnp.int32, target.shape, axis)
        column = lax.broadcasted_iota(jnp.int32, target.shape, 1 - axis)
        here = jnp.where(row < length, row + start, -1)
        target[...] = (here == column).astype(jnp.float32).astype(jnp.bfloat16)
    most = spread.shape[2]
    position = lax.broadcasted_iota(jnp.int32, (1, most), 1)
    bucket = bucket_of(jnp.where(position == 0, 0, most - position))
    slot = lax.broadcasted_iota(jnp.int32, spread.shape[1:], 0)
    for half in range(2):
        found = (slot == bucket + BUCKETS * half).astype(jnp.float32)
        spread[half] = found.astype(jnp.bfloat16)


def prepare_call(norms, table, segment_ids, encoder_docs, rows):
    total = segment_ids.shape[1]
    most = total // 2
    count = len(norms)

    def kernel(*refs):
        prepare_kernel(rows, refs[:count], *refs[count:])

    vmem = pl.BlockSpec(memory_space=pltpu.VMEM)
    return pl.pallas_call(
        kernel,
        out_shape=[
            jax.ShapeDtypeStruct((16, norms[0].shape[0]), jnp.float32),
            jax.ShapeDtypeStruct((most, total), jnp.bfloat16),
            jax.ShapeDtypeStruct((total, most), jnp.bfloat16),
            jax.ShapeDtypeStruct((2, 2 * HD, most), jnp.bfloat16),
        ],
        in_specs=[vmem] * (count + 3),
        out_specs=[vmem] * 4,
        name="prepare",
    )(*norms, table, segment_ids, encoder_docs)


def by_document(
    hidden_in,
    encoder_states,
    segment_ids,
    encoder_docs,
    self_query,
    self_key,
    self_value,
    self_out,
    cross_query,
    cross_key,
    cross_value,
    cross_out,
    feed_gate,
    feed_up,
    feed_down,
    norm_self,
    norm_cross,
    norm_feed,
    bias_table,
    out_grad,
):
    width = hidden_in.shape[2]
    encoded = encoder_states[0]
    small, chosen, chosen_t, spread = prepare_call(
        (norm_self, norm_cross, norm_feed), bias_table, segment_ids, encoder_docs, encoded.shape[0]
    )
    results = forward_call(
        (
            small,
            cross_key,
            cross_value,
            self_query,
            self_key,
            self_value,
            self_out,
            cross_query,
            cross_out,
            feed_gate,
            feed_up,
            feed_down,
        ),
        hidden_in[0],
        out_grad[0],
        chosen,
        encoded,
        spread,
    )
    kept = results[12:]
    grad_fd = results[-1].reshape(width // 256, 8, -1, 256)
    forward_side = [
        kept[i]
        for i in (
            Kept.inputs,
            Kept.normed_t,
            Kept.q,
            Kept.q_t,
            Kept.k,
            Kept.u,
            Kept.o1_t,
            Kept.after,
            Kept.normed2_t,
            Kept.cq,
            Kept.cq_t,
            Kept.ck,
            Kept.cv,
            Kept.o2_t,
            Kept.after2,
            Kept.normed3_t,
            Kept.w,
            Kept.slope,
            Kept.gelu,
            Kept.cot,
            Kept.states_t,
        )
    ]
    results = backward_call(
        forward_side + [chosen_t, spread] + list(results[:12]) + [grad_fd], hidden_in.shape[1]
    )
    smalls, encoder_grad, layer_out, hidden_grad = results[11:]
    fd, fg, fu, co, ck, cv, cq, so, sq, sk, sv, layer_out, hidden_grad, *lines = widen_call(
        results[:11], layer_out, hidden_grad, smalls, bias_table.shape[0]
    )
    return (
        layer_out[None],
        hidden_grad[None],
        encoder_grad[None],
        sq,
        sk,
        sv,
        so,
        cq,
        ck,
        cv,
        co,
        fg,
        fu,
        fd,
        *lines,
    )


def layer(sizes, *args):
    encoder_states, encoder_docs = args[1], args[3]
    whole_document = encoder_states.shape[1] * DOCS == encoder_docs.shape[1]
    if whole_document and sizes["fsdp"] == 8 and sizes["ctx"] == DOCS:
        return by_document(*args)
    return on_device(*args)


def solution(mesh):
    in_specs = (
        P("fsdp", "ctx", None),
        P("fsdp", "ctx", None),
        P("fsdp", None),
        P("fsdp", None),
        P("fsdp", None),
        P("fsdp", None),
        P("fsdp", None),
        P("fsdp", None),
        P("fsdp", None),
        P("fsdp", None),
        P("fsdp", None),
        P("fsdp", None),
        P("fsdp", None),
        P("fsdp", None),
        P("fsdp", None),
        P("fsdp"),
        P("fsdp"),
        P("fsdp"),
        P("fsdp"),
        P("fsdp", "ctx", None),
    )
    out_specs = (
        P("fsdp", "ctx", None),
        P("fsdp", "ctx", None),
        P("fsdp", "ctx", None),
        P("fsdp", None),
        P("fsdp", None),
        P("fsdp", None),
        P("fsdp", None),
        P("fsdp", None),
        P("fsdp", None),
        P("fsdp", None),
        P("fsdp", None),
        P("fsdp", None),
        P("fsdp", None),
        P("fsdp", None),
        P("fsdp"),
        P("fsdp"),
        P("fsdp"),
        P("fsdp"),
    )
    return jax.shard_map(
        functools.partial(layer, dict(mesh.shape)), mesh=mesh, in_specs=in_specs, out_specs=out_specs, check_vma=False
    )
```
